256 devices in a mesh: scan: 16 (over y, x), blk: 16 (over z, core).
Axes of the slice: x: 4, y: 4, z: 8, core: 2. Of those that a mesh axis runs over, the one named last changes fastest.
Arguments:
- ref_feats: bfloat16 [16, 8192, 256], P('scan', 'blk'), may hold values from -120 to 120
- src_feats: bfloat16 [16, 2048, 256], P('scan', 'blk'), may hold values from -120 to 120
- grad_out: bfloat16 [16, 8192, 256], P('scan', 'blk'), may hold values from -6 to 6
- w_query: bfloat16 [256, 256], replicated, may hold values from -1 to 1
- w_key: bfloat16 [256, 256], replicated, may hold values from -1 to 1
- w_value: bfloat16 [256, 256], replicated, may hold values from -0.375 to 0.375
- w_out: bfloat16 [256, 256], replicated, may hold values from -0.375 to 0.375
- intersection: int32 [16, 64, 16], P('scan', 'blk'), may hold values from 0 to 1, as said below
Outputs:
- matched: bfloat16 [16, 8192, 256], P('scan', 'blk')
- grad_ref: bfloat16 [16, 8192, 256], P('scan', 'blk')
- grad_src: bfloat16 [16, 2048, 256], P('scan', 'blk')
- grad_w_query: float32 [256, 256], replicated
- grad_w_key: float32 [256, 256], replicated
- grad_w_value: float32 [256, 256], replicated
- grad_w_out: float32 [256, 256], replicated
The draws below stay inside these ranges and needn't reach their ends.
Inputs may be any that keep to these rules, and one draw needn't show every extreme that they name: intersection[p, b, c] is 1 for c = b * 16 // 64, so every reference block and every source block of a pair has a listed partner.
All inputs are finite; a program needn't handle non-finite values.
Results may differ from the reference program's by a relative error of at most 0.035.
Values may be sent and summed in bfloat16 or wider, within the bound.
A program may use at most 64 MiB of HBM per device.

```python
import math
import jax
import jax.numpy as jnp
from jax import lax

D = 256
HEADS = 4
HEAD_DIM = 64
BLOCK = 128
PAIRS = 16
NQ = 8192
NK = 2048
NQB = 64
NKB = 16


def spread_scales(key, shape):
    return jnp.exp(jax.random.uniform(key, shape, jnp.float32, math.log(0.3), math.log(3.0)))


def base_values(key, shape):
    return jax.random.normal(key, shape, jnp.float32)


def source_values(key):
    values_out = base_values(jax.random.fold_in(key, 601), (PAIRS, NK, D))
    values_out = values_out * spread_scales(jax.random.fold_in(key, 602), (PAIRS, NK))[:, :, None]
    return jnp.clip(values_out, -120.0, 120.0)


def draw_src_feats(key, part):
    return source_values(key).astype(jnp.bfloat16)


def draw_ref_feats(key, part):
    position = 0.6 + 1.2 * jnp.arange(NQ, dtype=jnp.float32) / NQ
    row_scale = spread_scales(jax.random.fold_in(key, 702), (PAIRS, NQ)) * position[None, :]
    values_out = base_values(jax.random.fold_in(key, 701), (PAIRS, NQ, D)) * row_scale[:, :, None]
    return jnp.clip(values_out, -120.0, 120.0).astype(jnp.bfloat16)


def draw_w_query(key, part):
    return (jax.random.normal(jax.random.fold_in(key, 801), (D, D), jnp.float32) / math.sqrt(D)).astype(jnp.bfloat16)


def draw_w_key(key, part):
    return (jax.random.normal(jax.random.fold_in(key, 803), (D, D), jnp.float32) / math.sqrt(D)).astype(jnp.bfloat16)


def draw_intersection(key, part):
    query_block = jnp.arange(NQB)
    key_block = jnp.arange(NKB)
    band_block = query_block * NKB // NQB
    run_start = jax.random.randint(jax.random.fold_in(key, 901), (PAIRS, NQB), 0, NKB)
    run_length = jax.random.randint(jax.random.fold_in(key, 902), (PAIRS, NQB), 0, NKB // 2 + 1)
    offset = (key_block[None, None, :] - run_start[:, :, None]) % NKB
    listed = (offset < run_length[:, :, None]) | (key_block[None, None, :] == band_block[None, :, None])
    return listed.astype(jnp.int32)


def with_spikes(values, own_key, source, target, parts, factor):
    def block_of(axis_at):
        return (jnp.arange(values.shape[axis_at]) // (values.shape[axis_at] // parts)).reshape((-1,) + (1,) * (values.ndim - 1 - axis_at))

    near = jax.random.permutation(own_key, parts)[block_of(target)]
    other_side = (block_of(target) + parts // 2) % parts
    return jnp.where((block_of(source) == near) | (block_of(source) == other_side), factor * values, values)


def levels(key, extent, split, low, high):
    def one(dim, shards_of):
        heights = jax.random.uniform(jax.random.fold_in(jax.random.fold_in(key, 6), dim), (shards_of,), jnp.float32, low / len(split), high / len(split))
        return jnp.repeat(jnp.exp(heights), extent[dim] // shards_of).reshape((-1,) + (1,) * (len(extent) - dim - 1))

    gain = one(*split[0])
    for cut in split[1:]:
        gain = gain * one(*cut)
    return gain


def bell_draw(own_key, shape, spread, limit, shards=(), kind=jnp.bfloat16):
    loudness = levels(own_key, shape, shards, -0.22, 0.18) if shards else 1.0
    entries = jax.random.normal(own_key, shape, jnp.float32) * spread * loudness
    return jnp.minimum(jnp.maximum(entries, -limit), limit).astype(kind)


def noise_with(key, dims, width, bound, cuts, heavy, kind=jnp.bfloat16):
    values = width * jax.random.normal(key, dims, jnp.float32)
    if cuts:
        values = values * levels(key, dims, cuts, -0.22, 0.18)
    return jnp.clip(with_spikes(values, jax.random.fold_in(key, 3), *heavy), -bound, bound).astype(kind)


def setup_inputs(seed: int = 0) -> dict:
    key_list = jax.random.split(jax.random.key(seed), 9)
    ref_feats = draw_ref_feats(jax.random.fold_in(key_list[8], 71), 0)
    src_feats = draw_src_feats(jax.random.fold_in(key_list[8], 71), 0)
    grad_out = noise_with(key_list[2], (PAIRS, NQ, D), 1.0, 6.0, ((0, 16), (1, 16)), (1, 2, 16, 2.0))
    w_query = draw_w_query(jax.random.fold_in(key_list[8], 71), 0)
    w_key = draw_w_key(jax.random.fold_in(key_list[8], 71), 0)
    w_value = bell_draw(key_list[5], (D, D), D ** -0.5, 0.375)
    w_out = bell_draw(key_list[6], (D, D), D ** -0.5, 0.375)
    intersection = draw_intersection(jax.random.fold_in(key_list[8], 71), 0)
    return {"ref_feats": ref_feats, "src_feats": src_feats, "grad_out": grad_out, "w_query": w_query, "w_key": w_key, "w_value": w_value, "w_out": w_out, "intersection": intersection}


NEG = -1.0e30


def allowed_mask(block_rows):
    return jnp.repeat(jnp.repeat(block_rows == 1, BLOCK, axis=0), BLOCK, axis=1)


def exact_dot(left, right):
    return jnp.dot(left, right, precision=lax.Precision.HIGHEST)


def head_pass(allowed, query_head, key_head, value_head, grad_head):
    score_scale = HEAD_DIM ** -0.5
    scores = exact_dot(query_head, key_head.T) * score_scale
    masked = jnp.where(allowed, scores, NEG)
    row_peak = masked.max(axis=1, keepdims=True)
    row_exp = jnp.where(allowed, jnp.exp(scores - row_peak), 0.0)
    row_prob = row_exp / row_exp.sum(axis=1, keepdims=True)
    col_peak = masked.max(axis=0, keepdims=True)
    col_exp = jnp.where(allowed, jnp.exp(scores - col_peak), 0.0)
    col_prob = col_exp / col_exp.sum(axis=0, keepdims=True)
    match_prob = lax.optimization_barrier((row_prob * col_prob).astype(jnp.bfloat16)).astype(jnp.float32)
    attended = exact_dot(match_prob, value_head)
    grad_prob = exact_dot(grad_head, value_head.T)
    product = match_prob * grad_prob
    row_dot = product.sum(axis=1, keepdims=True)
    col_dot = product.sum(axis=0, keepdims=True)
    grad_score = score_scale * (2.0 * product - row_prob * row_dot - col_prob * col_dot)
    grad_score = lax.optimization_barrier(grad_score.astype(jnp.bfloat16)).astype(jnp.float32)
    grad_query = exact_dot(grad_score, key_head)
    grad_key = exact_dot(grad_score.T, query_head)
    grad_value = exact_dot(match_prob.T, grad_head)
    return attended, grad_query, grad_key, grad_value


def reference(ref_feats, src_feats, grad_out, w_query, w_key, w_value, w_out, intersection):
    def split_heads(matrix):
        return matrix.astype(jnp.float32).reshape(matrix.shape[0], HEADS, HEAD_DIM).transpose(1, 0, 2)

    def join_heads(stack):
        return stack.transpose(1, 0, 2).reshape(stack.shape[1], D)

    def one_pair(pair_inputs):
        ref_rows, src_rows, out_grad, block_rows = pair_inputs
        allowed = allowed_mask(block_rows)
        queries = jnp.dot(ref_rows, w_query, preferred_element_type=jnp.float32).astype(jnp.bfloat16)
        key_rows = jnp.dot(src_rows, w_key, preferred_element_type=jnp.float32).astype(jnp.bfloat16)
        values = jnp.dot(src_rows, w_value, preferred_element_type=jnp.float32).astype(jnp.bfloat16)
        grad_att = jnp.dot(out_grad, w_out.T, preferred_element_type=jnp.float32).astype(jnp.bfloat16)

        def one_head(head_inputs):
            return head_pass(allowed, head_inputs[0], head_inputs[1], head_inputs[2], head_inputs[3])

        attended, grad_query, grad_keys, grad_values = lax.map(
            one_head, (split_heads(queries), split_heads(key_rows), split_heads(values), split_heads(grad_att)))
        attended = join_heads(attended).astype(jnp.bfloat16)
        matched = (ref_rows.astype(jnp.float32) + jnp.dot(attended, w_out, preferred_element_type=jnp.float32)).astype(jnp.bfloat16)
        grad_query = join_heads(grad_query).astype(jnp.bfloat16)
        grad_keys = join_heads(grad_keys)
        grad_values = join_heads(grad_values)
        grad_ref = (out_grad.astype(jnp.float32) + jnp.dot(grad_query, w_query.T, preferred_element_type=jnp.float32)).astype(jnp.bfloat16)
        grad_src = (exact_dot(grad_keys, w_key.T.astype(jnp.float32)) + exact_dot(grad_values, w_value.T.astype(jnp.float32))).astype(jnp.bfloat16)
        source_wide = src_rows.astype(jnp.float32)
        weight_query = jnp.dot(ref_rows.T, grad_query, preferred_element_type=jnp.float32)
        weight_key = exact_dot(source_wide.T, grad_keys)
        weight_value = exact_dot(source_wide.T, grad_values)
        weight_out = jnp.dot(attended.T, out_grad, preferred_element_type=jnp.float32)
        return matched, grad_ref, grad_src, weight_query, weight_key, weight_value, weight_out

    results = lax.map(one_pair, (ref_feats, src_feats, grad_out, intersection))
    return (results[0], results[1], results[2], results[3].sum(axis=0), results[4].sum(axis=0),
            results[5].sum(axis=0), results[6].sum(axis=0))
```

```python
import functools
import math

import jax
import jax.numpy as jnp
from jax import lax
from jax.experimental import pallas as pl
from jax.experimental.pallas import tpu as pltpu
from jax.sharding import PartitionSpec as P

HEADS = 4
HEAD_DIM = 64
BLOCK = 128
D = 256
ROWS = 512
KEYS = 2048
TILE = 256
TILES = KEYS // TILE
QBLOCKS = ROWS // BLOCK
CHIPS = 8
PLANE = 16
NEG = -1.0e30
LOG2E = math.log2(math.e)
SCALE = HEAD_DIM**-0.5
F32 = jnp.float32
BF16 = jnp.bfloat16
MESH = pl.DeviceIdType.MESH
VMEM = pl.BlockSpec(memory_space=pltpu.VMEM)
SMEM = pl.BlockSpec(memory_space=pltpu.SMEM)


def nn(a, b):
    return jnp.dot(a, b, preferred_element_type=F32)


def nt(a, b):
    return lax.dot_general(a, b, (((1,), (1,)), ((), ())), preferred_element_type=F32)


def lane_mask(rows, parity):
    lane = lax.broadcasted_iota(jnp.int32, (rows, BLOCK), 1)
    return (lane < HEAD_DIM) if parity == 0 else (lane >= HEAD_DIM)


def one_head(array, head, rows):
    group = head // 2
    part = array[:, group * BLOCK : (group + 1) * BLOCK]
    return jnp.where(lane_mask(rows, head % 2), part, jnp.zeros_like(part))


def group_cols(head):
    return slice((head // 2) * BLOCK, (head // 2 + 1) * BLOCK)


def tile_rows(tile):
    return pl.ds(pl.multiple_of(tile * TILE, TILE), TILE)


def block_bias(inter, qb, kb):
    return jnp.where(inter[qb, kb] == 1, 0.0, NEG).astype(F32)


def scaled_tile(scores, inter, tile):
    out = []
    for qb in range(QBLOCKS):
        row = []
        for kb in range(TILE // BLOCK):
            piece = scores[qb * BLOCK : (qb + 1) * BLOCK, kb * BLOCK : (kb + 1) * BLOCK]
            row.append(piece * (SCALE * LOG2E) + block_bias(inter, qb, tile * (TILE // BLOCK) + kb))
        out.append(row)
    return out


def stats_kernel(ref, src, wq, wk, inter, q_out, k_out, lr_out, lc_out, t_scr, rm_scr):
    q_out[...] = nn(ref[...], wq[...]).astype(BF16)

    @pl.loop(0, TILES)
    def _(tile):
        k_out[tile_rows(tile), :] = nn(src[tile_rows(tile), :], wk[...]).astype(BF16)

    for head in range(HEADS):
        qm = one_head(q_out[...], head, ROWS)
        cols = group_cols(head)
        rm_scr[...] = jnp.full_like(rm_scr, -3.0e38)

        @pl.loop(0, TILES)
        def _(tile):
            scores = nt(qm, k_out[tile_rows(tile), cols])
            pieces = scaled_tile(scores, inter, tile)
            for qb in range(QBLOCKS):
                rows = slice(qb * BLOCK, (qb + 1) * BLOCK)
                rm_scr[rows, :] = jnp.maximum(rm_scr[rows, :], jnp.maximum(pieces[qb][0], pieces[qb][1]))
                for kb in range(2):
                    t_scr[tile, rows, kb * BLOCK : (kb + 1) * BLOCK] = pieces[qb][kb]
            for kb in range(2):
                peak = pieces[0][kb]
                for qb in range(1, QBLOCKS):
                    peak = jnp.maximum(peak, pieces[qb][kb])
                peak = peak.max(axis=0, keepdims=True)
                total = jnp.exp2(pieces[0][kb] - peak)
                for qb in range(1, QBLOCKS):
                    total = total + jnp.exp2(pieces[qb][kb] - peak)
                total = total.sum(axis=0, keepdims=True)
                lc_out[pl.ds(head * 16 + tile * 2 + kb, 1), :] = peak + jnp.log2(total)

        peak = rm_scr[...].max(axis=1, keepdims=True)
        rm_scr[...] = jnp.zeros_like(rm_scr)

        @pl.loop(0, TILES)
        def _(tile):
            rm_scr[...] += jnp.exp2(t_scr[tile, :, :BLOCK] - peak) + jnp.exp2(t_scr[tile, :, BLOCK:] - peak)

        total = rm_scr[...].sum(axis=1, keepdims=True)
        lr_out[head] = jnp.broadcast_to(peak + jnp.log2(total), (ROWS, BLOCK))


def probs(qm, k_ref, inter, lr, lc, head, tile):
    pieces = scaled_tile(nt(qm, k_ref[tile_rows(tile), group_cols(head)]), inter, tile)
    row, col = [], []
    for qb in range(QBLOCKS):
        lr_piece = lr[head, qb * BLOCK : (qb + 1) * BLOCK, :]
        row.append([jnp.exp2(pieces[qb][kb] - lr_piece) for kb in range(2)])
        col.append([
            jnp.exp2(pieces[qb][kb] - lc[pl.ds(head * 16 + tile * 2 + kb, 1), :]) for kb in range(2)
        ])
    return row, col


def joined(grid):
    return jnp.concatenate([jnp.concatenate(row, axis=1) for row in grid], axis=0)


def pack_weight(w_out, core, which, matrix):
    for half in range(2):
        for part in range(4):
            w_out[core, 4 * (2 * which + half) + part] = matrix[
                64 * part : 64 * (part + 1), half * BLOCK : (half + 1) * BLOCK
            ].astype(BF16)


def forward_kernel(
    ref, gout, src, q, k, wv, wo, inter, lr, lc,
    v_out, ga_out, gvt_out, cd_out, rd_out, matched_out, w_out,
    vt_scr, gat_scr, att_scr, att_all, gvt_scr, p_scr,
):
    ga_out[...] = nt(gout[...], wo[...]).astype(BF16)
    gat_scr[...] = nt(wo[...], gout[...]).astype(BF16)
    wvt = wv[...].T

    @pl.loop(0, TILES)
    def _(tile):
        rows = src[tile_rows(tile), :]
        v_out[tile_rows(tile), :] = nn(rows, wv[...]).astype(BF16)
        vt_scr[tile] = nt(wvt, rows).astype(BF16)

    for head in range(HEADS):
        qm = one_head(q[...], head, ROWS)
        cols = group_cols(head)
        lanes = slice(head * HEAD_DIM, (head + 1) * HEAD_DIM)
        gat = gat_scr[lanes, :]
        att_scr[...] = jnp.zeros_like(att_scr)

        @pl.loop(0, TILES)
        def _(tile):
            row, col = probs(qm, k, inter, lr, lc, head, tile)
            match = joined([[(row[a][b] * col[a][b]).astype(BF16) for b in range(2)] for a in range(QBLOCKS)])
            att_scr[...] += nn(match, v_out[tile_rows(tile), cols])
            gvt = nn(gat, match)
            gvt_scr[tile, lanes, :] = gvt.astype(BF16)
            dots = (gvt * vt_scr[tile, lanes, :].astype(F32)).sum(axis=0, keepdims=True)
            for kb in range(2):
                cd_out[pl.ds(head * 16 + tile * 2 + kb, 1), :] = dots[:, kb * BLOCK : (kb + 1) * BLOCK]

        mask = lane_mask(ROWS, head % 2)
        att = jnp.where(mask, att_scr[...], 0.0)
        rd = (att * ga_out[:, cols].astype(F32)).sum(axis=1, keepdims=True)
        rd_out[head] = jnp.broadcast_to(rd, (ROWS, BLOCK))
        if head % 2 == 0:
            att_all[:, cols] = att.astype(BF16)
        else:
            att_all[:, cols] = jnp.where(mask, att.astype(BF16), att_all[:, cols])

    matched_out[...] = (ref[...].astype(F32) + nn(att_all[...], wo[...])).astype(BF16)
    gvt_out[...] = gvt_scr[...]
    pack_weight(w_out, 0, 1, nn(att_all[...].T, gout[...]))
    wvg = jnp.zeros((D, D), F32)
    for tile in range(TILES):
        wvg = wvg + nn(gvt_scr[tile], src[tile * TILE : (tile + 1) * TILE, :])
    pack_weight(w_out, 0, 0, wvg.T)


def backward_kernel(
    ref, gout, src, q, k, v, ga, wq, wk, wv, inter, lr, lc, rd, cd, gvt, w_in,
    gref_out, gs_out, w_out,
    gkt_scr, gq_scr, gq_all,
):
    qt = q[...].T
    for head in range(HEADS):
        qm = one_head(q[...], head, ROWS)
        gam = one_head(ga[...], head, ROWS)
        cols = group_cols(head)
        lanes = slice(head * HEAD_DIM, (head + 1) * HEAD_DIM)
        qt_head = qt[lanes, :]
        gq_scr[...] = jnp.zeros_like(gq_scr)

        @pl.loop(0, TILES)
        def _(tile):
            row, col = probs(qm, k, inter, lr, lc, head, tile)
            gp = nt(gam, v[tile_rows(tile), cols])
            grid = []
            for qb in range(QBLOCKS):
                rows = slice(qb * BLOCK, (qb + 1) * BLOCK)
                rd_piece = rd[head, rows, :]
                line = []
                for kb in range(2):
                    cd_piece = cd[pl.ds(head * 16 + tile * 2 + kb, 1), :]
                    r, c = row[qb][kb], col[qb][kb]
                    match = (r * c).astype(BF16).astype(F32)
                    g = gp[rows, kb * BLOCK : (kb + 1) * BLOCK]
                    line.append((2.0 * match * g - r * rd_piece - c * cd_piece).astype(BF16))
                grid.append(line)
            gs = joined(grid)
            gq_scr[...] += nn(gs, k[tile_rows(tile), cols])
            gkt_scr[tile, lanes, :] = (nn(qt_head, gs) * SCALE).astype(BF16)

        mask = lane_mask(ROWS, head % 2)
        gq = (gq_scr[...] * SCALE).astype(BF16)
        if head % 2 == 0:
            gq_all[:, cols] = gq
        else:
            gq_all[:, cols] = jnp.where(mask, gq, gq_all[:, cols])

    gref_out[...] = (gout[...].astype(F32) + nt(gq_all[...], wq[...])).astype(BF16)
    pack_weight(w_out, 0, 0, nn(ref[...].T, gq_all[...]))
    wkg = jnp.zeros((D, D), F32)
    for tile in range(TILES):
        wkg = wkg + nn(gkt_scr[tile], src[tile * TILE : (tile + 1) * TILE, :])
        gst = nn(wk[...], gkt_scr[tile]) + nn(wv[...], gvt[tile])
        gs_out[0, tile] = gst[:, :BLOCK].astype(BF16)
        gs_out[1, tile] = gst[:, BLOCK:].astype(BF16)
    pack_weight(w_out, 0, 1, wkg.T)
    w_out[1] = w_in[0]


def place():
    blk = lax.axis_index("blk")
    scan = lax.axis_index("scan")
    chip = lax.div(blk, 2)
    core = lax.rem(blk, 2)
    return scan, blk, chip, core


def on_column(chip, core):
    return {"blk": chip * 2 + core}


def meet(targets):
    barrier = pltpu.get_barrier_semaphore()
    for target in targets:
        pl.semaphore_signal(barrier, inc=1, device_id=target, device_id_type=MESH)
    pl.semaphore_wait(barrier, len(targets))


def send(src, dst, sems, index, target):
    send_sem, recv_sem = sems
    return pltpu.make_async_remote_copy(
        src_ref=src, dst_ref=dst, send_sem=send_sem.at[index], recv_sem=recv_sem.at[index],
        device_id=target, device_id_type=MESH,
    )


FAR_FIRST = (4, 3, 5, 2, 6, 1, 7)


def gather_kernel(src, out, own_sem, s0, r0, s1, r1):
    scan, blk, chip, core = place()
    partner = {"blk": chip * 2 + 1 - core}
    peers = [on_column(lax.rem(chip + d, CHIPS), core) for d in range(1, CHIPS)]
    meet([partner] + peers)
    across = {}
    for d in FAR_FIRST:
        across[d] = send(src, out.at[blk], (s0, r0), d, peers[d - 1])
        across[d].start()
    forward = [send(src, out.at[blk], (s1, r1), 0, partner)]
    forward[0].start()
    own = pltpu.make_async_copy(src, out.at[blk], own_sem)
    own.start()
    for d in (1, 7, 2, 6, 3, 5, 4):
        across[d].wait_recv()
        origin = lax.rem(chip + CHIPS - d, CHIPS) * 2 + core
        copy = send(out.at[origin], out.at[origin], (s1, r1), d, partner)
        copy.start()
        forward.append(copy)
    own.wait()
    for copy in forward:
        copy.wait_recv()
    for copy in forward:
        copy.wait_send()
    for copy in across.values():
        copy.wait_send()


def exchange_kernel(combine, part, out, buf_a, half, buf_b, done, s0, r0, s1, r1):
    scan, blk, chip, core = place()
    partner = {"blk": chip * 2 + 1 - core}
    peers = [on_column(lax.rem(chip + d, CHIPS), core) for d in range(1, CHIPS)]
    meet([partner] + peers)
    mine = pl.ds(pl.multiple_of(core * 32, 32), 32)
    other = pl.ds(pl.multiple_of((1 - core) * 32, 32), 32)
    first = send(part.at[other], buf_a, (s0, r0), 0, partner)
    first.start()
    first.wait_recv()
    half[...] = combine([part[mine], buf_a[...]])
    across = {}
    for d in FAR_FIRST:
        across[d] = send(half, buf_b.at[d - 1], (s1, r1), d - 1, peers[d - 1])
        across[d].start()
    for d in (1, 7, 2, 6, 3, 5, 4):
        across[d].wait_recv()
    done[...] = combine([half[...]] + [buf_b[d] for d in range(CHIPS - 1)])
    last = send(done, out.at[mine], (s0, r0), 1, partner)
    last.start()
    out[mine] = done[...]
    last.wait_recv()
    first.wait_send()
    for copy in across.values():
        copy.wait_send()
    last.wait_send()


def log_sum(parts):
    peak = functools.reduce(jnp.maximum, parts)
    return peak + jnp.log2(sum(jnp.exp2(part - peak) for part in parts))


def plain_sum(parts):
    return sum(parts)


def final_kernel(
    gs, wg, gsrc_out, wq_out, wk_out, wv_out, wo_out,
    wbuf, gbuf, wsum, gsum, wrecv, grecv, wpart, zrecv, wdone, zall, wrow, wall,
    sp, rp, sx, rx, sg, rg, sz, rz, sa, ra, sb, rb,
):
    scan, blk, chip, core = place()
    partner = {"blk": chip * 2 + 1 - core}
    peers = [on_column(lax.rem(chip + d, CHIPS), core) for d in range(1, CHIPS)]
    plane = [{"scan": lax.rem(scan + d, PLANE)} for d in range(1, PLANE)]
    meet([partner] + peers + plane)
    copies = []

    def start(*args):
        copy = send(*args)
        copy.start()
        copies.append(copy)
        return copy

    w_swap = start(wg.at[1 - core], wbuf, (sp, rp), 0, partner)
    g_swap = start(gs.at[1 - core], gbuf, (sp, rp), 1, partner)
    w_swap.wait_recv()
    wsum[...] = (wg[core].astype(F32) + wbuf[...].astype(F32)).astype(BF16)
    plane_in = []
    for d in range(1, PLANE):
        to = lax.rem(scan + d, PLANE)
        plane_in.append(start(wsum.at[to], wrecv.at[d - 1], (sx, rx), d - 1, plane[d - 1]))
    g_swap.wait_recv()
    for c in range(CHIPS):
        gsum[c] = (gs[core, c].astype(F32) + gbuf[c].astype(F32)).astype(BF16)
    col_in = []
    for d in FAR_FIRST:
        to = lax.rem(chip + d, CHIPS)
        col_in.append(start(gsum.at[to], grecv.at[d - 1], (sg, rg), d - 1, peers[d - 1]))
    for copy in plane_in:
        copy.wait_recv()
    total = wsum[scan].astype(F32)
    for d in range(PLANE - 1):
        total = total + wrecv[d].astype(F32)
    wpart[...] = total.reshape(CHIPS, 8, BLOCK)
    z_in = []
    for d in range(1, CHIPS):
        to = lax.rem(chip + d, CHIPS)
        z_in.append(start(wpart.at[to], zrecv.at[d - 1], (sz, rz), d - 1, peers[d - 1]))
    for copy in z_in:
        copy.wait_recv()
    total = wpart[chip]
    for d in range(CHIPS - 1):
        total = total + zrecv[d]
    wdone[...] = total
    a_in = []
    for d in range(1, CHIPS):
        a_in.append(start(wdone, zall.at[chip], (sa, ra), d - 1, peers[d - 1]))
    zall[chip] = total
    for copy in col_in:
        copy.wait_recv()
    gsrc = gsum[chip].astype(F32)
    for d in range(CHIPS - 1):
        gsrc = gsrc + grecv[d].astype(F32)
    gsrc_out[...] = gsrc.T.astype(BF16)
    for copy in a_in:
        copy.wait_recv()
    row = zall[...].reshape(CHIPS * 8, BLOCK).astype(BF16)
    wrow[...] = row
    b_in = []
    for d in range(1, PLANE):
        b_in.append(start(wrow, wall.at[core, scan], (sb, rb), d - 1, plane[d - 1]))
    wall[core, scan] = row
    for copy in b_in:
        copy.wait_recv()
    last = start(wall.at[core], wall.at[core], (sp, rp), 2, partner)
    last.wait_recv()
    for core_at, pair in enumerate(((wq_out, wk_out), (wv_out, wo_out))):
        for which, out in enumerate(pair):
            for half in range(2):
                for part in range(4):
                    out[64 * part : 64 * (part + 1), half * BLOCK : (half + 1) * BLOCK] = wall[
                        core_at, 4 * (2 * which + half) + part
                    ].astype(F32)
    for copy in copies:
        copy.wait_send()


def shape(dims, dtype):
    return jax.ShapeDtypeStruct(dims, dtype)


DMA = pltpu.SemaphoreType.DMA


def call(kernel, outs, n_in, scratch, name, smem=(), collective_id=None, vmem=48 << 20):
    params = dict(vmem_limit_bytes=vmem)
    if collective_id is not None:
        params.update(collective_id=collective_id, has_side_effects=True)
    single = not isinstance(outs, (list, tuple))
    return pl.pallas_call(
        kernel,
        out_shape=outs,
        in_specs=[SMEM if i in smem else VMEM for i in range(n_in)],
        out_specs=VMEM if single else [VMEM] * len(outs),
        scratch_shapes=scratch,
        compiler_params=pltpu.CompilerParams(**params),
        name=name,
    )


def gather(src):
    out = call(
        gather_kernel, shape((16, BLOCK, D), BF16), 1,
        [DMA, DMA((8,)), DMA((8,)), DMA((8,)), DMA((8,))], "gather_src", collective_id=1,
    )(src)
    return out.reshape(KEYS, D)


def exchange(part, combine, ident):
    return call(
        functools.partial(exchange_kernel, combine), shape((64, BLOCK), F32), 1,
        [pltpu.VMEM((32, BLOCK), F32), pltpu.VMEM((32, BLOCK), F32), pltpu.VMEM((7, 32, BLOCK), F32),
         pltpu.VMEM((32, BLOCK), F32), DMA((2,)), DMA((2,)), DMA((7,)), DMA((7,))],
        "exchange_%d" % ident, collective_id=ident,
    )(part)


def stats(ref, src, wq, wk, inter):
    return call(
        stats_kernel,
        [shape((ROWS, D), BF16), shape((KEYS, D), BF16), shape((HEADS, ROWS, BLOCK), F32), shape((64, BLOCK), F32)],
        5, [pltpu.VMEM((TILES, ROWS, TILE), F32), pltpu.VMEM((ROWS, BLOCK), F32)], "stats", smem=(4,),
    )(ref, src, wq, wk, inter)


def forward(ref, gout, src, q, k, wv, wo, inter, lr, lc):
    return call(
        forward_kernel,
        [shape((KEYS, D), BF16), shape((ROWS, D), BF16), shape((TILES, D, TILE), BF16), shape((64, BLOCK), F32),
         shape((HEADS, ROWS, BLOCK), F32), shape((ROWS, D), BF16), shape((1, 16, 64, BLOCK), BF16)],
        10,
        [pltpu.VMEM((TILES, D, TILE), BF16), pltpu.VMEM((D, ROWS), BF16), pltpu.VMEM((ROWS, BLOCK), F32),
         pltpu.VMEM((ROWS, D), BF16), pltpu.VMEM((TILES, D, TILE), BF16), pltpu.VMEM((ROWS, TILE), BF16)],
        "forward", smem=(7,),
    )(ref, gout, src, q, k, wv, wo, inter, lr, lc)


def backward(*args):
    return call(
        backward_kernel,
        [shape((ROWS, D), BF16), shape((2, TILES, D, BLOCK), BF16), shape((2, 16, 64, BLOCK), BF16)],
        17,
        [pltpu.VMEM((TILES, D, TILE), BF16), pltpu.VMEM((ROWS, BLOCK), F32), pltpu.VMEM((ROWS, D), BF16)],
        "backward", smem=(10,),
    )(*args)


def final(gs, wg):
    row = (64, BLOCK)
    return call(
        final_kernel, [shape((BLOCK, D), BF16)] + [shape((D, D), F32)] * 4, 2,
        [pltpu.VMEM((16,) + row, BF16), pltpu.VMEM((8, D, BLOCK), BF16), pltpu.VMEM((16,) + row, BF16),
         pltpu.VMEM((8, D, BLOCK), BF16), pltpu.VMEM((15,) + row, BF16), pltpu.VMEM((7, D, BLOCK), BF16),
         pltpu.VMEM((8, 8, BLOCK), F32), pltpu.VMEM((7, 8, BLOCK), F32), pltpu.VMEM((8, BLOCK), F32),
         pltpu.VMEM((8, 8, BLOCK), F32), pltpu.VMEM(row, BF16), pltpu.VMEM((2, 16) + row, BF16)]
        + [DMA((n,)) for n in (3, 3, 15, 15, 7, 7, 7, 7, 7, 7, 15, 15)],
        "final", collective_id=4,
    )(gs, wg)


def on_device(ref_feats, src_feats, grad_out, w_query, w_key, w_value, w_out, intersection):
    ref, gout, inter = ref_feats[0], grad_out[0], intersection[0]
    src = gather(src_feats[0])
    q, k, lr, lc = stats(ref, src, w_query, w_key, inter)
    lc = exchange(lc, log_sum, 2)
    v, ga, gvt, cd, rd, matched, w_part = forward(ref, gout, src, q, k, w_value, w_out, inter, lr, lc)
    cd = exchange(cd, plain_sum, 3)
    gref, gs, wg = backward(
        ref, gout, src, q, k, v, ga, w_query, w_key, w_value, inter, lr, lc, rd, cd, gvt, w_part
    )
    gsrc, wqg, wkg, wvg, wog = final(gs, wg)
    return matched[None], gref[None], gsrc[None], wqg, wkg, wvg, wog


def solution(mesh):
    split = P("scan", "blk", None)
    return jax.shard_map(
        on_device, mesh=mesh,
        in_specs=(split, split, split, P(), P(), P(), P(), split),
        out_specs=(split, split, split, P(), P(), P(), P()),
        check_vma=False,
    )
```

```python
import functools
import math

import jax
import jax.numpy as jnp
from jax import lax
from jax.experimental import pallas as pl
from jax.experimental.pallas import tpu as pltpu
from jax.sharding import PartitionSpec as P

HEADS = 4
HEAD_DIM = 64
BLOCK = 128
D = 256
ROWS = 512
KEYS = 2048
TILE = 256
TILES = KEYS // TILE
QBLOCKS = ROWS // BLOCK
KBLOCKS = KEYS // BLOCK
CHIPS = 8
PLANE = 16
NEG = -1.0e30
SCALE = HEAD_DIM**-0.5
UNIT = SCALE * math.log2(math.e)
F32 = jnp.float32
BF16 = jnp.bfloat16
MESH = pl.DeviceIdType.MESH
VMEM = pl.BlockSpec(memory_space=pltpu.VMEM)
SMEM = pl.BlockSpec(memory_space=pltpu.SMEM)
DMA = pltpu.SemaphoreType.DMA


def nn(a, b):
    return jnp.dot(a, b, preferred_element_type=F32)


def nt(a, b):
    return lax.dot_general(a, b, (((1,), (1,)), ((), ())), preferred_element_type=F32)


def by_halves(a, b):
    half = a.shape[0] // 2
    return jnp.concatenate([nn(a[:half], b), nn(a[half:], b)], axis=0)


def lanes_of(rows):
    return lax.broadcasted_iota(jnp.int32, (rows, BLOCK), 1)


def own_lanes(rows, head):
    lane = lanes_of(rows)
    return (lane < HEAD_DIM) if head % 2 == 0 else (lane >= HEAD_DIM)


def spare(head):
    return HEAD_DIM if head % 2 == 0 else 0


def group_cols(head):
    return slice((head // 2) * BLOCK, (head // 2 + 1) * BLOCK)


def head_lanes(head):
    return slice(head * HEAD_DIM, (head + 1) * HEAD_DIM)


def query_extra(inter, head, pieces):
    base = spare(head)
    lane = lanes_of(1)
    grid = []
    for qb in range(QBLOCKS):
        row = jnp.zeros((1, BLOCK), F32)
        for kb in range(KBLOCKS):
            bias = jnp.where(inter[qb, kb] == 1, 0.0, NEG).astype(F32)
            row = jnp.where(lane == base + kb, bias, row)
        grid.append(jnp.broadcast_to(row, (BLOCK, BLOCK)))
    extra = jnp.concatenate(grid, axis=0)
    if pieces is not None:
        lane = lanes_of(ROWS)
        for at, piece in enumerate(pieces):
            extra = jnp.where(lane == base + KBLOCKS + at, piece, extra)
    return extra


def key_extra(tile, head):
    base = spare(head)
    lane = lanes_of(TILE)
    row = lax.broadcasted_iota(jnp.int32, (TILE, BLOCK), 0)
    block = tile * 2 + jnp.where(row >= BLOCK, 1, 0)
    hot = (lane - base == block) | ((lane >= base + KBLOCKS) & (lane < base + KBLOCKS + 3))
    return jnp.where(hot, 1.0, 0.0)


def in_three(value):
    first = value.astype(BF16).astype(F32)
    second = (value - first).astype(BF16).astype(F32)
    third = (value - first - second).astype(BF16).astype(F32)
    return first, second, third


def log_sum(parts):
    peak = functools.reduce(jnp.maximum, parts)
    return peak + jnp.log2(sum(jnp.exp2(part - peak) for part in parts))


def plain_sum(parts):
    return sum(parts)


def pack_weight(wg, core, which, matrix):
    for half in range(2):
        for part in range(4):
            wg[core, 4 * (2 * which + half) + part] = matrix[
                64 * part : 64 * (part + 1), half * BLOCK : (half + 1) * BLOCK
            ].astype(BF16)


def send(src, dst, sems, index, target):
    return pltpu.make_async_remote_copy(
        src_ref=src, dst_ref=dst, send_sem=sems[0].at[index], recv_sem=sems[1].at[index],
        device_id=target, device_id_type=MESH,
    )


def layer_kernel(
    ref, gout, src, wq, wk, wv, wo, inter,
    matched_out, gref_out, gsrc_out, wq_out, wk_out, wv_out, wo_out,
    src_all, k_scr, kh, v_scr, vt_scr, qs, qf, qb_scr, gam, gat_scr, qt_all, t_scr, rm, lr,
    lc_part, lc_swap, lc_chip, lc_in, lc_all, cd_part, cd_swap, cd_chip, cd_in, cd_all,
    att, att_all, gvt_scr, rd_scr, wvg, wkg, gq, gq_all,
    gs_part, gs_swap, gs_sum, gs_in, wg, w_swap, w_sum, w_in, w_part, z_in, w_done, z_all, w_row, w_all,
    own_sem, sa0, ra0, sa1, ra1, sl0, rl0, sl1, rl1, sc0, rc0, sc1, rc1, sg0, rg0, sg1, rg1,
    sp, rp, sx, rx, sz, rz, sy, ry, sb, rb,
):
    blk = lax.axis_index("blk")
    scan = lax.axis_index("scan")
    chip = lax.div(blk, 2)
    core = lax.rem(blk, 2)
    partner = {"blk": chip * 2 + 1 - core}

    def on_chip(offset, core_at):
        return {"blk": lax.rem(chip + offset, CHIPS) * 2 + core_at}

    plane = [{"scan": lax.rem(scan + d, PLANE)} for d in range(1, PLANE)]
    column = [on_chip(d, c) for d in range(1, CHIPS) for c in range(2)]
    barrier = pltpu.get_barrier_semaphore()
    everyone = [partner] + column + plane
    for target in everyone:
        pl.semaphore_signal(barrier, inc=1, device_id=target, device_id_type=MESH)

    q_rows = nn(ref[...], wq[...]).astype(BF16)
    for head in range(HEADS):
        part = q_rows[:, group_cols(head)]
        extra = query_extra(inter, head, None).astype(BF16)
        qs[head] = jnp.where(own_lanes(ROWS, head), part, extra)
    qt_all[...] = q_rows.T
    rm[...] = jnp.full_like(rm, -3.0e38)
    own = pltpu.make_async_copy(src, src_all.at[blk], own_sem)
    own.start()

    pl.semaphore_wait(barrier, len(everyone))
    for d in (4, 3, 5, 2, 6, 1, 7):
        send(src, src_all.at[blk], (sa0, ra0), d, on_chip(d, core)).start()
    send(src, src_all.at[blk], (sa1, ra1), 0, partner).start()

    ga_rows = nt(gout[...], wo[...]).astype(BF16)
    gat_scr[...] = nt(wo[...], gout[...]).astype(BF16)
    for head in range(HEADS):
        part = ga_rows[:, group_cols(head)]
        gam[head] = jnp.where(own_lanes(ROWS, head), part, jnp.zeros_like(part))
    wvt = wv[...].T
    own.wait()

    def near_first(step):
        half = lax.div(step + 1, 2)
        return jnp.where(lax.rem(step, 2) == 1, half, lax.rem(CHIPS - half, CHIPS))

    def far_first(step):
        return jnp.where(lax.rem(step, 2) == 0, 4 + lax.div(step, 2), 4 - lax.div(step + 1, 2))

    def from_offset(d):
        return lax.rem(chip + CHIPS - d, CHIPS)

    def to_offset(d):
        return lax.rem(chip + d, CHIPS)

    def swap_columns(tile, part, swap, sems):
        return send(part.at[tile], swap.at[tile], sems, tile, partner)

    def spread_columns(tile, combine, part, swap, chip_sum, inbox, sems_swap, sems):
        swap_columns(tile, part, swap, sems_swap).wait_recv()
        chip_sum[tile] = combine([part[tile], swap[tile]])
        for d in range(1, CHIPS):
            for c in range(2):
                send(chip_sum.at[tile, core], inbox.at[tile, d - 1, core], sems, tile, on_chip(d, c)).start()

    def collect_columns(tile, combine, chip_sum, inbox, total, sems):
        send(inbox.at[tile], inbox.at[tile], sems, tile, partner).wait_recv()
        total[tile] = combine([chip_sum[tile]] + [inbox[tile, d] for d in range(CHIPS - 1)])

    @pl.loop(0, TILES)
    def _(step):
        d = near_first(step)
        tile = from_offset(d)

        @pl.when(step < TILES - 1)
        def _():
            d_next = near_first(step + 1)
            origin = from_offset(d_next) * 2 + core
            send(src, src_all.at[origin], (sa0, ra0), d_next, partner).wait_recv()
            send(src_all.at[origin], src_all.at[origin], (sa1, ra1), d_next, partner).start()

        send(src, src_all.at[tile * 2 + 1 - core], (sa1, ra1), d, partner).wait_recv()
        rows = src_all[pl.ds(tile * 2, 2)].reshape(TILE, D)
        k_tile = nn(rows, wk[...]).astype(BF16)
        k_scr[tile] = k_tile
        v_scr[tile] = nn(rows, wv[...]).astype(BF16)
        vt_scr[tile] = nt(wvt, rows).astype(BF16)
        for head in range(HEADS):
            keys = jnp.where(own_lanes(TILE, head), k_tile[:, group_cols(head)], key_extra(tile, head).astype(BF16))
            kh[tile, head] = keys
            t = nt(qs[head], keys) * UNIT
            t_scr[tile, head] = t
            rm[head] = jnp.maximum(rm[head], jnp.maximum(t[:, :BLOCK], t[:, BLOCK:]))
            peak = t.max(axis=0, keepdims=True)
            total = jnp.exp2(t - peak).sum(axis=0, keepdims=True)
            lse = peak + jnp.log2(total)
            for kb in range(2):
                lc_part[tile, kb, head : head + 1, :] = lse[:, kb * BLOCK : (kb + 1) * BLOCK]
        swap_columns(tile, lc_part, lc_swap, (sl0, rl0)).start()

        @pl.when(step > 0)
        def _():
            before = from_offset(near_first(step - 1))
            spread_columns(before, log_sum, lc_part, lc_swap, lc_chip, lc_in, (sl0, rl0), (sl1, rl1))

    spread_columns(
        from_offset(4), log_sum, lc_part, lc_swap, lc_chip, lc_in, (sl0, rl0), (sl1, rl1)
    )

    for head in range(HEADS):
        peak = rm[head].max(axis=1, keepdims=True)
        rm[head] = jnp.zeros((ROWS, BLOCK), F32)

        @pl.loop(0, TILES)
        def _(tile):
            rm[head] += jnp.exp2(t_scr[tile, head, :, :BLOCK] - peak) + jnp.exp2(t_scr[tile, head, :, BLOCK:] - peak)

        total = rm[head].sum(axis=1, keepdims=True)
        row_term = peak + jnp.log2(total)
        lr[head] = jnp.broadcast_to(row_term, (ROWS, BLOCK))
        extra = query_extra(inter, head, in_three(row_term * (-1.0 / UNIT))).astype(BF16)
        part = qs[head]
        mask = own_lanes(ROWS, head)
        qb_scr[head] = jnp.where(mask, part, extra)
        qf[head] = jnp.where(mask, part + part, extra)

    att[...] = jnp.zeros_like(att)
    wvg[...] = jnp.zeros_like(wvg)

    @pl.loop(0, TILES)
    def _(tile):
        collect_columns(tile, log_sum, lc_chip, lc_in, lc_all, (sl1, rl1))
        rows = src_all[pl.ds(tile * 2, 2)].reshape(TILE, D)
        for head in range(HEADS):
            lc_row = jnp.concatenate([lc_all[tile, kb, head : head + 1, :] for kb in range(2)], axis=1)
            match = jnp.exp2(nt(qf[head], kh[tile, head]) * UNIT - lc_row).astype(BF16)
            att[head] += by_halves(match, v_scr[tile, :, group_cols(head)])
            gvt = nn(gat_scr[head_lanes(head), :], match)
            gvt_scr[tile, head_lanes(head), :] = gvt.astype(BF16)
            dots = (gvt * vt_scr[tile, head_lanes(head), :].astype(F32)).sum(axis=0, keepdims=True)
            for kb in range(2):
                cd_part[tile, kb, head : head + 1, :] = dots[:, kb * BLOCK : (kb + 1) * BLOCK]
        swap_columns(tile, cd_part, cd_swap, (sc0, rc0)).start()
        wvg[...] += nn(gvt_scr[tile], rows)

        @pl.when(tile > 0)
        def _():
            spread_columns(tile - 1, plain_sum, cd_part, cd_swap, cd_chip, cd_in, (sc0, rc0), (sc1, rc1))

    spread_columns(TILES - 1, plain_sum, cd_part, cd_swap, cd_chip, cd_in, (sc0, rc0), (sc1, rc1))

    for head in range(HEADS):
        mask = own_lanes(ROWS, head)
        value = jnp.where(mask, att[head], 0.0)
        rd = (value * gam[head].astype(F32)).sum(axis=1, keepdims=True)
        rd_scr[head] = jnp.broadcast_to(rd, (ROWS, BLOCK))
        if head % 2 == 0:
            att_all[:, group_cols(head)] = value.astype(BF16)
        else:
            att_all[:, group_cols(head)] = jnp.where(mask, value.astype(BF16), att_all[:, group_cols(head)])
        gam[head] = gam[head] + gam[head]
    matched_out[...] = (ref[...].astype(F32) + nn(att_all[...], wo[...])).astype(BF16)
    pack_weight(wg, 1, 1, nn(att_all[...].T, gout[...]))
    pack_weight(wg, 1, 0, wvg[...].T)
    gq[...] = jnp.zeros_like(gq)
    wkg[...] = jnp.zeros_like(wkg)

    def spread_source(d):
        tile = to_offset(d)
        send(gs_part.at[tile, core], gs_swap.at[tile], (sg0, rg0), tile, partner).wait_recv()
        gs_sum[tile] = (gs_part[tile, core].astype(F32) + gs_swap[tile].astype(F32)).astype(BF16)

    def source_copy(d):
        return send(gs_sum.at[to_offset(d)], gs_in.at[d - 1], (sg1, rg1), d, on_chip(d, core))

    @pl.loop(0, TILES)
    def _(step):
        d = far_first(step)
        tile = to_offset(d)
        collect_columns(tile, plain_sum, cd_chip, cd_in, cd_all, (sc1, rc1))
        rows = src_all[pl.ds(tile * 2, 2)].reshape(TILE, D)
        gk_heads = []
        for head in range(HEADS):
            cols = group_cols(head)
            x = nt(qb_scr[head], kh[tile, head])
            gp = nt(gam[head], v_scr[tile, :, cols])
            lines = []
            for kb in range(2):
                lanes = slice(kb * BLOCK, (kb + 1) * BLOCK)
                lc_row = lc_all[tile, kb, head : head + 1, :]
                cd_row = cd_all[tile, kb, head : head + 1, :]
                u = x[:, lanes] * UNIT
                r = jnp.exp2(u)
                c = jnp.exp2(u + lr[head] - lc_row)
                match = (r * c).astype(BF16).astype(F32)
                lines.append((match * gp[:, lanes] - r * rd_scr[head] - c * cd_row).astype(BF16))
            gs = jnp.concatenate(lines, axis=1)
            gq[head] += by_halves(gs, k_scr[tile, :, cols])
            gk_heads.append((nn(qt_all[head_lanes(head), :], gs) * SCALE).astype(BF16))
        gkt = jnp.concatenate(gk_heads, axis=0)
        wkg[...] += nn(gkt, rows)
        gst = nn(wk[...], gkt) + nn(wv[...], gvt_scr[tile])
        for kb in range(2):
            gs_part[tile, kb] = gst[:, kb * BLOCK : (kb + 1) * BLOCK].astype(BF16)
        send(gs_part.at[tile, 1 - core], gs_swap.at[tile], (sg0, rg0), tile, partner).start()

        @pl.when(step > 0)
        def _():
            d_before = far_first(step - 1)
            spread_source(d_before)
            source_copy(d_before).start()

    for head in range(HEADS):
        mask = own_lanes(ROWS, head)
        value = (gq[head] * SCALE).astype(BF16)
        if head % 2 == 0:
            gq_all[:, group_cols(head)] = value
        else:
            gq_all[:, group_cols(head)] = jnp.where(mask, value, gq_all[:, group_cols(head)])
    pack_weight(wg, 0, 0, nn(ref[...].T, gq_all[...]))
    pack_weight(wg, 0, 1, wkg[...].T)

    copies = []

    def start(*args):
        copy = send(*args)
        copy.start()
        copies.append(copy)
        return copy

    swap = start(wg.at[1 - core], w_swap, (sp, rp), 0, partner)
    gref_out[...] = (gout[...].astype(F32) + nt(gq_all[...], wq[...])).astype(BF16)
    swap.wait_recv()
    w_sum[...] = (wg[core].astype(F32) + w_swap[...].astype(F32)).astype(BF16)
    arrivals = []
    for d in range(1, PLANE):
        arrivals.append(start(w_sum.at[lax.rem(scan + d, PLANE)], w_in.at[d - 1], (sx, rx), d - 1, plane[d - 1]))
    spread_source(0)
    for copy in arrivals:
        copy.wait_recv()
    total = w_sum[scan].astype(F32)
    for d in range(PLANE - 1):
        total = total + w_in[d].astype(F32)
    w_part[...] = total.reshape(CHIPS, 8, BLOCK)
    arrivals = []
    for d in range(1, CHIPS):
        arrivals.append(start(w_part.at[to_offset(d)], z_in.at[d - 1], (sz, rz), d - 1, on_chip(d, core)))
    for copy in arrivals:
        copy.wait_recv()
    total = w_part[chip]
    for d in range(CHIPS - 1):
        total = total + z_in[d]
    w_done[...] = total
    arrivals = []
    for d in range(1, CHIPS):
        arrivals.append(start(w_done, z_all.at[chip], (sy, ry), d - 1, on_chip(d, core)))
    z_all[chip] = total
    for d in (4, 3, 5, 2, 6, 1, 7):
        source_copy(d).wait_recv()
    gsrc = gs_sum[chip].astype(F32)
    for d in range(CHIPS - 1):
        gsrc = gsrc + gs_in[d].astype(F32)
    gsrc_out[...] = gsrc.T.astype(BF16)
    for copy in arrivals:
        copy.wait_recv()
    row = z_all[...].reshape(CHIPS * 8, BLOCK).astype(BF16)
    w_row[...] = row
    arrivals = []
    for d in range(1, PLANE):
        arrivals.append(start(w_row, w_all.at[core, scan], (sb, rb), d - 1, plane[d - 1]))
    w_all[core, scan] = row
    for copy in arrivals:
        copy.wait_recv()
    start(w_all.at[core], w_all.at[core], (sp, rp), 1, partner).wait_recv()
    for core_at, pair in enumerate(((wq_out, wk_out), (wv_out, wo_out))):
        for which, out in enumerate(pair):
            for half in range(2):
                for part in range(4):
                    out[64 * part : 64 * (part + 1), half * BLOCK : (half + 1) * BLOCK] = w_all[
                        core_at, 4 * (2 * which + half) + part
                    ].astype(F32)

    for copy in copies:
        copy.wait_send()

    @pl.loop(0, TILES)
    def _(tile):
        send(src, src_all.at[blk], (sa1, ra1), tile, partner).wait_send()
        swap_columns(tile, lc_part, lc_swap, (sl0, rl0)).wait_send()
        swap_columns(tile, cd_part, cd_swap, (sc0, rc0)).wait_send()
        send(lc_in.at[tile], lc_in.at[tile], (sl1, rl1), tile, partner).wait_send()
        send(cd_in.at[tile], cd_in.at[tile], (sc1, rc1), tile, partner).wait_send()
        send(gs_part.at[tile, core], gs_swap.at[tile], (sg0, rg0), tile, partner).wait_send()

        @pl.when(tile > 0)
        def _():
            send(src, src_all.at[blk], (sa0, ra0), tile, partner).wait_send()
            send(gs_sum.at[tile], gs_in.at[0], (sg1, rg1), tile, partner).wait_send()


def shape(dims, dtype):
    return jax.ShapeDtypeStruct(dims, dtype)


def layer(ref, gout, src, wq, wk, wv, wo, inter):
    vm = pltpu.VMEM
    row = (64, BLOCK)
    heads = (HEADS, ROWS, BLOCK)
    pair = (TILES, 2, HEADS, BLOCK)
    columns = [vm(pair, F32), vm(pair, F32), vm(pair, F32), vm((TILES, CHIPS - 1, 2, HEADS, BLOCK), F32), vm(pair, F32)]
    scratch = [
        vm((2 * CHIPS, BLOCK, D), BF16), vm((TILES, TILE, D), BF16), vm((TILES, HEADS, TILE, BLOCK), BF16),
        vm((TILES, TILE, D), BF16), vm((TILES, D, TILE), BF16), vm(heads, BF16), vm(heads, BF16), vm(heads, BF16),
        vm(heads, BF16), vm((D, ROWS), BF16), vm((D, ROWS), BF16), vm((TILES, HEADS, ROWS, TILE), F32), vm(heads, F32), vm(heads, F32),
        *columns, *columns,
        vm(heads, F32), vm((ROWS, D), BF16), vm((TILES, D, TILE), BF16), vm(heads, F32), vm((D, D), F32),
        vm((D, D), F32), vm(heads, F32), vm((ROWS, D), BF16),
        vm((TILES, 2, D, BLOCK), BF16), vm((TILES, D, BLOCK), BF16), vm((TILES, D, BLOCK), BF16),
        vm((CHIPS - 1, D, BLOCK), BF16),
        vm((2, PLANE) + row, BF16), vm((PLANE,) + row, BF16), vm((PLANE,) + row, BF16), vm((PLANE - 1,) + row, BF16),
        vm((CHIPS, 8, BLOCK), F32), vm((CHIPS - 1, 8, BLOCK), F32), vm((8, BLOCK), F32), vm((CHIPS, 8, BLOCK), F32),
        vm(row, BF16), vm((2, PLANE) + row, BF16),
        DMA,
    ] + [DMA((n,)) for n in (8,) * 16 + (2, 2, 15, 15, 7, 7, 7, 7, 15, 15)]
    return pl.pallas_call(
        layer_kernel,
        out_shape=[shape((ROWS, D), BF16)] * 2 + [shape((BLOCK, D), BF16)] + [shape((D, D), F32)] * 4,
        in_specs=[VMEM] * 7 + [SMEM],
        out_specs=[VMEM] * 7,
        scratch_shapes=scratch,
        compiler_params=pltpu.CompilerParams(vmem_limit_bytes=60 << 20, collective_id=1, has_side_effects=True),
        name="layer",
    )(ref, gout, src, wq, wk, wv, wo, inter)


def on_device(ref_feats, src_feats, grad_out, w_query, w_key, w_value, w_out, intersection):
    matched, gref, gsrc, wqg, wkg, wvg, wog = layer(
        ref_feats[0], grad_out[0], src_feats[0], w_query, w_key, w_value, w_out, intersection[0]
    )
    return matched[None], gref[None], gsrc[None], wqg, wkg, wvg, wog


def solution(mesh):
    split = P("scan", "blk", None)
    return jax.shard_map(
        on_device, mesh=mesh,
        in_specs=(split, split, split, P(), P(), P(), P(), split),
        out_specs=(split, split, split, P(), P(), P(), P()),
        check_vma=False,
    )
```

```python
import functools
import math

import jax
import jax.numpy as jnp
from jax import lax
from jax.experimental import pallas as pl
from jax.experimental.pallas import tpu as pltpu
from jax.sharding import PartitionSpec as P

HEADS = 4
HEAD_DIM = 64
BLOCK = 128
D = 256
ROWS = 512
KEYS = 2048
TILE = 256
TILES = KEYS // TILE
QBLOCKS = ROWS // BLOCK
KBLOCKS = KEYS // BLOCK
CHIPS = 8
PLANE = 16
CHUNK = 32
PIECE = CHUNK // CHIPS
NEG = -1.0e30
SCALE = HEAD_DIM**-0.5
UNIT = SCALE * math.log2(math.e)
F32 = jnp.float32
BF16 = jnp.bfloat16
MESH = pl.DeviceIdType.MESH
VMEM = pl.BlockSpec(memory_space=pltpu.VMEM)
SMEM = pl.BlockSpec(memory_space=pltpu.SMEM)
DMA = pltpu.SemaphoreType.DMA


def nn(a, b):
    return jnp.dot(a, b, preferred_element_type=F32)


def nt(a, b):
    return lax.dot_general(a, b, (((1,), (1,)), ((), ())), preferred_element_type=F32)


def by_halves(a, b):
    half = a.shape[0] // 2
    return jnp.concatenate([nn(a[:half], b), nn(a[half:], b)], axis=0)


def lanes_of(rows):
    return lax.broadcasted_iota(jnp.int32, (rows, BLOCK), 1)


def own_lanes(rows, head):
    lane = lanes_of(rows)
    return (lane < HEAD_DIM) if head % 2 == 0 else (lane >= HEAD_DIM)


def spare(head):
    return HEAD_DIM if head % 2 == 0 else 0


def group_cols(head):
    return slice((head // 2) * BLOCK, (head // 2 + 1) * BLOCK)


def head_lanes(head):
    return slice(head * HEAD_DIM, (head + 1) * HEAD_DIM)


def query_extra(inter, head, pieces):
    base = spare(head)
    lane = lanes_of(1)
    grid = []
    for qb in range(QBLOCKS):
        row = jnp.zeros((1, BLOCK), F32)
        for kb in range(KBLOCKS):
            bias = jnp.where(inter[qb, kb] == 1, 0.0, NEG).astype(F32)
            row = jnp.where(lane == base + kb, bias, row)
        grid.append(jnp.broadcast_to(row, (BLOCK, BLOCK)))
    extra = jnp.concatenate(grid, axis=0)
    if pieces is not None:
        lane = lanes_of(ROWS)
        for at, piece in enumerate(pieces):
            extra = jnp.where(lane == base + KBLOCKS + at, piece, extra)
    return extra


def key_extra(tile, head):
    base = spare(head)
    lane = lanes_of(TILE)
    row = lax.broadcasted_iota(jnp.int32, (TILE, BLOCK), 0)
    block = tile * 2 + jnp.where(row >= BLOCK, 1, 0)
    hot = (lane - base == block) | ((lane >= base + KBLOCKS) & (lane < base + KBLOCKS + 3))
    return jnp.where(hot, 1.0, 0.0)


def in_three(value):
    first = value.astype(BF16).astype(F32)
    second = (value - first).astype(BF16).astype(F32)
    third = (value - first - second).astype(BF16).astype(F32)
    return first, second, third


def log_sum(parts):
    peak = functools.reduce(jnp.maximum, parts)
    return peak + jnp.log2(sum(jnp.exp2(part - peak) for part in parts))


def plain_sum(parts):
    return sum(parts)


def pack_weight(wg, core, matrix):
    for half in range(2):
        for part in range(8):
            wg[core, 8 * half + part] = matrix[
                CHUNK * part : CHUNK * (part + 1), half * BLOCK : (half + 1) * BLOCK
            ].astype(BF16)


def unpack_weight(out, packed, core):
    for half in range(2):
        for part in range(8):
            out[CHUNK * part : CHUNK * (part + 1), half * BLOCK : (half + 1) * BLOCK] = packed[
                core, 8 * half + part
            ].astype(F32)


def send(src, dst, sems, index, target):
    return pltpu.make_async_remote_copy(
        src_ref=src, dst_ref=dst, send_sem=sems[0].at[index], recv_sem=sems[1].at[index],
        device_id=target, device_id_type=MESH,
    )


def layer_kernel(
    ref, gout, src, wq, wk, wv, wo, inter,
    matched_out, gref_out, gsrc_out, early_out, late_out,
    src_all, k_scr, kh, v_scr, vt_scr, qs, qf, qb_scr, gam, gat_scr, qt_all, t_scr, rm, lr,
    lc_part, lc_swap, lc_chip, lc_in, lc_all, cd_part, cd_swap, cd_chip, cd_in, cd_all,
    att, att_all, gvt_scr, rd_scr, wvg, wkg, gq, gq_all,
    gs_part, gs_swap, gs_sum, gs_in, *rest,
):
    early_bufs, late_bufs, rest = rest[:10], rest[10:20], rest[20:]
    own_sem, sa0, ra0, sa1, ra1, sl0, rl0, sl1, rl1, sc0, rc0, sc1, rc1, sg0, rg0, sg1, rg1 = rest[:17]
    early_sems, late_sems = rest[17:27], rest[27:37]
    blk = lax.axis_index("blk")
    scan = lax.axis_index("scan")
    chip = lax.div(blk, 2)
    core = lax.rem(blk, 2)
    partner = {"blk": chip * 2 + 1 - core}

    def on_chip(offset, core_at):
        return {"blk": lax.rem(chip + offset, CHIPS) * 2 + core_at}

    def from_offset(d):
        return lax.rem(chip + CHIPS - d, CHIPS)

    def to_offset(d):
        return lax.rem(chip + d, CHIPS)

    def ring_copy(block, way, hops, piece, source=None):
        rows = pl.ds(piece * (BLOCK // 2), BLOCK // 2)
        landing = src_all.at[block, rows]
        return send(
            landing if source is None else source.at[rows], landing, (sa0, ra0),
            way * 8 + (hops - 1) * 2 + piece, on_chip(1 if way == 0 else CHIPS - 1, core),
        )

    def pieces_of(way, hops):
        return range(2) if hops < 4 else (way,)

    def relay(hops):
        for way in range(2):
            origin = from_offset(hops if way == 0 else CHIPS - hops) * 2 + core
            for piece in pieces_of(way, hops):
                ring_copy(origin, way, hops, piece).wait_recv()
                if hops < 4 and piece in pieces_of(way, hops + 1):
                    ring_copy(origin, way, hops + 1, piece).start()
        for d in (hops, CHIPS - hops) if hops < 4 else (hops,):
            origin = from_offset(d) * 2 + core
            send(src_all.at[origin], src_all.at[origin], (sa1, ra1), d, partner).start()

    plane = [{"scan": lax.rem(scan + d, PLANE)} for d in range(1, PLANE)]
    column = [on_chip(d, c) for d in range(1, CHIPS) for c in range(2)]
    barrier = pltpu.get_barrier_semaphore()
    everyone = [partner] + column + plane
    for target in everyone:
        pl.semaphore_signal(barrier, inc=1, device_id=target, device_id_type=MESH)

    def all_reduce(bufs, sems):
        wg, w_swap, w_sum, w_in, w_part, z_in, w_done, z_all, w_row, w_all = bufs
        swap_sems, in_sems, z_sems, back_sems, out_sems = [sems[2 * i : 2 * i + 2] for i in range(5)]
        swap = [
            send(wg.at[1 - core], w_swap, swap_sems, 0, partner),
            send(w_all.at[core], w_all.at[core], swap_sems, 1, partner),
        ]

        def in_plane(d):
            return send(w_sum.at[lax.rem(scan + d, PLANE)], w_in.at[d - 1], in_sems, d - 1, plane[d - 1])

        def in_column(d):
            return send(w_part.at[to_offset(d)], z_in.at[d - 1], z_sems, d - 1, on_chip(d, core))

        def back_column(d):
            return send(w_done, z_all.at[chip], back_sems, d - 1, on_chip(d, core))

        def back_plane(d):
            return send(w_row, w_all.at[core, scan], out_sems, d - 1, plane[d - 1])

        def stage_1():
            swap[0].wait_recv()
            w_sum[...] = (wg[core].astype(F32) + w_swap[...].astype(F32)).astype(BF16)
            for d in range(1, PLANE):
                in_plane(d).start()

        def stage_2():
            for d in range(1, PLANE):
                in_plane(d).wait_recv()
            total = w_sum[scan].astype(F32)
            for d in range(PLANE - 1):
                total = total + w_in[d].astype(F32)
            for c in range(CHIPS):
                w_part[c] = total[c * PIECE : (c + 1) * PIECE, :]
            for d in range(1, CHIPS):
                in_column(d).start()

        def stage_3():
            for d in range(1, CHIPS):
                in_column(d).wait_recv()
            total = w_part[chip]
            for d in range(CHIPS - 1):
                total = total + z_in[d]
            w_done[...] = total
            z_all[chip] = total
            for d in range(1, CHIPS):
                back_column(d).start()

        def stage_4():
            for d in range(1, CHIPS):
                back_column(d).wait_recv()
            row = jnp.concatenate([z_all[c] for c in range(CHIPS)], axis=0).astype(BF16)
            w_row[...] = row
            w_all[core, scan] = row
            for d in range(1, PLANE):
                back_plane(d).start()

        def stage_5():
            for d in range(1, PLANE):
                back_plane(d).wait_recv()
            swap[1].start()

        def left():
            for copy in swap:
                copy.wait_send()
            for make, count in ((in_plane, PLANE), (in_column, CHIPS), (back_column, CHIPS), (back_plane, PLANE)):
                for d in range(1, count):
                    make(d).wait_send()

        return swap[0].start, stage_1, stage_2, stage_3, stage_4, stage_5, swap[1].wait_recv, left

    q_rows = nn(ref[...], wq[...]).astype(BF16)
    for head in range(HEADS):
        part = q_rows[:, group_cols(head)]
        extra = query_extra(inter, head, None).astype(BF16)
        qs[head] = jnp.where(own_lanes(ROWS, head), part, extra)
    qt_all[...] = q_rows.T
    rm[...] = jnp.full_like(rm, -3.0e38)
    own = pltpu.make_async_copy(src, src_all.at[blk], own_sem)
    own.start()

    pl.semaphore_wait(barrier, len(everyone))
    for piece in range(2):
        for way in range(2):
            ring_copy(blk, way, 1, piece, src).start()
    send(src, src_all.at[blk], (sa1, ra1), 0, partner).start()

    ga_rows = nt(gout[...], wo[...]).astype(BF16)
    gat_scr[...] = nt(wo[...], gout[...]).astype(BF16)
    for head in range(HEADS):
        part = ga_rows[:, group_cols(head)]
        gam[head] = jnp.where(own_lanes(ROWS, head), part, jnp.zeros_like(part))
    wvt = wv[...].T
    own.wait()

    def near_first(step):
        half = lax.div(step + 1, 2)
        return jnp.where(lax.rem(step, 2) == 1, half, lax.rem(CHIPS - half, CHIPS))

    def by_quarters(step):
        return lax.div(step, 4) * 4 + lax.rem(chip + 1 + step, 4)

    def swap_columns(tile, part, swap, sems):
        return send(part.at[tile], swap.at[tile], sems, tile, partner)

    def spread_columns(tile, combine, part, swap, chip_sum, inbox, sems_swap, sems):
        swap_columns(tile, part, swap, sems_swap).wait_recv()
        chip_sum[tile] = combine([part[tile], swap[tile]])
        for d in range(1, CHIPS):
            for c in range(2):
                send(chip_sum.at[tile, core], inbox.at[tile, d - 1, core], sems, tile, on_chip(d, c)).start()

    def collect_columns(tile, combine, chip_sum, inbox, total, sems):
        send(inbox.at[tile], inbox.at[tile], sems, tile, partner).wait_recv()
        total[tile] = combine([chip_sum[tile]] + [inbox[tile, d] for d in range(CHIPS - 1)])

    @pl.loop(0, TILES)
    def _(step):
        d = near_first(step)
        tile = from_offset(d)

        for at, hops in ((1, 1), (2, 2), (4, 3), (6, 4)):

            @pl.when(step == at)
            def _():
                relay(hops)

        send(src, src_all.at[tile * 2 + 1 - core], (sa1, ra1), d, partner).wait_recv()
        rows = src_all[pl.ds(tile * 2, 2)].reshape(TILE, D)
        k_tile = nn(rows, wk[...]).astype(BF16)
        k_scr[tile] = k_tile
        v_scr[tile] = nn(rows, wv[...]).astype(BF16)
        vt_scr[tile] = nt(wvt, rows).astype(BF16)
        for head in range(HEADS):
            keys = jnp.where(own_lanes(TILE, head), k_tile[:, group_cols(head)], key_extra(tile, head).astype(BF16))
            kh[tile, head] = keys
            t = nt(qs[head], keys) * UNIT
            t_scr[tile, head] = t
            rm[head] = jnp.maximum(rm[head], jnp.maximum(t[:, :BLOCK], t[:, BLOCK:]))
            peak = t.max(axis=0, keepdims=True)
            total = jnp.exp2(t - peak).sum(axis=0, keepdims=True)
            lse = peak + jnp.log2(total)
            for kb in range(2):
                lc_part[tile, kb, head : head + 1, :] = lse[:, kb * BLOCK : (kb + 1) * BLOCK]
        swap_columns(tile, lc_part, lc_swap, (sl0, rl0)).start()

        @pl.when(step > 0)
        def _():
            before = from_offset(near_first(step - 1))
            spread_columns(before, log_sum, lc_part, lc_swap, lc_chip, lc_in, (sl0, rl0), (sl1, rl1))

    spread_columns(
        from_offset(4), log_sum, lc_part, lc_swap, lc_chip, lc_in, (sl0, rl0), (sl1, rl1)
    )

    for head in range(HEADS):
        peak = rm[head].max(axis=1, keepdims=True)
        rm[head] = jnp.zeros((ROWS, BLOCK), F32)

        @pl.loop(0, TILES)
        def _(tile):
            rm[head] += jnp.exp2(t_scr[tile, head, :, :BLOCK] - peak) + jnp.exp2(t_scr[tile, head, :, BLOCK:] - peak)

        total = rm[head].sum(axis=1, keepdims=True)
        row_term = peak + jnp.log2(total)
        lr[head] = jnp.broadcast_to(row_term, (ROWS, BLOCK))
        extra = query_extra(inter, head, in_three(row_term * (-1.0 / UNIT))).astype(BF16)
        part = qs[head]
        mask = own_lanes(ROWS, head)
        qb_scr[head] = jnp.where(mask, part, extra)
        qf[head] = jnp.where(mask, part + part, extra)

    att[...] = jnp.zeros_like(att)
    wvg[...] = jnp.zeros_like(wvg)

    @pl.loop(0, TILES)
    def _(tile):
        collect_columns(tile, log_sum, lc_chip, lc_in, lc_all, (sl1, rl1))
        rows = src_all[pl.ds(tile * 2, 2)].reshape(TILE, D)
        for head in range(HEADS):
            lc_row = jnp.concatenate([lc_all[tile, kb, head : head + 1, :] for kb in range(2)], axis=1)
            match = jnp.exp2(nt(qf[head], kh[tile, head]) * UNIT - lc_row).astype(BF16)
            att[head] += by_halves(match, v_scr[tile, :, group_cols(head)])
            gvt = nn(gat_scr[head_lanes(head), :], match)
            gvt_scr[tile, head_lanes(head), :] = gvt.astype(BF16)
            dots = (gvt * vt_scr[tile, head_lanes(head), :].astype(F32)).sum(axis=0, keepdims=True)
            for kb in range(2):
                cd_part[tile, kb, head : head + 1, :] = dots[:, kb * BLOCK : (kb + 1) * BLOCK]
        swap_columns(tile, cd_part, cd_swap, (sc0, rc0)).start()
        wvg[...] += nn(gvt_scr[tile], rows)

        @pl.when(tile > 0)
        def _():
            spread_columns(tile - 1, plain_sum, cd_part, cd_swap, cd_chip, cd_in, (sc0, rc0), (sc1, rc1))

    spread_columns(TILES - 1, plain_sum, cd_part, cd_swap, cd_chip, cd_in, (sc0, rc0), (sc1, rc1))

    for head in range(HEADS):
        mask = own_lanes(ROWS, head)
        value = jnp.where(mask, att[head], 0.0)
        rd = (value * gam[head].astype(F32)).sum(axis=1, keepdims=True)
        rd_scr[head] = jnp.broadcast_to(rd, (ROWS, BLOCK))
        if head % 2 == 0:
            att_all[:, group_cols(head)] = value.astype(BF16)
        else:
            att_all[:, group_cols(head)] = jnp.where(mask, value.astype(BF16), att_all[:, group_cols(head)])
        gam[head] = gam[head] + gam[head]
    matched_out[...] = (ref[...].astype(F32) + nn(att_all[...], wo[...])).astype(BF16)
    pack_weight(early_bufs[0], 1, nn(att_all[...].T, gout[...]))
    pack_weight(early_bufs[0], 0, wvg[...].T)
    early = all_reduce(early_bufs, early_sems)
    early[0]()
    gq[...] = jnp.zeros_like(gq)
    wkg[...] = jnp.zeros_like(wkg)

    def source_copy(d):
        return send(gs_sum.at[to_offset(d)], gs_in.at[d - 1], (sg1, rg1), d, on_chip(d, core))

    def spread_source(tile):
        send(gs_part.at[tile, core], gs_swap.at[tile], (sg0, rg0), tile, partner).wait_recv()
        gs_sum[tile] = (gs_part[tile, core].astype(F32) + gs_swap[tile].astype(F32)).astype(BF16)
        d = lax.rem(tile + CHIPS - chip, CHIPS)

        @pl.when(d > 0)
        def _():
            source_copy(d).start()

    @pl.loop(0, TILES)
    def _(step):
        tile = by_quarters(step)
        for at, stage in ((1, 1), (3, 2), (6, 3)):

            @pl.when(step == at)
            def _():
                early[stage]()

        collect_columns(tile, plain_sum, cd_chip, cd_in, cd_all, (sc1, rc1))
        rows = src_all[pl.ds(tile * 2, 2)].reshape(TILE, D)
        gk_heads = []
        for head in range(HEADS):
            cols = group_cols(head)
            x = nt(qb_scr[head], kh[tile, head])
            gp = nt(gam[head], v_scr[tile, :, cols])
            lines = []
            for kb in range(2):
                lanes = slice(kb * BLOCK, (kb + 1) * BLOCK)
                lc_row = lc_all[tile, kb, head : head + 1, :]
                cd_row = cd_all[tile, kb, head : head + 1, :]
                u = x[:, lanes] * UNIT
                r = jnp.exp2(u)
                c = jnp.exp2(u + lr[head] - lc_row)
                match = (r * c).astype(BF16).astype(F32)
                lines.append((match * gp[:, lanes] - r * rd_scr[head] - c * cd_row).astype(BF16))
            gs = jnp.concatenate(lines, axis=1)
            gq[head] += by_halves(gs, k_scr[tile, :, cols])
            gk_heads.append((nn(qt_all[head_lanes(head), :], gs) * SCALE).astype(BF16))
        gkt = jnp.concatenate(gk_heads, axis=0)
        wkg[...] += nn(gkt, rows)
        gst = nn(wk[...], gkt) + nn(wv[...], gvt_scr[tile])
        for kb in range(2):
            gs_part[tile, kb] = gst[:, kb * BLOCK : (kb + 1) * BLOCK].astype(BF16)
        send(gs_part.at[tile, 1 - core], gs_swap.at[tile], (sg0, rg0), tile, partner).start()

        @pl.when(step > 0)
        def _():
            spread_source(by_quarters(step - 1))

    for head in range(HEADS):
        mask = own_lanes(ROWS, head)
        value = (gq[head] * SCALE).astype(BF16)
        if head % 2 == 0:
            gq_all[:, group_cols(head)] = value
        else:
            gq_all[:, group_cols(head)] = jnp.where(mask, value, gq_all[:, group_cols(head)])
    pack_weight(late_bufs[0], 0, nn(ref[...].T, gq_all[...]))
    pack_weight(late_bufs[0], 1, wkg[...].T)
    late = all_reduce(late_bufs, late_sems)
    late[0]()
    early[4]()
    gref_out[...] = (gout[...].astype(F32) + nt(gq_all[...], wq[...])).astype(BF16)
    late[1]()
    spread_source(by_quarters(TILES - 1))
    early[5]()
    late[2]()
    late[3]()
    for d in (4, 3, 5, 2, 6, 1, 7):
        source_copy(d).wait_recv()
    gsrc = gs_sum[chip].astype(F32)
    for d in range(CHIPS - 1):
        gsrc = gsrc + gs_in[d].astype(F32)
    gsrc_out[...] = gsrc.T.astype(BF16)
    early[6]()
    early_out[...] = early_bufs[-1][...]
    late[4]()
    late[5]()
    late[6]()
    late_out[...] = late_bufs[-1][...]

    early[7]()
    late[7]()
    for way in range(2):
        for hops in range(1, 5):
            for piece in pieces_of(way, hops):
                ring_copy(blk, way, hops, piece).wait_send()

    @pl.loop(0, TILES)
    def _(tile):
        send(src, src_all.at[blk], (sa1, ra1), tile, partner).wait_send()
        swap_columns(tile, lc_part, lc_swap, (sl0, rl0)).wait_send()
        swap_columns(tile, cd_part, cd_swap, (sc0, rc0)).wait_send()
        send(lc_in.at[tile], lc_in.at[tile], (sl1, rl1), tile, partner).wait_send()
        send(cd_in.at[tile], cd_in.at[tile], (sc1, rc1), tile, partner).wait_send()
        send(gs_part.at[tile, core], gs_swap.at[tile], (sg0, rg0), tile, partner).wait_send()

        @pl.when(tile > 0)
        def _():
            send(gs_sum.at[tile], gs_in.at[0], (sg1, rg1), tile, partner).wait_send()


def shape(dims, dtype):
    return jax.ShapeDtypeStruct(dims, dtype)


def layer(ref, gout, src, wq, wk, wv, wo, inter):
    vm = pltpu.VMEM
    row = (CHUNK, BLOCK)
    reduction = [
        vm((2, PLANE) + row, BF16), vm((PLANE,) + row, BF16), vm((PLANE,) + row, BF16), vm((PLANE - 1,) + row, BF16),
        vm((CHIPS, PIECE, BLOCK), F32), vm((CHIPS - 1, PIECE, BLOCK), F32), vm((PIECE, BLOCK), F32),
        vm((CHIPS, PIECE, BLOCK), F32), vm(row, BF16), vm((2, PLANE) + row, BF16),
    ]
    heads = (HEADS, ROWS, BLOCK)
    pair = (TILES, 2, HEADS, BLOCK)
    columns = [vm(pair, F32), vm(pair, F32), vm(pair, F32), vm((TILES, CHIPS - 1, 2, HEADS, BLOCK), F32), vm(pair, F32)]
    scratch = [
        vm((2 * CHIPS, BLOCK, D), BF16), vm((TILES, TILE, D), BF16), vm((TILES, HEADS, TILE, BLOCK), BF16),
        vm((TILES, TILE, D), BF16), vm((TILES, D, TILE), BF16), vm(heads, BF16), vm(heads, BF16), vm(heads, BF16),
        vm(heads, BF16), vm((D, ROWS), BF16), vm((D, ROWS), BF16), vm((TILES, HEADS, ROWS, TILE), F32), vm(heads, F32), vm(heads, F32),
        *columns, *columns,
        vm(heads, F32), vm((ROWS, D), BF16), vm((TILES, D, TILE), BF16), vm(heads, F32), vm((D, D), F32),
        vm((D, D), F32), vm(heads, F32), vm((ROWS, D), BF16),
        vm((TILES, 2, D, BLOCK), BF16), vm((TILES, D, BLOCK), BF16), vm((TILES, D, BLOCK), BF16),
        vm((CHIPS - 1, D, BLOCK), BF16),
        *reduction, *reduction,
        DMA, DMA((16,)), DMA((16,)),
    ] + [DMA((n,)) for n in (8,) * 14 + 2 * (2, 2, 15, 15, 7, 7, 7, 7, 15, 15)]
    return pl.pallas_call(
        layer_kernel,
        out_shape=[shape((ROWS, D), BF16)] * 2 + [shape((BLOCK, D), BF16)] + [shape((2, PLANE) + row, BF16)] * 2,
        in_specs=[VMEM] * 7 + [SMEM],
        out_specs=[VMEM] * 5,
        scratch_shapes=scratch,
        compiler_params=pltpu.CompilerParams(vmem_limit_bytes=60 << 20, collective_id=1, has_side_effects=True),
        name="layer",
    )(ref, gout, src, wq, wk, wv, wo, inter)


def finish_kernel(matched, gref, gsrc, early, late, matched_out, gref_out, gsrc_out, wq_out, wk_out, wv_out, wo_out):
    matched_out[...] = matched[...]
    gref_out[...] = gref[...]
    gsrc_out[...] = gsrc[...]
    unpack_weight(wq_out, late, 0)
    unpack_weight(wk_out, late, 1)
    unpack_weight(wv_out, early, 0)
    unpack_weight(wo_out, early, 1)


def finish(*parts):
    return pl.pallas_call(
        finish_kernel,
        out_shape=[shape((ROWS, D), BF16)] * 2 + [shape((BLOCK, D), BF16)] + [shape((D, D), F32)] * 4,
        in_specs=[VMEM] * 5,
        out_specs=[VMEM] * 7,
        compiler_params=pltpu.CompilerParams(vmem_limit_bytes=32 << 20),
        name="finish",
    )(*parts)


def on_device(ref_feats, src_feats, grad_out, w_query, w_key, w_value, w_out, intersection):
    parts = layer(ref_feats[0], grad_out[0], src_feats[0], w_query, w_key, w_value, w_out, intersection[0])
    matched, gref, gsrc, wqg, wkg, wvg, wog = finish(*parts)
    return matched[None], gref[None], gsrc[None], wqg, wkg, wvg, wog


def solution(mesh):
    split = P("scan", "blk", None)
    return jax.shard_map(
        on_device, mesh=mesh,
        in_specs=(split, split, split, P(), P(), P(), P(), split),
        out_specs=(split, split, split, P(), P(), P(), P()),
        check_vma=False,
    )
```

```python
import functools
import math

import jax
import jax.numpy as jnp
from jax import lax
from jax.experimental import pallas as pl
from jax.experimental.pallas import tpu as pltpu
from jax.sharding import PartitionSpec as P

HEADS = 4
HEAD_DIM = 64
BLOCK = 128
D = 256
ROWS = 512
KEYS = 2048
TILE = 256
TILES = KEYS // TILE
QBLOCKS = ROWS // BLOCK
KBLOCKS = KEYS // BLOCK
CHIPS = 8
PLANE = 16
CHUNK = 32
OUT_ROWS = 2 * ROWS + BLOCK + 4 * D
NEG = -1.0e30
SCALE = HEAD_DIM**-0.5
UNIT = SCALE * math.log2(math.e)
F32 = jnp.float32
BF16 = jnp.bfloat16
MESH = pl.DeviceIdType.MESH
VMEM = pl.BlockSpec(memory_space=pltpu.VMEM)
SMEM = pl.BlockSpec(memory_space=pltpu.SMEM)
DMA = pltpu.SemaphoreType.DMA


def nn(a, b):
    return jnp.dot(a, b, preferred_element_type=F32)


def nt(a, b):
    return lax.dot_general(a, b, (((1,), (1,)), ((), ())), preferred_element_type=F32)


def lanes_of(rows):
    return lax.broadcasted_iota(jnp.int32, (rows, BLOCK), 1)


def own_lanes(rows, head):
    lane = lanes_of(rows)
    return (lane < HEAD_DIM) if head % 2 == 0 else (lane >= HEAD_DIM)


def spare(head):
    return HEAD_DIM if head % 2 == 0 else 0


def group_cols(head):
    return slice((head // 2) * BLOCK, (head // 2 + 1) * BLOCK)


def head_lanes(head):
    return slice(head * HEAD_DIM, (head + 1) * HEAD_DIM)


def query_extra(inter, head, pieces):
    base = spare(head)
    lane = lanes_of(1)
    grid = []
    for qb in range(QBLOCKS):
        row = jnp.zeros((1, BLOCK), F32)
        for kb in range(KBLOCKS):
            bias = jnp.where(inter[qb, kb] == 1, 0.0, NEG).astype(F32)
            row = jnp.where(lane == base + kb, bias, row)
        grid.append(jnp.broadcast_to(row, (BLOCK, BLOCK)))
    extra = jnp.concatenate(grid, axis=0)
    if pieces is not None:
        lane = lanes_of(ROWS)
        for at, piece in enumerate(pieces):
            extra = jnp.where(lane == base + KBLOCKS + at, piece, extra)
    return extra


def key_extra(tile, head):
    base = spare(head)
    lane = lanes_of(TILE)
    row = lax.broadcasted_iota(jnp.int32, (TILE, BLOCK), 0)
    block = tile * 2 + jnp.where(row >= BLOCK, 1, 0)
    hot = (lane - base == block) | ((lane >= base + KBLOCKS) & (lane < base + KBLOCKS + 3))
    return jnp.where(hot, 1.0, 0.0)


def in_three(value):
    first = value.astype(BF16).astype(F32)
    second = (value - first).astype(BF16).astype(F32)
    third = (value - first - second).astype(BF16).astype(F32)
    return first, second, third


def log_sum(parts):
    peak = functools.reduce(jnp.maximum, parts)
    return peak + jnp.log2(sum(jnp.exp2(part - peak) for part in parts))


def plain_sum(parts):
    return sum(parts)


def pack_weight(wg, core, matrix):
    for half in range(2):
        for part in range(8):
            wg[core, 8 * half + part] = matrix[
                CHUNK * part : CHUNK * (part + 1), half * BLOCK : (half + 1) * BLOCK
            ].astype(BF16)


def put_weights(out, packed, pair):
    for core in range(2):
        first = 2 * ROWS + BLOCK + (2 * pair + core) * D
        for half in range(2):
            for part in range(8):
                out[first + CHUNK * part : first + CHUNK * (part + 1), half * BLOCK : (half + 1) * BLOCK] = packed[
                    core, 8 * half + part
                ]


def in_turn(make, use):
    make(0)
    for head in range(HEADS):
        if head + 1 < HEADS:
            make(head + 1)
        use(head)


def send(src, dst, sems, index, target):
    return pltpu.make_async_remote_copy(
        src_ref=src, dst_ref=dst, send_sem=sems[0].at[index], recv_sem=sems[1].at[index],
        device_id=target, device_id_type=MESH,
    )


def layer_kernel(
    ref, gout, src, wq, wk, wv, wo, inter,
    out,
    src_all, kt_scr, kh, v_scr, vt_scr, qs, qf, qb_scr, gam, gat_scr, qt_all, t_scr, rm, lr,
    lc_part, lc_swap, lc_chip, lc_in, lc_all, cd_part, cd_swap, cd_chip, cd_in, cd_all,
    att, match_scr, gvt_scr, rd_scr, wvg, wkg, gq,
    gs_part, gs_swap, gs_sum, gs_in, *rest,
):
    early_bufs, late_bufs, rest = rest[:8], rest[8:16], rest[16:]
    own_sem, sa0, ra0, sa1, ra1, sl0, rl0, sl1, rl1, sc0, rc0, sc1, rc1, sg0, rg0, sg1, rg1 = rest[:17]
    early_sems, late_sems = rest[17:25], rest[25:33]
    blk = lax.axis_index("blk")
    scan = lax.axis_index("scan")
    chip = lax.div(blk, 2)
    core = lax.rem(blk, 2)
    partner = {"blk": chip * 2 + 1 - core}

    def on_chip(offset, core_at):
        return {"blk": lax.rem(chip + offset, CHIPS) * 2 + core_at}

    def from_offset(d):
        return lax.rem(chip + CHIPS - d, CHIPS)

    def to_offset(d):
        return lax.rem(chip + d, CHIPS)

    def ring_copy(block, way, hops, piece, source=None):
        rows = pl.ds(piece * (BLOCK // 2), BLOCK // 2)
        landing = src_all.at[block, rows]
        return send(
            landing if source is None else source.at[rows], landing, (sa0, ra0),
            way * 8 + (hops - 1) * 2 + piece, on_chip(1 if way == 0 else CHIPS - 1, core),
        )

    def pieces_of(way, hops):
        return range(2) if hops < 4 else (way,)

    def relay(hops):
        for way in range(2):
            origin = from_offset(hops if way == 0 else CHIPS - hops) * 2 + core
            for piece in pieces_of(way, hops):
                ring_copy(origin, way, hops, piece).wait_recv()
                if hops < 4 and piece in pieces_of(way, hops + 1):
                    ring_copy(origin, way, hops + 1, piece).start()
        for d in (hops, CHIPS - hops) if hops < 4 else (hops,):
            origin = from_offset(d) * 2 + core
            send(src_all.at[origin], src_all.at[origin], (sa1, ra1), d, partner).start()

    plane = [{"scan": lax.rem(scan + d, PLANE)} for d in range(1, PLANE)]
    column = [on_chip(d, c) for d in range(1, CHIPS) for c in range(2)]
    barrier = pltpu.get_barrier_semaphore()
    everyone = [partner] + column + plane
    for target in everyone:
        pl.semaphore_signal(barrier, inc=1, device_id=target, device_id_type=MESH)

    def all_reduce(bufs, sems):
        wg, w_swap, w_sum, w_in, w_part, z_all, w_row, w_all = bufs
        swap_sems, in_sems, z_sems, out_sems = [sems[2 * i : 2 * i + 2] for i in range(4)]
        swap = [
            send(wg.at[1 - core], w_swap, swap_sems, 0, partner),
            send(w_all.at[core], w_all.at[core], swap_sems, 1, partner),
        ]

        def in_plane(d):
            return send(w_sum.at[lax.rem(scan + d, PLANE)], w_in.at[d - 1], in_sems, d - 1, plane[d - 1])

        def in_column(d):
            return send(w_part, z_all.at[chip], z_sems, d - 1, on_chip(d, core))

        def back_plane(d):
            return send(w_row, w_all.at[core, scan], out_sems, d - 1, plane[d - 1])

        def stage_1():
            swap[0].wait_recv()
            w_sum[...] = (wg[core].astype(F32) + w_swap[...].astype(F32)).astype(BF16)
            for d in range(1, PLANE):
                in_plane(d).start()

        def stage_2():
            for d in range(1, PLANE):
                in_plane(d).wait_recv()
            total = w_sum[scan].astype(F32)
            for d in range(PLANE - 1):
                total = total + w_in[d].astype(F32)
            part = total.astype(BF16)
            w_part[...] = part
            z_all[chip] = part
            for d in range(1, CHIPS):
                in_column(d).start()

        def stage_3():
            for d in range(1, CHIPS):
                in_column(d).wait_recv()
            total = z_all[0].astype(F32)
            for c in range(1, CHIPS):
                total = total + z_all[c].astype(F32)
            row = total.astype(BF16)
            w_row[...] = row
            w_all[core, scan] = row
            for d in range(1, PLANE):
                back_plane(d).start()

        def stage_4():
            for d in range(1, PLANE):
                back_plane(d).wait_recv()
            swap[1].start()

        def left():
            for copy in swap:
                copy.wait_send()
            for make, count in ((in_plane, PLANE), (in_column, CHIPS), (back_plane, PLANE)):
                for d in range(1, count):
                    make(d).wait_send()

        return swap[0].start, stage_1, stage_2, stage_3, stage_4, swap[1].wait_recv, left

    q_rows = nn(ref[...], wq[...]).astype(BF16)
    for head in range(HEADS):
        part = q_rows[:, group_cols(head)]
        extra = query_extra(inter, head, None).astype(BF16)
        qs[head] = jnp.where(own_lanes(ROWS, head), part, extra)
    qt_all[...] = q_rows.T
    rm[...] = jnp.full_like(rm, -3.0e38)
    own = pltpu.make_async_copy(src, src_all.at[blk], own_sem)
    own.start()

    pl.semaphore_wait(barrier, len(everyone))
    for piece in range(2):
        for way in range(2):
            ring_copy(blk, way, 1, piece, src).start()
    send(src, src_all.at[blk], (sa1, ra1), 0, partner).start()

    ga_rows = nt(gout[...], wo[...]).astype(BF16)
    gat_scr[...] = nt(wo[...], gout[...]).astype(BF16)
    for head in range(HEADS):
        part = ga_rows[:, group_cols(head)]
        gam[head] = jnp.where(own_lanes(ROWS, head), part, jnp.zeros_like(part))
    wvt = wv[...].T
    wkt = wk[...].T
    own.wait()

    def near_first(step):
        half = lax.div(step + 1, 2)
        return jnp.where(lax.rem(step, 2) == 1, half, lax.rem(CHIPS - half, CHIPS))

    def by_quarters(step):
        return lax.div(step, 4) * 4 + lax.rem(chip + 1 + step, 4)

    def swap_columns(tile, part, swap, sems):
        return send(part.at[tile], swap.at[tile], sems, tile, partner)

    def spread_columns(tile, combine, part, swap, chip_sum, inbox, sems_swap, sems):
        swap_columns(tile, part, swap, sems_swap).wait_recv()
        chip_sum[tile] = combine([part[tile], swap[tile]])
        for d in range(1, CHIPS):
            for c in range(2):
                send(chip_sum.at[tile, core], inbox.at[tile, d - 1, core], sems, tile, on_chip(d, c)).start()

    def collect_columns(tile, combine, chip_sum, inbox, total, sems):
        send(inbox.at[tile], inbox.at[tile], sems, tile, partner).wait_recv()
        total[tile] = combine([chip_sum[tile]] + [inbox[tile, d] for d in range(CHIPS - 1)])

    @pl.loop(0, TILES)
    def _(step):
        d = near_first(step)
        tile = from_offset(d)

        for at, hops in ((1, 1), (2, 2), (4, 3), (6, 4)):

            @pl.when(step == at)
            def _():
                relay(hops)

        send(src, src_all.at[tile * 2 + 1 - core], (sa1, ra1), d, partner).wait_recv()
        rows = src_all[pl.ds(tile * 2, 2)].reshape(TILE, D)
        k_tile = nn(rows, wk[...]).astype(BF16)
        kt_scr[tile] = nt(wkt, rows).astype(BF16)
        v_scr[tile] = nn(rows, wv[...]).astype(BF16)
        vt_scr[tile] = nt(wvt, rows).astype(BF16)
        for head in range(HEADS):
            keys = jnp.where(own_lanes(TILE, head), k_tile[:, group_cols(head)], key_extra(tile, head).astype(BF16))
            kh[tile, head] = keys
            t = nt(qs[head], keys) * UNIT
            t_scr[tile, head] = t
            rm[head] = jnp.maximum(rm[head], jnp.maximum(t[:, :BLOCK], t[:, BLOCK:]))
            peak = t.max(axis=0, keepdims=True)
            total = jnp.exp2(t - peak).sum(axis=0, keepdims=True)
            lse = peak + jnp.log2(total)
            for kb in range(2):
                lc_part[tile, kb, head : head + 1, :] = lse[:, kb * BLOCK : (kb + 1) * BLOCK]
        swap_columns(tile, lc_part, lc_swap, (sl0, rl0)).start()

        @pl.when(step > 0)
        def _():
            before = from_offset(near_first(step - 1))
            spread_columns(before, log_sum, lc_part, lc_swap, lc_chip, lc_in, (sl0, rl0), (sl1, rl1))

    spread_columns(
        from_offset(4), log_sum, lc_part, lc_swap, lc_chip, lc_in, (sl0, rl0), (sl1, rl1)
    )

    for head in range(HEADS):
        peak = rm[head].max(axis=1, keepdims=True)
        rm[head] = jnp.zeros((ROWS, BLOCK), F32)

        @pl.loop(0, TILES)
        def _(tile):
            rm[head] += jnp.exp2(t_scr[tile, head, :, :BLOCK] - peak) + jnp.exp2(t_scr[tile, head, :, BLOCK:] - peak)

        total = rm[head].sum(axis=1, keepdims=True)
        row_term = peak + jnp.log2(total)
        lr[head] = jnp.broadcast_to(row_term, (ROWS, BLOCK))
        extra = query_extra(inter, head, in_three(row_term * (-1.0 / UNIT))).astype(BF16)
        part = qs[head]
        mask = own_lanes(ROWS, head)
        qb_scr[head] = jnp.where(mask, part, extra)
        qf[head] = jnp.where(mask, part + part, extra)

    att[...] = jnp.zeros_like(att)
    wvg[...] = jnp.zeros_like(wvg)

    @pl.loop(0, TILES)
    def _(tile):
        collect_columns(tile, log_sum, lc_chip, lc_in, lc_all, (sl1, rl1))
        rows = src_all[pl.ds(tile * 2, 2)].reshape(TILE, D)

        def make_match(head):
            lc_row = jnp.concatenate([lc_all[tile, kb, head : head + 1, :] for kb in range(2)], axis=1)
            match_scr[head] = jnp.exp2(nt(qf[head], kh[tile, head]) * UNIT - lc_row).astype(BF16)

        def use_match(head):
            match = match_scr[head]
            att[head] += nt(vt_scr[tile, head_lanes(head), :], match)
            gvt = nn(gat_scr[head_lanes(head), :], match)
            gvt_scr[tile, head_lanes(head), :] = gvt.astype(BF16)
            dots = (gvt * vt_scr[tile, head_lanes(head), :].astype(F32)).sum(axis=0, keepdims=True)
            for kb in range(2):
                cd_part[tile, kb, head : head + 1, :] = dots[:, kb * BLOCK : (kb + 1) * BLOCK]

        in_turn(make_match, use_match)
        swap_columns(tile, cd_part, cd_swap, (sc0, rc0)).start()
        wvg[...] += nn(gvt_scr[tile], rows)

        @pl.when(tile > 0)
        def _():
            spread_columns(tile - 1, plain_sum, cd_part, cd_swap, cd_chip, cd_in, (sc0, rc0), (sc1, rc1))

    spread_columns(TILES - 1, plain_sum, cd_part, cd_swap, cd_chip, cd_in, (sc0, rc0), (sc1, rc1))

    att_t = att[...].reshape(D, ROWS)
    att_rows = att_t.T
    for head in range(HEADS):
        rd = (att_rows[:, group_cols(head)] * gam[head].astype(F32)).sum(axis=1, keepdims=True)
        rd_scr[head] = jnp.broadcast_to(rd, (ROWS, BLOCK))
        gam[head] = gam[head] + gam[head]
    out[:ROWS] = (ref[...].astype(F32) + nn(att_rows.astype(BF16), wo[...])).astype(BF16)
    pack_weight(early_bufs[0], 1, nn(att_t.astype(BF16), gout[...]))
    pack_weight(early_bufs[0], 0, wvg[...].T)
    early = all_reduce(early_bufs, early_sems)
    early[0]()
    gq[...] = jnp.zeros_like(gq)
    wkg[...] = jnp.zeros_like(wkg)

    def source_copy(d):
        return send(gs_sum.at[to_offset(d)], gs_in.at[d - 1], (sg1, rg1), d, on_chip(d, core))

    def spread_source(tile):
        send(gs_part.at[tile, core], gs_swap.at[tile], (sg0, rg0), tile, partner).wait_recv()
        gs_sum[tile] = (gs_part[tile, core].astype(F32) + gs_swap[tile].astype(F32)).astype(BF16)
        d = lax.rem(tile + CHIPS - chip, CHIPS)

        @pl.when(d > 0)
        def _():
            source_copy(d).start()

    @pl.loop(0, TILES)
    def _(step):
        tile = by_quarters(step)
        for at, stage in ((1, 1), (5, 2)):

            @pl.when(step == at)
            def _():
                early[stage]()

        collect_columns(tile, plain_sum, cd_chip, cd_in, cd_all, (sc1, rc1))
        rows = src_all[pl.ds(tile * 2, 2)].reshape(TILE, D)
        gk_heads = []

        def make_grad(head):
            cols = group_cols(head)
            x = nt(qb_scr[head], kh[tile, head])
            gp = nt(gam[head], v_scr[tile, :, cols])
            lines = []
            for kb in range(2):
                lanes = slice(kb * BLOCK, (kb + 1) * BLOCK)
                lc_row = lc_all[tile, kb, head : head + 1, :]
                cd_row = cd_all[tile, kb, head : head + 1, :]
                u = x[:, lanes] * UNIT
                r = jnp.exp2(u)
                c = jnp.exp2(u + lr[head] - lc_row)
                lines.append((r * (c * gp[:, lanes] - rd_scr[head]) - c * cd_row).astype(BF16))
            match_scr[head] = jnp.concatenate(lines, axis=1)

        def use_grad(head):
            gs = match_scr[head]
            gq[head] += nt(kt_scr[tile, head_lanes(head), :], gs)
            gk_heads.append((nn(qt_all[head_lanes(head), :], gs) * SCALE).astype(BF16))
        in_turn(make_grad, use_grad)
        gkt = jnp.concatenate(gk_heads, axis=0)
        wkg[...] += nn(gkt, rows)
        gst = nn(wk[...], gkt) + nn(wv[...], gvt_scr[tile])
        for kb in range(2):
            gs_part[tile, kb] = gst[:, kb * BLOCK : (kb + 1) * BLOCK].astype(BF16)
        send(gs_part.at[tile, 1 - core], gs_swap.at[tile], (sg0, rg0), tile, partner).start()

        @pl.when(step > 0)
        def _():
            spread_source(by_quarters(step - 1))

    gq_t = (gq[...].reshape(D, ROWS) * SCALE).astype(BF16)
    pack_weight(late_bufs[0], 0, nn(gq_t, ref[...]).T)
    pack_weight(late_bufs[0], 1, wkg[...].T)
    late = all_reduce(late_bufs, late_sems)
    late[0]()
    early[3]()
    gref = (gout[...].astype(F32) + nt(gq_t.T, wq[...])).astype(BF16)
    late[1]()
    out[ROWS : 2 * ROWS] = gref
    spread_source(by_quarters(TILES - 1))
    early[4]()
    late[2]()
    for d in (4, 3, 5, 2, 6, 1, 7):
        source_copy(d).wait_recv()
    gsrc = gs_sum[chip].astype(F32)
    for d in range(CHIPS - 1):
        gsrc = gsrc + gs_in[d].astype(F32)
    out[2 * ROWS : 2 * ROWS + BLOCK] = gsrc.T.astype(BF16)
    early[5]()
    put_weights(out, early_bufs[-1], 1)
    late[3]()
    late[4]()
    late[5]()
    put_weights(out, late_bufs[-1], 0)

    early[6]()
    late[6]()
    for way in range(2):
        for hops in range(1, 5):
            for piece in pieces_of(way, hops):
                ring_copy(blk, way, hops, piece).wait_send()

    @pl.loop(0, TILES)
    def _(tile):
        send(src, src_all.at[blk], (sa1, ra1), tile, partner).wait_send()
        swap_columns(tile, lc_part, lc_swap, (sl0, rl0)).wait_send()
        swap_columns(tile, cd_part, cd_swap, (sc0, rc0)).wait_send()
        send(lc_in.at[tile], lc_in.at[tile], (sl1, rl1), tile, partner).wait_send()
        send(cd_in.at[tile], cd_in.at[tile], (sc1, rc1), tile, partner).wait_send()
        send(gs_part.at[tile, core], gs_swap.at[tile], (sg0, rg0), tile, partner).wait_send()

        @pl.when(tile > 0)
        def _():
            send(gs_sum.at[tile], gs_in.at[0], (sg1, rg1), tile, partner).wait_send()


def shape(dims, dtype):
    return jax.ShapeDtypeStruct(dims, dtype)


def layer(ref, gout, src, wq, wk, wv, wo, inter):
    vm = pltpu.VMEM
    row = (CHUNK, BLOCK)
    reduction = [
        vm((2, PLANE) + row, BF16), vm((PLANE,) + row, BF16), vm((PLANE,) + row, BF16), vm((PLANE - 1,) + row, BF16),
        vm(row, BF16), vm((CHIPS,) + row, BF16), vm(row, BF16), vm((2, PLANE) + row, BF16),
    ]
    heads = (HEADS, ROWS, BLOCK)
    turned = (HEADS, HEAD_DIM, ROWS)
    pair = (TILES, 2, HEADS, BLOCK)
    columns = [vm(pair, F32), vm(pair, F32), vm(pair, F32), vm((TILES, CHIPS - 1, 2, HEADS, BLOCK), F32), vm(pair, F32)]
    scratch = [
        vm((2 * CHIPS, BLOCK, D), BF16), vm((TILES, D, TILE), BF16), vm((TILES, HEADS, TILE, BLOCK), BF16),
        vm((TILES, TILE, D), BF16), vm((TILES, D, TILE), BF16), vm(heads, BF16), vm(heads, BF16), vm(heads, BF16),
        vm(heads, BF16), vm((D, ROWS), BF16), vm((D, ROWS), BF16), vm((TILES, HEADS, ROWS, TILE), F32), vm(heads, F32), vm(heads, F32),
        *columns, *columns,
        vm(turned, F32), vm((HEADS, ROWS, TILE), BF16), vm((TILES, D, TILE), BF16), vm(heads, F32), vm((D, D), F32), vm((D, D), F32), vm(turned, F32),
        vm((TILES, 2, D, BLOCK), BF16), vm((TILES, D, BLOCK), BF16), vm((TILES, D, BLOCK), BF16),
        vm((CHIPS - 1, D, BLOCK), BF16),
        *reduction, *reduction,
        DMA, DMA((16,)), DMA((16,)),
    ] + [DMA((n,)) for n in (8,) * 14 + 2 * (2, 2, 15, 15, 7, 7, 15, 15)]
    return pl.pallas_call(
        layer_kernel,
        out_shape=shape((OUT_ROWS, D), BF16),
        in_specs=[VMEM] * 7 + [SMEM],
        out_specs=VMEM,
        scratch_shapes=scratch,
        compiler_params=pltpu.CompilerParams(vmem_limit_bytes=60 << 20, collective_id=1, has_side_effects=True),
        name="layer",
    )(ref, gout, src, wq, wk, wv, wo, inter)


def finish_kernel(parts, matched_out, gref_out, gsrc_out, *weights):
    matched_out[...] = parts[:ROWS]
    gref_out[...] = parts[ROWS : 2 * ROWS]
    gsrc_out[...] = parts[2 * ROWS : 2 * ROWS + BLOCK]
    for at, out in enumerate(weights):
        first = 2 * ROWS + BLOCK + at * D
        out[...] = parts[first : first + D].astype(F32)


def finish(parts):
    return pl.pallas_call(
        finish_kernel,
        out_shape=[shape((ROWS, D), BF16)] * 2 + [shape((BLOCK, D), BF16)] + [shape((D, D), F32)] * 4,
        in_specs=[VMEM],
        out_specs=[VMEM] * 7,
        compiler_params=pltpu.CompilerParams(vmem_limit_bytes=32 << 20),
        name="finish",
    )(parts)


def on_device(ref_feats, src_feats, grad_out, w_query, w_key, w_value, w_out, intersection):
    parts = layer(ref_feats[0], grad_out[0], src_feats[0], w_query, w_key, w_value, w_out, intersection[0])
    matched, gref, gsrc, wqg, wkg, wvg, wog = finish(parts)
    return matched[None], gref[None], gsrc[None], wqg, wkg, wvg, wog


def solution(mesh):
    split = P("scan", "blk", None)
    return jax.shard_map(
        on_device, mesh=mesh,
        in_specs=(split, split, split, P(), P(), P(), P(), split),
        out_specs=(split, split, split, P(), P(), P(), P()),
        check_vma=False,
    )
```

```python
import functools
import math

import jax
import jax.numpy as jnp
from jax import lax
from jax.experimental import pallas as pl
from jax.experimental.pallas import tpu as pltpu
from jax.sharding import PartitionSpec as P

HEADS = 4
HEAD_DIM = 64
BLOCK = 128
D = 256
ROWS = 512
KEYS = 2048
TILE = 256
TILES = KEYS // TILE
QBLOCKS = ROWS // BLOCK
KBLOCKS = KEYS // BLOCK
CHIPS = 8
PLANE = 16
CHUNK = 32
PIECES = 4
OUT_ROWS = 2 * ROWS + BLOCK + 4 * D
NEG = -1.0e30
SCALE = HEAD_DIM**-0.5
UNIT = SCALE * math.log2(math.e)
F32 = jnp.float32
BF16 = jnp.bfloat16
MESH = pl.DeviceIdType.MESH
VMEM = pl.BlockSpec(memory_space=pltpu.VMEM)
HBM = pl.BlockSpec(memory_space=pltpu.HBM)
SMEM = pl.BlockSpec(memory_space=pltpu.SMEM)
DMA = pltpu.SemaphoreType.DMA


def nn(a, b):
    return jnp.dot(a, b, preferred_element_type=F32)


def nt(a, b):
    return lax.dot_general(a, b, (((1,), (1,)), ((), ())), preferred_element_type=F32)


def lanes_of(rows):
    return lax.broadcasted_iota(jnp.int32, (rows, BLOCK), 1)


def own_lanes(rows, head):
    lane = lanes_of(rows)
    return (lane < HEAD_DIM) if head % 2 == 0 else (lane >= HEAD_DIM)


def spare(head):
    return HEAD_DIM if head % 2 == 0 else 0


def group_cols(head):
    return slice((head // 2) * BLOCK, (head // 2 + 1) * BLOCK)


def head_lanes(head):
    return slice(head * HEAD_DIM, (head + 1) * HEAD_DIM)


def query_extra(inter, head, pieces):
    base = spare(head)
    lane = lanes_of(1)
    grid = []
    for qb in range(QBLOCKS):
        row = jnp.zeros((1, BLOCK), F32)
        for kb in range(KBLOCKS):
            bias = jnp.where(inter[qb, kb] == 1, 0.0, NEG).astype(F32)
            row = jnp.where(lane == base + kb, bias, row)
        grid.append(jnp.broadcast_to(row, (BLOCK, BLOCK)))
    extra = jnp.concatenate(grid, axis=0)
    if pieces is not None:
        lane = lanes_of(ROWS)
        for at, piece in enumerate(pieces):
            extra = jnp.where(lane == base + KBLOCKS + at, piece, extra)
    return extra


def key_extra(tile, head):
    base = spare(head)
    lane = lanes_of(TILE)
    row = lax.broadcasted_iota(jnp.int32, (TILE, BLOCK), 0)
    block = tile * 2 + jnp.where(row >= BLOCK, 1, 0)
    hot = (lane - base == block) | ((lane >= base + KBLOCKS) & (lane < base + KBLOCKS + 3))
    return jnp.where(hot, 1.0, 0.0)


def in_three(value):
    first = value.astype(BF16).astype(F32)
    second = (value - first).astype(BF16).astype(F32)
    third = (value - first - second).astype(BF16).astype(F32)
    return first, second, third


def log_sum(parts):
    peak = functools.reduce(jnp.maximum, parts)
    return peak + jnp.log2(sum(jnp.exp2(part - peak) for part in parts))


def plain_sum(parts):
    return sum(parts)


def pack_weight(wg, core, matrix):
    for half in range(2):
        for part in range(8):
            wg[core, 8 * half + part] = matrix[
                CHUNK * part : CHUNK * (part + 1), half * BLOCK : (half + 1) * BLOCK
            ].astype(BF16)


def put_weights(out, packed, pair):
    for core in range(2):
        first = 2 * ROWS + BLOCK + (2 * pair + core) * D
        for half in range(2):
            for part in range(8):
                out[first + CHUNK * part : first + CHUNK * (part + 1), half * BLOCK : (half + 1) * BLOCK] = packed[
                    core, 8 * half + part
                ]


def in_turn(make, use):
    make(0)
    for head in range(HEADS):
        if head + 1 < HEADS:
            make(head + 1)
        use(head)


def send(src, dst, sems, index, target):
    return pltpu.make_async_remote_copy(
        src_ref=src, dst_ref=dst, send_sem=sems[0].at[index], recv_sem=sems[1].at[index],
        device_id=target, device_id_type=MESH,
    )


def layer_kernel(
    ref, gout, src, wq, wk, wv, wo, inter,
    out_hbm,
    out, src_all, kt_scr, kh, v_scr, vt_scr, qs, qf, qb_scr, gam, gat_scr, qt_all, t_scr, rm, lr,
    lc_part, lc_swap, lc_chip, lc_in, lc_all, cd_part, cd_swap, cd_chip, cd_in, cd_all,
    att, match_scr, gvt_scr, rd_scr, wvg, wkg, gq,
    gs_part, gs_swap, gs_sum, gs_in, *rest,
):
    early_bufs, late_bufs, rest = rest[:8], rest[8:16], rest[16:]
    own_sem, sa0, ra0, sa1, ra1, sl0, rl0, sl1, rl1, sc0, rc0, sc1, rc1, sg0, rg0, sg1, rg1 = rest[:17]
    early_sems, late_sems, out_sems = rest[17:25], rest[25:33], rest[33]
    blk = lax.axis_index("blk")
    scan = lax.axis_index("scan")
    chip = lax.div(blk, 2)
    core = lax.rem(blk, 2)
    partner = {"blk": chip * 2 + 1 - core}

    def on_chip(offset, core_at):
        return {"blk": lax.rem(chip + offset, CHIPS) * 2 + core_at}

    def from_offset(d):
        return lax.rem(chip + CHIPS - d, CHIPS)

    def to_offset(d):
        return lax.rem(chip + d, CHIPS)

    def ring_copy(block, way, hops, piece, source=None):
        rows = pl.ds(piece * (BLOCK // PIECES), BLOCK // PIECES)
        landing = src_all.at[block, rows]
        return send(
            landing if source is None else source.at[rows], landing, (sa0, ra0),
            (way * 4 + hops - 1) * PIECES + piece, on_chip(1 if way == 0 else CHIPS - 1, core),
        )

    def pieces_of(way, hops):
        return range(PIECES) if hops < 4 else range(way * PIECES // 2, (way + 1) * PIECES // 2)

    def relay(hops):
        for piece in range(PIECES):
            for way in range(2):
                if piece not in pieces_of(way, hops):
                    continue
                origin = from_offset(hops if way == 0 else CHIPS - hops) * 2 + core
                ring_copy(origin, way, hops, piece).wait_recv()
                if hops < 4 and piece in pieces_of(way, hops + 1):
                    ring_copy(origin, way, hops + 1, piece).start()
        for d in (hops, CHIPS - hops) if hops < 4 else (hops,):
            origin = from_offset(d) * 2 + core
            send(src_all.at[origin], src_all.at[origin], (sa1, ra1), d, partner).start()

    plane = [{"scan": lax.rem(scan + d, PLANE)} for d in range(1, PLANE)]
    column = [on_chip(d, c) for d in range(1, CHIPS) for c in range(2)]
    barrier = pltpu.get_barrier_semaphore()
    everyone = [partner] + column + plane
    for target in everyone:
        pl.semaphore_signal(barrier, inc=1, device_id=target, device_id_type=MESH)

    def all_reduce(bufs, sems):
        wg, w_swap, w_sum, w_in, w_part, z_all, w_row, w_all = bufs
        swap_sems, in_sems, z_sems, out_sems = [sems[2 * i : 2 * i + 2] for i in range(4)]
        swap = [
            send(wg.at[1 - core], w_swap, swap_sems, 0, partner),
            send(w_all.at[core], w_all.at[core], swap_sems, 1, partner),
        ]

        def in_plane(d):
            return send(w_sum.at[lax.rem(scan + d, PLANE)], w_in.at[d - 1], in_sems, d - 1, plane[d - 1])

        def in_column(d):
            return send(w_part, z_all.at[chip], z_sems, d - 1, on_chip(d, core))

        def back_plane(d):
            return send(w_row, w_all.at[core, scan], out_sems, d - 1, plane[d - 1])

        def stage_1():
            swap[0].wait_recv()
            w_sum[...] = (wg[core].astype(F32) + w_swap[...].astype(F32)).astype(BF16)
            for d in range(1, PLANE):
                in_plane(d).start()

        def stage_2():
            for d in range(1, PLANE):
                in_plane(d).wait_recv()
            total = w_sum[scan].astype(F32)
            for d in range(PLANE - 1):
                total = total + w_in[d].astype(F32)
            part = total.astype(BF16)
            w_part[...] = part
            z_all[chip] = part
            for d in range(1, CHIPS):
                in_column(d).start()

        def stage_3():
            for d in range(1, CHIPS):
                in_column(d).wait_recv()
            total = z_all[0].astype(F32)
            for c in range(1, CHIPS):
                total = total + z_all[c].astype(F32)
            row = total.astype(BF16)
            w_row[...] = row
            w_all[core, scan] = row
            for d in range(1, PLANE):
                back_plane(d).start()

        def stage_4():
            for d in range(1, PLANE):
                back_plane(d).wait_recv()
            swap[1].start()

        def left():
            for copy in swap:
                copy.wait_send()
            for make, count in ((in_plane, PLANE), (in_column, CHIPS), (back_plane, PLANE)):
                for d in range(1, count):
                    make(d).wait_send()

        return swap[0].start, stage_1, stage_2, stage_3, stage_4, swap[1].wait_recv, left

    q_rows = nn(ref[...], wq[...]).astype(BF16)
    for head in range(HEADS):
        part = q_rows[:, group_cols(head)]
        extra = query_extra(inter, head, None).astype(BF16)
        qs[head] = jnp.where(own_lanes(ROWS, head), part, extra)
    qt_all[...] = q_rows.T
    rm[...] = jnp.full_like(rm, -3.0e38)
    own = pltpu.make_async_copy(src, src_all.at[blk], own_sem)
    own.start()

    pl.semaphore_wait(barrier, len(everyone))
    for piece in range(PIECES):
        for way in range(2):
            ring_copy(blk, way, 1, piece, src).start()
    send(src, src_all.at[blk], (sa1, ra1), 0, partner).start()

    ga_rows = nt(gout[...], wo[...]).astype(BF16)
    gat_scr[...] = nt(wo[...], gout[...]).astype(BF16)
    for head in range(HEADS):
        part = ga_rows[:, group_cols(head)]
        gam[head] = jnp.where(own_lanes(ROWS, head), part, jnp.zeros_like(part))
    wvt = wv[...].T
    wkt = wk[...].T
    own.wait()

    def near_first(step):
        half = lax.div(step + 1, 2)
        return jnp.where(lax.rem(step, 2) == 1, half, lax.rem(CHIPS - half, CHIPS))

    def by_quarters(step):
        return lax.div(step, 4) * 4 + lax.rem(chip + 1 + step, 4)

    def swap_columns(tile, part, swap, sems):
        return send(part.at[tile], swap.at[tile], sems, tile, partner)

    def spread_columns(tile, combine, part, swap, chip_sum, inbox, sems_swap, sems):
        swap_columns(tile, part, swap, sems_swap).wait_recv()
        chip_sum[tile] = combine([part[tile], swap[tile]])
        for d in range(1, CHIPS):
            for c in range(2):
                send(chip_sum.at[tile, core], inbox.at[tile, d - 1, core], sems, tile, on_chip(d, c)).start()

    def collect_columns(tile, combine, chip_sum, inbox, total, sems):
        send(inbox.at[tile], inbox.at[tile], sems, tile, partner).wait_recv()
        total[tile] = combine([chip_sum[tile]] + [inbox[tile, d] for d in range(CHIPS - 1)])

    @pl.loop(0, TILES)
    def _(step):
        d = near_first(step)
        tile = from_offset(d)

        for at, hops in ((1, 1), (2, 2), (4, 3), (6, 4)):

            @pl.when(step == at)
            def _():
                relay(hops)

        send(src, src_all.at[tile * 2 + 1 - core], (sa1, ra1), d, partner).wait_recv()
        rows = src_all[pl.ds(tile * 2, 2)].reshape(TILE, D)
        k_tile = nn(rows, wk[...]).astype(BF16)
        kt_scr[tile] = nt(wkt, rows).astype(BF16)
        v_scr[tile] = nn(rows, wv[...]).astype(BF16)
        vt_scr[tile] = nt(wvt, rows).astype(BF16)
        for head in range(HEADS):
            keys = jnp.where(own_lanes(TILE, head), k_tile[:, group_cols(head)], key_extra(tile, head).astype(BF16))
            kh[tile, head] = keys
            t = nt(qs[head], keys) * UNIT
            t_scr[tile, head] = t
            rm[head] = jnp.maximum(rm[head], jnp.maximum(t[:, :BLOCK], t[:, BLOCK:]))
            peak = t.max(axis=0, keepdims=True)
            total = jnp.exp2(t - peak).sum(axis=0, keepdims=True)
            lse = peak + jnp.log2(total)
            for kb in range(2):
                lc_part[tile, kb, head : head + 1, :] = lse[:, kb * BLOCK : (kb + 1) * BLOCK]
        swap_columns(tile, lc_part, lc_swap, (sl0, rl0)).start()

        @pl.when(step > 0)
        def _():
            before = from_offset(near_first(step - 1))
            spread_columns(before, log_sum, lc_part, lc_swap, lc_chip, lc_in, (sl0, rl0), (sl1, rl1))

    spread_columns(
        from_offset(4), log_sum, lc_part, lc_swap, lc_chip, lc_in, (sl0, rl0), (sl1, rl1)
    )

    for head in range(HEADS):
        peak = rm[head].max(axis=1, keepdims=True)
        rm[head] = jnp.zeros((ROWS, BLOCK), F32)

        @pl.loop(0, TILES)
        def _(tile):
            rm[head] += jnp.exp2(t_scr[tile, head, :, :BLOCK] - peak) + jnp.exp2(t_scr[tile, head, :, BLOCK:] - peak)

        total = rm[head].sum(axis=1, keepdims=True)
        row_term = peak + jnp.log2(total)
        lr[head] = jnp.broadcast_to(row_term, (ROWS, BLOCK))
        extra = query_extra(inter, head, in_three(row_term * (-1.0 / UNIT))).astype(BF16)
        part = qs[head]
        mask = own_lanes(ROWS, head)
        qb_scr[head] = jnp.where(mask, part, extra)
        qf[head] = jnp.where(mask, part + part, extra)

    att[...] = jnp.zeros_like(att)
    wvg[...] = jnp.zeros_like(wvg)

    @pl.loop(0, TILES)
    def _(tile):
        collect_columns(tile, log_sum, lc_chip, lc_in, lc_all, (sl1, rl1))
        rows = src_all[pl.ds(tile * 2, 2)].reshape(TILE, D)

        def make_match(head):
            lc_row = jnp.concatenate([lc_all[tile, kb, head : head + 1, :] for kb in range(2)], axis=1)
            match_scr[head] = jnp.exp2(nt(qf[head], kh[tile, head]) * UNIT - lc_row).astype(BF16)

        def use_match(head):
            match = match_scr[head]
            att[head] += nt(vt_scr[tile, head_lanes(head), :], match)
            gvt = nn(gat_scr[head_lanes(head), :], match)
            gvt_scr[tile, head_lanes(head), :] = gvt.astype(BF16)
            dots = (gvt * vt_scr[tile, head_lanes(head), :].astype(F32)).sum(axis=0, keepdims=True)
            for kb in range(2):
                cd_part[tile, kb, head : head + 1, :] = dots[:, kb * BLOCK : (kb + 1) * BLOCK]

        in_turn(make_match, use_match)
        swap_columns(tile, cd_part, cd_swap, (sc0, rc0)).start()
        wvg[...] += nn(gvt_scr[tile], rows)

        @pl.when(tile > 0)
        def _():
            spread_columns(tile - 1, plain_sum, cd_part, cd_swap, cd_chip, cd_in, (sc0, rc0), (sc1, rc1))

    spread_columns(TILES - 1, plain_sum, cd_part, cd_swap, cd_chip, cd_in, (sc0, rc0), (sc1, rc1))

    att_t = att[...].reshape(D, ROWS)
    att_rows = att_t.T
    for head in range(HEADS):
        rd = (att_rows[:, group_cols(head)] * gam[head].astype(F32)).sum(axis=1, keepdims=True)
        rd_scr[head] = jnp.broadcast_to(rd, (ROWS, BLOCK))
        gam[head] = gam[head] + gam[head]
    out[:ROWS] = (ref[...].astype(F32) + nn(att_rows.astype(BF16), wo[...])).astype(BF16)
    pack_weight(early_bufs[0], 1, nn(att_t.astype(BF16), gout[...]))
    pack_weight(early_bufs[0], 0, wvg[...].T)
    early = all_reduce(early_bufs, early_sems)
    early[0]()
    gq[...] = jnp.zeros_like(gq)
    wkg[...] = jnp.zeros_like(wkg)

    def source_copy(d):
        return send(gs_sum.at[to_offset(d)], gs_in.at[d - 1], (sg1, rg1), d, on_chip(d, core))

    def spread_source(tile):
        send(gs_part.at[tile, core], gs_swap.at[tile], (sg0, rg0), tile, partner).wait_recv()
        gs_sum[tile] = (gs_part[tile, core].astype(F32) + gs_swap[tile].astype(F32)).astype(BF16)
        d = lax.rem(tile + CHIPS - chip, CHIPS)

        @pl.when(d > 0)
        def _():
            source_copy(d).start()

    @pl.loop(0, TILES)
    def _(step):
        tile = by_quarters(step)
        for at, stage in ((1, 1), (5, 2)):

            @pl.when(step == at)
            def _():
                early[stage]()

        collect_columns(tile, plain_sum, cd_chip, cd_in, cd_all, (sc1, rc1))
        rows = src_all[pl.ds(tile * 2, 2)].reshape(TILE, D)
        gk_heads = []

        def make_grad(head):
            cols = group_cols(head)
            x = nt(qb_scr[head], kh[tile, head])
            gp = nt(gam[head], v_scr[tile, :, cols])
            lines = []
            for kb in range(2):
                lanes = slice(kb * BLOCK, (kb + 1) * BLOCK)
                lc_row = lc_all[tile, kb, head : head + 1, :]
                cd_row = cd_all[tile, kb, head : head + 1, :]
                u = x[:, lanes] * UNIT
                r = jnp.exp2(u)
                c = jnp.exp2(u + lr[head] - lc_row)
                lines.append((r * (c * gp[:, lanes] - rd_scr[head]) - c * cd_row).astype(BF16))
            match_scr[head] = jnp.concatenate(lines, axis=1)

        def use_grad(head):
            gs = match_scr[head]
            gq[head] += nt(kt_scr[tile, head_lanes(head), :], gs)
            gk_heads.append((nn(qt_all[head_lanes(head), :], gs) * SCALE).astype(BF16))
        in_turn(make_grad, use_grad)
        gkt = jnp.concatenate(gk_heads, axis=0)
        wkg[...] += nn(gkt, rows)
        gst = nn(wk[...], gkt) + nn(wv[...], gvt_scr[tile])
        for kb in range(2):
            gs_part[tile, kb] = gst[:, kb * BLOCK : (kb + 1) * BLOCK].astype(BF16)
        send(gs_part.at[tile, 1 - core], gs_swap.at[tile], (sg0, rg0), tile, partner).start()

        @pl.when(step > 0)
        def _():
            spread_source(by_quarters(step - 1))

    gq_t = (gq[...].reshape(D, ROWS) * SCALE).astype(BF16)
    pack_weight(late_bufs[0], 0, nn(gq_t, ref[...]).T)
    pack_weight(late_bufs[0], 1, wkg[...].T)
    late = all_reduce(late_bufs, late_sems)

    def leave(at, first, count):
        rows = pl.ds(first, count)
        return pltpu.make_async_copy(out.at[rows], out_hbm.at[rows], out_sems.at[at])

    late[0]()
    early[3]()
    gref = (gout[...].astype(F32) + nt(gq_t.T, wq[...])).astype(BF16)
    late[1]()
    out[ROWS : 2 * ROWS] = gref
    spread_source(by_quarters(TILES - 1))
    early[4]()
    late[2]()
    for d in (4, 3, 5, 2, 6, 1, 7):
        source_copy(d).wait_recv()
    gsrc = gs_sum[chip].astype(F32)
    for d in range(CHIPS - 1):
        gsrc = gsrc + gs_in[d].astype(F32)
    out[2 * ROWS : 2 * ROWS + BLOCK] = gsrc.T.astype(BF16)
    leave(0, 0, 2 * ROWS + BLOCK).start()
    early[5]()
    put_weights(out, early_bufs[-1], 1)
    leave(1, OUT_ROWS - 2 * D, 2 * D).start()
    late[3]()

    early[6]()
    for way in range(2):
        for hops in range(1, 5):
            for piece in pieces_of(way, hops):
                ring_copy(blk, way, hops, piece).wait_send()

    @pl.loop(0, TILES)
    def _(tile):
        send(src, src_all.at[blk], (sa1, ra1), tile, partner).wait_send()
        swap_columns(tile, lc_part, lc_swap, (sl0, rl0)).wait_send()
        swap_columns(tile, cd_part, cd_swap, (sc0, rc0)).wait_send()
        send(lc_in.at[tile], lc_in.at[tile], (sl1, rl1), tile, partner).wait_send()
        send(cd_in.at[tile], cd_in.at[tile], (sc1, rc1), tile, partner).wait_send()
        send(gs_part.at[tile, core], gs_swap.at[tile], (sg0, rg0), tile, partner).wait_send()

        @pl.when(tile > 0)
        def _():
            send(gs_sum.at[tile], gs_in.at[0], (sg1, rg1), tile, partner).wait_send()

    late[4]()
    late[5]()
    put_weights(out, late_bufs[-1], 0)
    leave(2, 2 * ROWS + BLOCK, 2 * D).start()
    leave(2, 2 * ROWS + BLOCK, 2 * D).wait()
    leave(1, OUT_ROWS - 2 * D, 2 * D).wait()
    leave(0, 0, 2 * ROWS + BLOCK).wait()

    late[6]()


def shape(dims, dtype):
    return jax.ShapeDtypeStruct(dims, dtype)


def layer(ref, gout, src, wq, wk, wv, wo, inter):
    vm = pltpu.VMEM
    row = (CHUNK, BLOCK)
    reduction = [
        vm((2, PLANE) + row, BF16), vm((PLANE,) + row, BF16), vm((PLANE,) + row, BF16), vm((PLANE - 1,) + row, BF16),
        vm(row, BF16), vm((CHIPS,) + row, BF16), vm(row, BF16), vm((2, PLANE) + row, BF16),
    ]
    heads = (HEADS, ROWS, BLOCK)
    turned = (HEADS, HEAD_DIM, ROWS)
    pair = (TILES, 2, HEADS, BLOCK)
    columns = [vm(pair, F32), vm(pair, F32), vm(pair, F32), vm((TILES, CHIPS - 1, 2, HEADS, BLOCK), F32), vm(pair, F32)]
    scratch = [
        vm((OUT_ROWS, D), BF16),
        vm((2 * CHIPS, BLOCK, D), BF16), vm((TILES, D, TILE), BF16), vm((TILES, HEADS, TILE, BLOCK), BF16),
        vm((TILES, TILE, D), BF16), vm((TILES, D, TILE), BF16), vm(heads, BF16), vm(heads, BF16), vm(heads, BF16),
        vm(heads, BF16), vm((D, ROWS), BF16), vm((D, ROWS), BF16), vm((TILES, HEADS, ROWS, TILE), F32), vm(heads, F32), vm(heads, F32),
        *columns, *columns,
        vm(turned, F32), vm((HEADS, ROWS, TILE), BF16), vm((TILES, D, TILE), BF16), vm(heads, F32), vm((D, D), F32), vm((D, D), F32), vm(turned, F32),
        vm((TILES, 2, D, BLOCK), BF16), vm((TILES, D, BLOCK), BF16), vm((TILES, D, BLOCK), BF16),
        vm((CHIPS - 1, D, BLOCK), BF16),
        *reduction, *reduction,
        DMA, DMA((8 * PIECES,)), DMA((8 * PIECES,)),
    ] + [DMA((n,)) for n in (8,) * 14 + 2 * (2, 2, 15, 15, 7, 7, 15, 15) + (3,)]
    return pl.pallas_call(
        layer_kernel,
        out_shape=shape((OUT_ROWS, D), BF16),
        in_specs=[VMEM] * 7 + [SMEM],
        out_specs=HBM,
        scratch_shapes=scratch,
        compiler_params=pltpu.CompilerParams(vmem_limit_bytes=60 << 20, collective_id=1, has_side_effects=True),
        name="layer",
    )(ref, gout, src, wq, wk, wv, wo, inter)


def finish_kernel(parts, matched_out, gref_out, gsrc_out, *rest):
    weights, (rows, packed, wide, in_sems, out_sems) = rest[:4], rest[4:]
    first = 2 * ROWS + BLOCK
    load_weights = pltpu.make_async_copy(parts.at[pl.ds(first, 4 * D)], packed, in_sems.at[0])
    load_rows = pltpu.make_async_copy(parts.at[pl.ds(0, first)], rows, in_sems.at[1])
    load_weights.start()
    load_rows.start()
    stores = []
    load_weights.wait()
    for at, out in enumerate(weights):
        wide[at] = packed[at * D : (at + 1) * D].astype(F32)
        stores.append(pltpu.make_async_copy(wide.at[at], out, out_sems.at[at]))
        stores[-1].start()
    load_rows.wait()
    for at, (out, begin, count) in enumerate(
        ((matched_out, 0, ROWS), (gref_out, ROWS, ROWS), (gsrc_out, 2 * ROWS, BLOCK))
    ):
        stores.append(pltpu.make_async_copy(rows.at[pl.ds(begin, count)], out, out_sems.at[4 + at]))
        stores[-1].start()
    for store in stores:
        store.wait()


def finish(parts):
    return pl.pallas_call(
        finish_kernel,
        out_shape=[shape((ROWS, D), BF16)] * 2 + [shape((BLOCK, D), BF16)] + [shape((D, D), F32)] * 4,
        in_specs=[HBM],
        out_specs=[HBM] * 7,
        scratch_shapes=[
            pltpu.VMEM((2 * ROWS + BLOCK, D), BF16), pltpu.VMEM((4 * D, D), BF16), pltpu.VMEM((4, D, D), F32),
            DMA((2,)), DMA((7,)),
        ],
        compiler_params=pltpu.CompilerParams(vmem_limit_bytes=60 << 20),
        name="finish",
    )(parts)


def on_device(ref_feats, src_feats, grad_out, w_query, w_key, w_value, w_out, intersection):
    parts = layer(ref_feats[0], grad_out[0], src_feats[0], w_query, w_key, w_value, w_out, intersection[0])
    matched, gref, gsrc, wqg, wkg, wvg, wog = finish(parts)
    return matched[None], gref[None], gsrc[None], wqg, wkg, wvg, wog


def solution(mesh):
    split = P("scan", "blk", None)
    return jax.shard_map(
        on_device, mesh=mesh,
        in_specs=(split, split, split, P(), P(), P(), P(), split),
        out_specs=(split, split, split, P(), P(), P(), P()),
        check_vma=False,
    )
```

```python
import functools
import math

import jax
import jax.numpy as jnp
from jax import lax
from jax.experimental import pallas as pl
from jax.experimental.pallas import tpu as pltpu
from jax.sharding import PartitionSpec as P

HEADS = 4
HEAD_DIM = 64
BLOCK = 128
D = 256
ROWS = 512
KEYS = 2048
TILE = 256
TILES = KEYS // TILE
QBLOCKS = ROWS // BLOCK
KBLOCKS = KEYS // BLOCK
CHIPS = 8
PLANE = 16
CHUNK = 32
PIECES = 4
OUT_ROWS = 2 * ROWS + BLOCK + 4 * D
NEG = -1.0e30
SCALE = HEAD_DIM**-0.5
UNIT = SCALE * math.log2(math.e)
F32 = jnp.float32
BF16 = jnp.bfloat16
MESH = pl.DeviceIdType.MESH
VMEM = pl.BlockSpec(memory_space=pltpu.VMEM)
HBM = pl.BlockSpec(memory_space=pltpu.HBM)
SMEM = pl.BlockSpec(memory_space=pltpu.SMEM)
DMA = pltpu.SemaphoreType.DMA


def nn(a, b):
    return jnp.dot(a, b, preferred_element_type=F32)


def nt(a, b):
    return lax.dot_general(a, b, (((1,), (1,)), ((), ())), preferred_element_type=F32)


def lanes_of(rows):
    return lax.broadcasted_iota(jnp.int32, (rows, BLOCK), 1)


def own_lanes(rows, head):
    lane = lanes_of(rows)
    return (lane < HEAD_DIM) if head % 2 == 0 else (lane >= HEAD_DIM)


def spare(head):
    return HEAD_DIM if head % 2 == 0 else 0


def group_cols(head):
    return slice((head // 2) * BLOCK, (head // 2 + 1) * BLOCK)


def head_lanes(head):
    return slice(head * HEAD_DIM, (head + 1) * HEAD_DIM)


def query_extra(inter, head, pieces):
    base = spare(head)
    lane = lanes_of(1)
    grid = []
    for qb in range(QBLOCKS):
        row = jnp.zeros((1, BLOCK), F32)
        for kb in range(KBLOCKS):
            bias = jnp.where(inter[qb, kb] == 1, 0.0, NEG).astype(F32)
            row = jnp.where(lane == base + kb, bias, row)
        grid.append(jnp.broadcast_to(row, (BLOCK, BLOCK)))
    extra = jnp.concatenate(grid, axis=0)
    if pieces is not None:
        lane = lanes_of(ROWS)
        for at, piece in enumerate(pieces):
            extra = jnp.where(lane == base + KBLOCKS + at, piece, extra)
    return extra


def key_extra(tile, head):
    base = spare(head)
    lane = lanes_of(TILE)
    row = lax.broadcasted_iota(jnp.int32, (TILE, BLOCK), 0)
    block = tile * 2 + jnp.where(row >= BLOCK, 1, 0)
    hot = (lane - base == block) | ((lane >= base + KBLOCKS) & (lane < base + KBLOCKS + 3))
    return jnp.where(hot, 1.0, 0.0)


def in_three(value):
    first = value.astype(BF16).astype(F32)
    second = (value - first).astype(BF16).astype(F32)
    third = (value - first - second).astype(BF16).astype(F32)
    return first, second, third


def log_sum(parts):
    peak = functools.reduce(jnp.maximum, parts)
    return peak + jnp.log2(sum(jnp.exp2(part - peak) for part in parts))


def plain_sum(parts):
    return sum(parts)


def pack_weight(wg, core, matrix):
    for half in range(2):
        for part in range(8):
            wg[core, 8 * half + part] = matrix[
                CHUNK * part : CHUNK * (part + 1), half * BLOCK : (half + 1) * BLOCK
            ].astype(BF16)


def put_weights(out, packed, pair):
    for core in range(2):
        first = 2 * ROWS + BLOCK + (2 * pair + core) * D
        for half in range(2):
            for part in range(8):
                out[first + CHUNK * part : first + CHUNK * (part + 1), half * BLOCK : (half + 1) * BLOCK] = packed[
                    core, 8 * half + part
                ]


def in_turn(make, use):
    make(0)
    for head in range(HEADS):
        if head + 1 < HEADS:
            make(head + 1)
        use(head)


def send(src, dst, sems, index, target):
    return pltpu.make_async_remote_copy(
        src_ref=src, dst_ref=dst, send_sem=sems[0].at[index], recv_sem=sems[1].at[index],
        device_id=target, device_id_type=MESH,
    )


def layer_kernel(
    ref, gout, src, wq, wk, wv, wo, inter,
    out_hbm,
    out, src_all, kt_scr, kh, v_scr, vt_scr, qs, qf, qb_scr, gam, gat_scr, qt_all, t_scr, rm, lr,
    lc_part, lc_swap, lc_chip, lc_in, lc_all, cd_part, cd_swap, cd_chip, cd_in, cd_all,
    att, match_scr, gvt_scr, rd_scr, wvg, wkg, gq,
    gs_part, gs_swap, gs_sum, gs_in, *rest,
):
    early_bufs, late_bufs, rest = rest[:8], rest[8:16], rest[16:]
    own_sem, sa0, ra0, sa1, ra1, sl0, rl0, sl1, rl1, sc0, rc0, sc1, rc1, sg0, rg0, sg1, rg1 = rest[:17]
    early_sems, late_sems, out_sems, known = rest[17:25], rest[25:33], rest[33], rest[34]
    blk = lax.axis_index("blk")
    scan = lax.axis_index("scan")
    chip = lax.div(blk, 2)
    core = lax.rem(blk, 2)
    partner = {"blk": chip * 2 + 1 - core}

    def on_chip(offset, core_at):
        return {"blk": lax.rem(chip + offset, CHIPS) * 2 + core_at}

    def from_offset(d):
        return lax.rem(chip + CHIPS - d, CHIPS)

    def to_offset(d):
        return lax.rem(chip + d, CHIPS)

    def ring_copy(block, way, hops, piece, source=None):
        rows = pl.ds(piece * (BLOCK // PIECES), BLOCK // PIECES)
        landing = src_all.at[block, rows]
        return send(
            landing if source is None else source.at[rows], landing, (sa0, ra0),
            (way * 4 + hops - 1) * PIECES + piece, on_chip(1 if way == 0 else CHIPS - 1, core),
        )

    def pieces_of(way, hops):
        return range(PIECES) if hops < 4 else range(way * PIECES // 2, (way + 1) * PIECES // 2)

    def relay(hops):
        for piece in range(PIECES):
            for way in range(2):
                if piece not in pieces_of(way, hops):
                    continue
                origin = from_offset(hops if way == 0 else CHIPS - hops) * 2 + core
                ring_copy(origin, way, hops, piece).wait_recv()
                if hops < 4 and piece in pieces_of(way, hops + 1):
                    ring_copy(origin, way, hops + 1, piece).start()
        for d in (hops, CHIPS - hops) if hops < 4 else (hops,):
            origin = from_offset(d) * 2 + core
            send(src_all.at[origin], src_all.at[origin], (sa1, ra1), d, partner).start()

    plane = [{"scan": lax.rem(scan + d, PLANE)} for d in range(1, PLANE)]
    barrier = pltpu.get_barrier_semaphore()
    row_at, col_at = lax.div(scan, 4), lax.rem(scan, 4)
    beside_z = [on_chip(1, core), on_chip(CHIPS - 1, core)]
    beside_x = [{"scan": row_at * 4 + lax.rem(col_at + d, 4)} for d in (1, 3)]
    beside_y = [{"scan": lax.rem(row_at + d, 4) * 4 + col_at} for d in (1, 3)]
    everyone = [partner] + beside_z + beside_x + beside_y

    def tell(at, targets):
        for target in targets:
            pl.semaphore_signal(known.at[at], inc=1, device_id=target, device_id_type=MESH)

    def hear(at):
        pl.semaphore_wait(known.at[at], 2)

    for target in everyone:
        pl.semaphore_signal(barrier, inc=1, device_id=target, device_id_type=MESH)

    def all_reduce(bufs, sems):
        wg, w_swap, w_sum, w_in, w_part, z_all, w_row, w_all = bufs
        swap_sems, in_sems, z_sems, out_sems = [sems[2 * i : 2 * i + 2] for i in range(4)]
        swap = [
            send(wg.at[1 - core], w_swap, swap_sems, 0, partner),
            send(w_all.at[core], w_all.at[core], swap_sems, 1, partner),
        ]

        def in_plane(d):
            return send(w_sum.at[lax.rem(scan + d, PLANE)], w_in.at[d - 1], in_sems, d - 1, plane[d - 1])

        def in_column(d):
            return send(w_part, z_all.at[chip], z_sems, d - 1, on_chip(d, core))

        def back_plane(d):
            return send(w_row, w_all.at[core, scan], out_sems, d - 1, plane[d - 1])

        def stage_1():
            swap[0].wait_recv()
            w_sum[...] = (wg[core].astype(F32) + w_swap[...].astype(F32)).astype(BF16)
            for d in range(1, PLANE):
                in_plane(d).start()

        def stage_2():
            for d in range(1, PLANE):
                in_plane(d).wait_recv()
            total = w_sum[scan].astype(F32)
            for d in range(PLANE - 1):
                total = total + w_in[d].astype(F32)
            part = total.astype(BF16)
            w_part[...] = part
            z_all[chip] = part
            for d in range(1, CHIPS):
                in_column(d).start()

        def stage_3():
            for d in range(1, CHIPS):
                in_column(d).wait_recv()
            total = z_all[0].astype(F32)
            for c in range(1, CHIPS):
                total = total + z_all[c].astype(F32)
            row = total.astype(BF16)
            w_row[...] = row
            w_all[core, scan] = row
            for d in range(1, PLANE):
                back_plane(d).start()

        def stage_4():
            for d in range(1, PLANE):
                back_plane(d).wait_recv()
            swap[1].start()

        def left():
            for copy in swap:
                copy.wait_send()
            for make, count in ((in_plane, PLANE), (in_column, CHIPS), (back_plane, PLANE)):
                for d in range(1, count):
                    make(d).wait_send()

        return swap[0].start, stage_1, stage_2, stage_3, stage_4, swap[1].wait_recv, left

    q_rows = nn(ref[...], wq[...]).astype(BF16)
    for head in range(HEADS):
        part = q_rows[:, group_cols(head)]
        extra = query_extra(inter, head, None).astype(BF16)
        qs[head] = jnp.where(own_lanes(ROWS, head), part, extra)
    qt_all[...] = q_rows.T
    rm[...] = jnp.full_like(rm, -3.0e38)
    own = pltpu.make_async_copy(src, src_all.at[blk], own_sem)
    own.start()

    pl.semaphore_wait(barrier, len(everyone))
    for piece in range(PIECES):
        for way in range(2):
            ring_copy(blk, way, 1, piece, src).start()
    send(src, src_all.at[blk], (sa1, ra1), 0, partner).start()
    tell(0, beside_z)
    tell(4, beside_x)

    ga_rows = nt(gout[...], wo[...]).astype(BF16)
    gat_scr[...] = nt(wo[...], gout[...]).astype(BF16)
    for head in range(HEADS):
        part = ga_rows[:, group_cols(head)]
        gam[head] = jnp.where(own_lanes(ROWS, head), part, jnp.zeros_like(part))
    wvt = wv[...].T
    wkt = wk[...].T
    own.wait()
    hear(0)
    tell(1, beside_z)

    def near_first(step):
        half = lax.div(step + 1, 2)
        return jnp.where(lax.rem(step, 2) == 1, half, lax.rem(CHIPS - half, CHIPS))

    def by_quarters(step):
        return lax.div(step, 4) * 4 + lax.rem(chip + 1 + step, 4)

    def swap_columns(tile, part, swap, sems):
        return send(part.at[tile], swap.at[tile], sems, tile, partner)

    def spread_columns(tile, combine, part, swap, chip_sum, inbox, sems_swap, sems):
        swap_columns(tile, part, swap, sems_swap).wait_recv()
        chip_sum[tile] = combine([part[tile], swap[tile]])
        for d in range(1, CHIPS):
            for c in range(2):
                send(chip_sum.at[tile, core], inbox.at[tile, d - 1, core], sems, tile, on_chip(d, c)).start()

    def collect_columns(tile, combine, chip_sum, inbox, total, sems):
        send(inbox.at[tile], inbox.at[tile], sems, tile, partner).wait_recv()
        total[tile] = combine([chip_sum[tile]] + [inbox[tile, d] for d in range(CHIPS - 1)])

    @pl.loop(0, TILES)
    def _(step):
        d = near_first(step)
        tile = from_offset(d)

        @pl.when(step == 1)
        def _():
            hear(2)
            tell(3, beside_z)

        @pl.when(step == 2)
        def _():
            hear(4)
            tell(5, beside_y)

        @pl.when(step == 4)
        def _():
            hear(5)
            tell(6, beside_y)

        @pl.when(step == 6)
        def _():
            hear(6)

        for at, hops in ((1, 1), (2, 2), (4, 3), (6, 4)):

            @pl.when(step == at)
            def _():
                relay(hops)

        send(src, src_all.at[tile * 2 + 1 - core], (sa1, ra1), d, partner).wait_recv()
        rows = src_all[pl.ds(tile * 2, 2)].reshape(TILE, D)
        k_tile = nn(rows, wk[...]).astype(BF16)
        kt_scr[tile] = nt(wkt, rows).astype(BF16)
        v_scr[tile] = nn(rows, wv[...]).astype(BF16)
        vt_scr[tile] = nt(wvt, rows).astype(BF16)
        for head in range(HEADS):
            keys = jnp.where(own_lanes(TILE, head), k_tile[:, group_cols(head)], key_extra(tile, head).astype(BF16))
            kh[tile, head] = keys
            t = nt(qs[head], keys) * UNIT
            t_scr[tile, head] = t
            rm[head] = jnp.maximum(rm[head], jnp.maximum(t[:, :BLOCK], t[:, BLOCK:]))
            peak = t.max(axis=0, keepdims=True)
            total = jnp.exp2(t - peak).sum(axis=0, keepdims=True)
            lse = peak + jnp.log2(total)
            for kb in range(2):
                lc_part[tile, kb, head : head + 1, :] = lse[:, kb * BLOCK : (kb + 1) * BLOCK]
        swap_columns(tile, lc_part, lc_swap, (sl0, rl0)).start()

        @pl.when(step == 0)
        def _():
            hear(1)
            tell(2, beside_z)

        @pl.when(step == 1)
        def _():
            hear(3)

        @pl.when(step > 0)
        def _():
            before = from_offset(near_first(step - 1))
            spread_columns(before, log_sum, lc_part, lc_swap, lc_chip, lc_in, (sl0, rl0), (sl1, rl1))

    spread_columns(
        from_offset(4), log_sum, lc_part, lc_swap, lc_chip, lc_in, (sl0, rl0), (sl1, rl1)
    )

    for head in range(HEADS):
        peak = rm[head].max(axis=1, keepdims=True)
        rm[head] = jnp.zeros((ROWS, BLOCK), F32)

        @pl.loop(0, TILES)
        def _(tile):
            rm[head] += jnp.exp2(t_scr[tile, head, :, :BLOCK] - peak) + jnp.exp2(t_scr[tile, head, :, BLOCK:] - peak)

        total = rm[head].sum(axis=1, keepdims=True)
        row_term = peak + jnp.log2(total)
        lr[head] = jnp.broadcast_to(row_term, (ROWS, BLOCK))
        extra = query_extra(inter, head, in_three(row_term * (-1.0 / UNIT))).astype(BF16)
        part = qs[head]
        mask = own_lanes(ROWS, head)
        qb_scr[head] = jnp.where(mask, part, extra)
        qf[head] = jnp.where(mask, part + part, extra)

    att[...] = jnp.zeros_like(att)
    wvg[...] = jnp.zeros_like(wvg)

    @pl.loop(0, TILES)
    def _(tile):
        collect_columns(tile, log_sum, lc_chip, lc_in, lc_all, (sl1, rl1))
        rows = src_all[pl.ds(tile * 2, 2)].reshape(TILE, D)

        def make_match(head):
            lc_row = jnp.concatenate([lc_all[tile, kb, head : head + 1, :] for kb in range(2)], axis=1)
            match_scr[head] = jnp.exp2(nt(qf[head], kh[tile, head]) * UNIT - lc_row).astype(BF16)

        def use_match(head):
            match = match_scr[head]
            att[head] += nt(vt_scr[tile, head_lanes(head), :], match)
            gvt = nn(gat_scr[head_lanes(head), :], match)
            gvt_scr[tile, head_lanes(head), :] = gvt.astype(BF16)
            dots = (gvt * vt_scr[tile, head_lanes(head), :].astype(F32)).sum(axis=0, keepdims=True)
            for kb in range(2):
                cd_part[tile, kb, head : head + 1, :] = dots[:, kb * BLOCK : (kb + 1) * BLOCK]

        in_turn(make_match, use_match)
        swap_columns(tile, cd_part, cd_swap, (sc0, rc0)).start()
        wvg[...] += nn(gvt_scr[tile], rows)

        @pl.when(tile > 0)
        def _():
            spread_columns(tile - 1, plain_sum, cd_part, cd_swap, cd_chip, cd_in, (sc0, rc0), (sc1, rc1))

    spread_columns(TILES - 1, plain_sum, cd_part, cd_swap, cd_chip, cd_in, (sc0, rc0), (sc1, rc1))

    att_t = att[...].reshape(D, ROWS)
    att_rows = att_t.T
    for head in range(HEADS):
        rd = (att_rows[:, group_cols(head)] * gam[head].astype(F32)).sum(axis=1, keepdims=True)
        rd_scr[head] = jnp.broadcast_to(rd, (ROWS, BLOCK))
        gam[head] = gam[head] + gam[head]
    out[:ROWS] = (ref[...].astype(F32) + nn(att_rows.astype(BF16), wo[...])).astype(BF16)
    pack_weight(early_bufs[0], 1, nn(att_t.astype(BF16), gout[...]))
    pack_weight(early_bufs[0], 0, wvg[...].T)
    early = all_reduce(early_bufs, early_sems)
    early[0]()
    gq[...] = jnp.zeros_like(gq)
    wkg[...] = jnp.zeros_like(wkg)

    def source_copy(d):
        return send(gs_sum.at[to_offset(d)], gs_in.at[d - 1], (sg1, rg1), d, on_chip(d, core))

    def spread_source(tile):
        send(gs_part.at[tile, core], gs_swap.at[tile], (sg0, rg0), tile, partner).wait_recv()
        gs_sum[tile] = (gs_part[tile, core].astype(F32) + gs_swap[tile].astype(F32)).astype(BF16)
        d = lax.rem(tile + CHIPS - chip, CHIPS)

        @pl.when(d > 0)
        def _():
            source_copy(d).start()

    @pl.loop(0, TILES)
    def _(step):
        tile = by_quarters(step)
        for at, stage in ((1, 1), (5, 2)):

            @pl.when(step == at)
            def _():
                early[stage]()

        collect_columns(tile, plain_sum, cd_chip, cd_in, cd_all, (sc1, rc1))
        rows = src_all[pl.ds(tile * 2, 2)].reshape(TILE, D)
        gk_heads = []

        def make_grad(head):
            cols = group_cols(head)
            for half in range(2):
                rows = slice(half * TILE, (half + 1) * TILE)
                x = nt(qb_scr[head, rows], kh[tile, head])
                gp = nt(gam[head, rows], v_scr[tile, :, cols])
                lines = []
                for kb in range(2):
                    lanes = slice(kb * BLOCK, (kb + 1) * BLOCK)
                    lc_row = lc_all[tile, kb, head : head + 1, :]
                    cd_row = cd_all[tile, kb, head : head + 1, :]
                    u = x[:, lanes] * UNIT
                    r = jnp.exp2(u)
                    c = jnp.exp2(u + lr[head, rows] - lc_row)
                    lines.append((r * (c * gp[:, lanes] - rd_scr[head, rows]) - c * cd_row).astype(BF16))
                match_scr[head, rows] = jnp.concatenate(lines, axis=1)

        def use_grad(head):
            gs = match_scr[head]
            gq[head] += nt(kt_scr[tile, head_lanes(head), :], gs)
            gk_heads.append((nn(qt_all[head_lanes(head), :], gs) * SCALE).astype(BF16))
        in_turn(make_grad, use_grad)
        gkt = jnp.concatenate(gk_heads, axis=0)
        wkg[...] += nn(gkt, rows)
        gst = nn(wk[...], gkt) + nn(wv[...], gvt_scr[tile])
        for kb in range(2):
            gs_part[tile, kb] = gst[:, kb * BLOCK : (kb + 1) * BLOCK].astype(BF16)
        send(gs_part.at[tile, 1 - core], gs_swap.at[tile], (sg0, rg0), tile, partner).start()

        @pl.when(step > 0)
        def _():
            spread_source(by_quarters(step - 1))

    gq_t = (gq[...].reshape(D, ROWS) * SCALE).astype(BF16)
    pack_weight(late_bufs[0], 0, nn(gq_t, ref[...]).T)
    pack_weight(late_bufs[0], 1, wkg[...].T)
    late = all_reduce(late_bufs, late_sems)

    def leave(at, first, count):
        rows = pl.ds(first, count)
        return pltpu.make_async_copy(out.at[rows], out_hbm.at[rows], out_sems.at[at])

    late[0]()
    early[3]()
    gref = (gout[...].astype(F32) + nt(gq_t.T, wq[...])).astype(BF16)
    late[1]()
    out[ROWS : 2 * ROWS] = gref
    spread_source(by_quarters(TILES - 1))
    early[4]()
    late[2]()
    for d in (4, 3, 5, 2, 6, 1, 7):
        source_copy(d).wait_recv()
    gsrc = gs_sum[chip].astype(F32)
    for d in range(CHIPS - 1):
        gsrc = gsrc + gs_in[d].astype(F32)
    out[2 * ROWS : 2 * ROWS + BLOCK] = gsrc.T.astype(BF16)
    leave(0, 0, 2 * ROWS + BLOCK).start()
    early[5]()
    put_weights(out, early_bufs[-1], 1)
    leave(1, OUT_ROWS - 2 * D, 2 * D).start()
    late[3]()

    early[6]()
    for way in range(2):
        for hops in range(1, 5):
            for piece in pieces_of(way, hops):
                ring_copy(blk, way, hops, piece).wait_send()

    @pl.loop(0, TILES)
    def _(tile):
        send(src, src_all.at[blk], (sa1, ra1), tile, partner).wait_send()
        swap_columns(tile, lc_part, lc_swap, (sl0, rl0)).wait_send()
        swap_columns(tile, cd_part, cd_swap, (sc0, rc0)).wait_send()
        send(lc_in.at[tile], lc_in.at[tile], (sl1, rl1), tile, partner).wait_send()
        send(cd_in.at[tile], cd_in.at[tile], (sc1, rc1), tile, partner).wait_send()
        send(gs_part.at[tile, core], gs_swap.at[tile], (sg0, rg0), tile, partner).wait_send()

        @pl.when(tile > 0)
        def _():
            send(gs_sum.at[tile], gs_in.at[0], (sg1, rg1), tile, partner).wait_send()

    late[4]()
    late[5]()
    put_weights(out, late_bufs[-1], 0)
    leave(2, 2 * ROWS + BLOCK, 2 * D).start()
    leave(2, 2 * ROWS + BLOCK, 2 * D).wait()
    leave(1, OUT_ROWS - 2 * D, 2 * D).wait()
    leave(0, 0, 2 * ROWS + BLOCK).wait()

    late[6]()


def shape(dims, dtype):
    return jax.ShapeDtypeStruct(dims, dtype)


def layer(ref, gout, src, wq, wk, wv, wo, inter):
    vm = pltpu.VMEM
    row = (CHUNK, BLOCK)
    reduction = [
        vm((2, PLANE) + row, BF16), vm((PLANE,) + row, BF16), vm((PLANE,) + row, BF16), vm((PLANE - 1,) + row, BF16),
        vm(row, BF16), vm((CHIPS,) + row, BF16), vm(row, BF16), vm((2, PLANE) + row, BF16),
    ]
    heads = (HEADS, ROWS, BLOCK)
    turned = (HEADS, HEAD_DIM, ROWS)
    pair = (TILES, 2, HEADS, BLOCK)
    columns = [vm(pair, F32), vm(pair, F32), vm(pair, F32), vm((TILES, CHIPS - 1, 2, HEADS, BLOCK), F32), vm(pair, F32)]
    scratch = [
        vm((OUT_ROWS, D), BF16),
        vm((2 * CHIPS, BLOCK, D), BF16), vm((TILES, D, TILE), BF16), vm((TILES, HEADS, TILE, BLOCK), BF16),
        vm((TILES, TILE, D), BF16), vm((TILES, D, TILE), BF16), vm(heads, BF16), vm(heads, BF16), vm(heads, BF16),
        vm(heads, BF16), vm((D, ROWS), BF16), vm((D, ROWS), BF16), vm((TILES, HEADS, ROWS, TILE), F32), vm(heads, F32), vm(heads, F32),
        *columns, *columns,
        vm(turned, F32), vm((HEADS, ROWS, TILE), BF16), vm((TILES, D, TILE), BF16), vm(heads, F32), vm((D, D), F32), vm((D, D), F32), vm(turned, F32),
        vm((TILES, 2, D, BLOCK), BF16), vm((TILES, D, BLOCK), BF16), vm((TILES, D, BLOCK), BF16),
        vm((CHIPS - 1, D, BLOCK), BF16),
        *reduction, *reduction,
        DMA, DMA((8 * PIECES,)), DMA((8 * PIECES,)),
    ] + [DMA((n,)) for n in (8,) * 14 + 2 * (2, 2, 15, 15, 7, 7, 15, 15) + (3,)] + [pltpu.SemaphoreType.REGULAR((7,))]
    return pl.pallas_call(
        layer_kernel,
        out_shape=shape((OUT_ROWS, D), BF16),
        in_specs=[VMEM] * 7 + [SMEM],
        out_specs=HBM,
        scratch_shapes=scratch,
        compiler_params=pltpu.CompilerParams(vmem_limit_bytes=60 << 20, collective_id=1, has_side_effects=True),
        name="layer",
    )(ref, gout, src, wq, wk, wv, wo, inter)


def finish_kernel(parts, matched_out, gref_out, gsrc_out, *rest):
    weights, (rows, packed, wide, in_sems, out_sems) = rest[:4], rest[4:]
    first = 2 * ROWS + BLOCK
    load_weights = pltpu.make_async_copy(parts.at[pl.ds(first, 4 * D)], packed, in_sems.at[0])
    load_rows = pltpu.make_async_copy(parts.at[pl.ds(0, first)], rows, in_sems.at[1])
    load_weights.start()
    load_rows.start()
    stores = []
    load_weights.wait()
    for at, out in enumerate(weights):
        wide[at] = packed[at * D : (at + 1) * D].astype(F32)
        stores.append(pltpu.make_async_copy(wide.at[at], out, out_sems.at[at]))
        stores[-1].start()
    load_rows.wait()
    for at, (out, begin, count) in enumerate(
        ((matched_out, 0, ROWS), (gref_out, ROWS, ROWS), (gsrc_out, 2 * ROWS, BLOCK))
    ):
        stores.append(pltpu.make_async_copy(rows.at[pl.ds(begin, count)], out, out_sems.at[4 + at]))
        stores[-1].start()
    for store in stores:
        store.wait()


def finish(parts):
    return pl.pallas_call(
        finish_kernel,
        out_shape=[shape((ROWS, D), BF16)] * 2 + [shape((BLOCK, D), BF16)] + [shape((D, D), F32)] * 4,
        in_specs=[HBM],
        out_specs=[HBM] * 7,
        scratch_shapes=[
            pltpu.VMEM((2 * ROWS + BLOCK, D), BF16), pltpu.VMEM((4 * D, D), BF16), pltpu.VMEM((4, D, D), F32),
            DMA((2,)), DMA((7,)),
        ],
        compiler_params=pltpu.CompilerParams(vmem_limit_bytes=60 << 20),
        name="finish",
    )(parts)


def on_device(ref_feats, src_feats, grad_out, w_query, w_key, w_value, w_out, intersection):
    parts = layer(ref_feats[0], grad_out[0], src_feats[0], w_query, w_key, w_value, w_out, intersection[0])
    matched, gref, gsrc, wqg, wkg, wvg, wog = finish(parts)
    return matched[None], gref[None], gsrc[None], wqg, wkg, wvg, wog


def solution(mesh):
    split = P("scan", "blk", None)
    return jax.shard_map(
        on_device, mesh=mesh,
        in_specs=(split, split, split, P(), P(), P(), P(), split),
        out_specs=(split, split, split, P(), P(), P(), P()),
        check_vma=False,
    )
```

```python
import functools
import math

import jax
import jax.numpy as jnp
from jax import lax
from jax.experimental import pallas as pl
from jax.experimental.pallas import tpu as pltpu
from jax.sharding import PartitionSpec as P

HEADS = 4
HEAD_DIM = 64
BLOCK = 128
D = 256
ROWS = 512
KEYS = 2048
TILE = 256
TILES = KEYS // TILE
QBLOCKS = ROWS // BLOCK
KBLOCKS = KEYS // BLOCK
CHIPS = 8
PLANE = 16
CHUNK = 32
PIECES = 4
OUT_ROWS = 2 * ROWS + BLOCK + 4 * D
NEG = -1.0e30
SCALE = HEAD_DIM**-0.5
UNIT = SCALE * math.log2(math.e)
F32 = jnp.float32
BF16 = jnp.bfloat16
MESH = pl.DeviceIdType.MESH
VMEM = pl.BlockSpec(memory_space=pltpu.VMEM)
HBM = pl.BlockSpec(memory_space=pltpu.HBM)
SMEM = pl.BlockSpec(memory_space=pltpu.SMEM)
DMA = pltpu.SemaphoreType.DMA


def nn(a, b):
    return jnp.dot(a, b, preferred_element_type=F32)


def nt(a, b):
    return lax.dot_general(a, b, (((1,), (1,)), ((), ())), preferred_element_type=F32)


def lanes_of(rows):
    return lax.broadcasted_iota(jnp.int32, (rows, BLOCK), 1)


def own_lanes(rows, head):
    lane = lanes_of(rows)
    return (lane < HEAD_DIM) if head % 2 == 0 else (lane >= HEAD_DIM)


def spare(head):
    return HEAD_DIM if head % 2 == 0 else 0


def group_cols(head):
    return slice((head // 2) * BLOCK, (head // 2 + 1) * BLOCK)


def head_lanes(head):
    return slice(head * HEAD_DIM, (head + 1) * HEAD_DIM)


def query_extra(inter, head, pieces):
    base = spare(head)
    lane = lanes_of(1)
    grid = []
    for qb in range(QBLOCKS):
        row = jnp.zeros((1, BLOCK), F32)
        for kb in range(KBLOCKS):
            bias = jnp.where(inter[qb, kb] == 1, 0.0, NEG).astype(F32)
            row = jnp.where(lane == base + kb, bias, row)
        grid.append(jnp.broadcast_to(row, (BLOCK, BLOCK)))
    extra = jnp.concatenate(grid, axis=0)
    if pieces is not None:
        lane = lanes_of(ROWS)
        for at, piece in enumerate(pieces):
            extra = jnp.where(lane == base + KBLOCKS + at, piece, extra)
    return extra


def key_extra(tile, head):
    base = spare(head)
    lane = lanes_of(TILE)
    row = lax.broadcasted_iota(jnp.int32, (TILE, BLOCK), 0)
    block = tile * 2 + jnp.where(row >= BLOCK, 1, 0)
    hot = (lane - base == block) | ((lane >= base + KBLOCKS) & (lane < base + KBLOCKS + 3))
    return jnp.where(hot, 1.0, 0.0)


def in_three(value):
    first = value.astype(BF16).astype(F32)
    second = (value - first).astype(BF16).astype(F32)
    third = (value - first - second).astype(BF16).astype(F32)
    return first, second, third


def log_sum(parts):
    peak = functools.reduce(jnp.maximum, parts)
    return peak + jnp.log2(sum(jnp.exp2(part - peak) for part in parts))


def plain_sum(parts):
    return sum(parts)


def pack_weight(wg, core, matrix):
    for half in range(2):
        for part in range(8):
            wg[core, 8 * half + part] = matrix[
                CHUNK * part : CHUNK * (part + 1), half * BLOCK : (half + 1) * BLOCK
            ].astype(BF16)


def put_weights(out, packed, pair):
    for core in range(2):
        first = 2 * ROWS + BLOCK + (2 * pair + core) * D
        for half in range(2):
            for part in range(8):
                out[first + CHUNK * part : first + CHUNK * (part + 1), half * BLOCK : (half + 1) * BLOCK] = packed[
                    core, 8 * half + part
                ]


def in_turn(make, use):
    make(0)
    for head in range(HEADS):
        if head + 1 < HEADS:
            make(head + 1)
        use(head)


def send(src, dst, sems, index, target):
    return pltpu.make_async_remote_copy(
        src_ref=src, dst_ref=dst, send_sem=sems[0].at[index], recv_sem=sems[1].at[index],
        device_id=target, device_id_type=MESH,
    )


def layer_kernel(
    ref, gout, src, wq, wk, wv, wo, inter,
    out_hbm,
    out, src_all, kt_scr, kh, v_scr, vt_scr, qs, qf, qb_scr, gam, gat_scr, qt_all, t_scr, rm, lr,
    lc_part, lc_swap, lc_chip, lc_in, lc_all, cd_part, cd_swap, cd_chip, cd_in, cd_all,
    att, match_scr, gvt_scr, rd_scr, wvg, wkg, gq,
    gs_part, gs_swap, gs_sum, gs_in, *rest,
):
    early_bufs, late_bufs, rest = rest[:8], rest[8:16], rest[16:]
    own_sem, sa0, ra0, sa1, ra1, sl0, rl0, sl1, rl1, sc0, rc0, sc1, rc1, sg0, rg0, sg1, rg1 = rest[:17]
    early_sems, late_sems, out_sems, known = rest[17:25], rest[25:33], rest[33], rest[34]
    blk = lax.axis_index("blk")
    scan = lax.axis_index("scan")
    chip = lax.div(blk, 2)
    core = lax.rem(blk, 2)
    partner = {"blk": chip * 2 + 1 - core}

    def on_chip(offset, core_at):
        return {"blk": lax.rem(chip + offset, CHIPS) * 2 + core_at}

    def from_offset(d):
        return lax.rem(chip + CHIPS - d, CHIPS)

    def to_offset(d):
        return lax.rem(chip + d, CHIPS)

    def ring_copy(block, way, hops, piece, source=None):
        rows = pl.ds(piece * (BLOCK // PIECES), BLOCK // PIECES)
        landing = src_all.at[block, rows]
        return send(
            landing if source is None else source.at[rows], landing, (sa0, ra0),
            (way * 4 + hops - 1) * PIECES + piece, on_chip(1 if way == 0 else CHIPS - 1, core),
        )

    def pieces_of(way, hops):
        return range(PIECES) if hops < 4 else range(way * PIECES // 2, (way + 1) * PIECES // 2)

    def relay(hops):
        for piece in range(PIECES):
            for way in range(2):
                if piece not in pieces_of(way, hops):
                    continue
                origin = from_offset(hops if way == 0 else CHIPS - hops) * 2 + core
                ring_copy(origin, way, hops, piece).wait_recv()
                if hops < 4 and piece in pieces_of(way, hops + 1):
                    ring_copy(origin, way, hops + 1, piece).start()
        for d in (hops, CHIPS - hops) if hops < 4 else (hops,):
            origin = from_offset(d) * 2 + core
            send(src_all.at[origin], src_all.at[origin], (sa1, ra1), d, partner).start()

    plane = [{"scan": lax.rem(scan + d, PLANE)} for d in range(1, PLANE)]
    barrier = pltpu.get_barrier_semaphore()
    row_at, col_at = lax.div(scan, 4), lax.rem(scan, 4)
    beside_z = [on_chip(1, core), on_chip(CHIPS - 1, core)]
    beside_x = [{"scan": row_at * 4 + lax.rem(col_at + d, 4)} for d in (1, 3)]
    beside_y = [{"scan": lax.rem(row_at + d, 4) * 4 + col_at} for d in (1, 3)]
    everyone = [partner] + beside_z + beside_x + beside_y

    def tell(at, targets):
        for target in targets:
            pl.semaphore_signal(known.at[at], inc=1, device_id=target, device_id_type=MESH)

    def hear(at):
        pl.semaphore_wait(known.at[at], 2)

    for target in everyone:
        pl.semaphore_signal(barrier, inc=1, device_id=target, device_id_type=MESH)

    def all_reduce(bufs, sems):
        wg, w_swap, w_sum, w_in, w_part, z_all, w_row, w_all = bufs
        swap_sems, in_sems, z_sems, out_sems = [sems[2 * i : 2 * i + 2] for i in range(4)]
        swap = [
            send(wg.at[1 - core], w_swap, swap_sems, 0, partner),
            send(w_all.at[core], w_all.at[core], swap_sems, 1, partner),
        ]

        def in_plane(d):
            return send(w_sum.at[lax.rem(scan + d, PLANE)], w_in.at[d - 1], in_sems, d - 1, plane[d - 1])

        def in_column(d):
            return send(w_part, z_all.at[chip], z_sems, d - 1, on_chip(d, core))

        def back_plane(d):
            return send(w_row, w_all.at[core, scan], out_sems, d - 1, plane[d - 1])

        def stage_1():
            swap[0].wait_recv()
            w_sum[...] = (wg[core].astype(F32) + w_swap[...].astype(F32)).astype(BF16)
            for d in range(1, PLANE):
                in_plane(d).start()

        def stage_2():
            for d in range(1, PLANE):
                in_plane(d).wait_recv()
            total = w_sum[scan].astype(F32)
            for d in range(PLANE - 1):
                total = total + w_in[d].astype(F32)
            part = total.astype(BF16)
            w_part[...] = part
            z_all[chip] = part
            for d in range(1, CHIPS):
                in_column(d).start()

        def stage_3():
            for d in range(1, CHIPS):
                in_column(d).wait_recv()
            total = z_all[0].astype(F32)
            for c in range(1, CHIPS):
                total = total + z_all[c].astype(F32)
            row = total.astype(BF16)
            w_row[...] = row
            w_all[core, scan] = row
            for d in range(1, PLANE):
                back_plane(d).start()

        def stage_4():
            for d in range(1, PLANE):
                back_plane(d).wait_recv()
            swap[1].start()

        def left():
            for copy in swap:
                copy.wait_send()
            for make, count in ((in_plane, PLANE), (in_column, CHIPS), (back_plane, PLANE)):
                for d in range(1, count):
                    make(d).wait_send()

        return swap[0].start, stage_1, stage_2, stage_3, stage_4, swap[1].wait_recv, left

    q_rows = nn(ref[...], wq[...]).astype(BF16)
    for head in range(HEADS):
        part = q_rows[:, group_cols(head)]
        extra = query_extra(inter, head, None).astype(BF16)
        qs[head] = jnp.where(own_lanes(ROWS, head), part, extra)
    qt_all[...] = q_rows.T
    rm[...] = jnp.full_like(rm, -3.0e38)
    own = pltpu.make_async_copy(src, src_all.at[blk], own_sem)
    own.start()

    pl.semaphore_wait(barrier, len(everyone))
    for piece in range(PIECES):
        for way in range(2):
            ring_copy(blk, way, 1, piece, src).start()
    send(src, src_all.at[blk], (sa1, ra1), 0, partner).start()
    tell(0, beside_z)
    tell(4, beside_x)

    ga_rows = nt(gout[...], wo[...]).astype(BF16)
    gat_scr[...] = nt(wo[...], gout[...]).astype(BF16)
    for head in range(HEADS):
        part = ga_rows[:, group_cols(head)]
        gam[head] = jnp.where(own_lanes(ROWS, head), part, jnp.zeros_like(part))
    wvt = wv[...].T
    wkt = wk[...].T
    own.wait()

    def near_first(step):
        half = lax.div(step + 1, 2)
        return jnp.where(lax.rem(step, 2) == 1, half, lax.rem(CHIPS - half, CHIPS))

    def by_quarters(step):
        return lax.div(step, 4) * 4 + lax.rem(chip + 1 + step, 4)

    def swap_columns(tile, part, swap, sems):
        return send(part.at[tile], swap.at[tile], sems, tile, partner)

    def spread_columns(tile, combine, part, swap, chip_sum, inbox, sems_swap, sems):
        swap_columns(tile, part, swap, sems_swap).wait_recv()
        chip_sum[tile] = combine([part[tile], swap[tile]])
        for d in range(1, CHIPS):
            for c in range(2):
                send(chip_sum.at[tile, core], inbox.at[tile, d - 1, core], sems, tile, on_chip(d, c)).start()

    def collect_columns(tile, combine, chip_sum, inbox, total, sems):
        send(inbox.at[tile], inbox.at[tile], sems, tile, partner).wait_recv()
        total[tile] = combine([chip_sum[tile]] + [inbox[tile, d] for d in range(CHIPS - 1)])

    @pl.loop(0, TILES)
    def _(step):
        d = near_first(step)
        tile = from_offset(d)

        for at, hops in ((1, 1), (2, 2), (4, 3), (6, 4)):

            @pl.when(step == at)
            def _():
                relay(hops)

        for at, rounds in (
            (1, ((0, 1, beside_z),)), (2, ((1, 2, beside_z), (4, 5, beside_y))), (3, ((2, 3, beside_z),)),
            (4, ((3, None, None), (5, 6, beside_y))), (6, ((6, None, None),)),
        ):

            @pl.when(step == at)
            def _():
                for heard, told, targets in rounds:
                    hear(heard)
                    if told is not None:
                        tell(told, targets)

        send(src, src_all.at[tile * 2 + 1 - core], (sa1, ra1), d, partner).wait_recv()
        rows = src_all[pl.ds(tile * 2, 2)].reshape(TILE, D)
        k_tile = nn(rows, wk[...]).astype(BF16)
        kt_scr[tile] = nt(wkt, rows).astype(BF16)
        v_scr[tile] = nn(rows, wv[...]).astype(BF16)
        vt_scr[tile] = nt(wvt, rows).astype(BF16)
        for head in range(HEADS):
            keys = jnp.where(own_lanes(TILE, head), k_tile[:, group_cols(head)], key_extra(tile, head).astype(BF16))
            kh[tile, head] = keys
            t = nt(qs[head], keys) * UNIT
            t_scr[tile, head] = t
            rm[head] = jnp.maximum(rm[head], jnp.maximum(t[:, :BLOCK], t[:, BLOCK:]))
            peak = t.max(axis=0, keepdims=True)
            total = jnp.exp2(t - peak).sum(axis=0, keepdims=True)
            lse = peak + jnp.log2(total)
            for kb in range(2):
                lc_part[tile, kb, head : head + 1, :] = lse[:, kb * BLOCK : (kb + 1) * BLOCK]
        swap_columns(tile, lc_part, lc_swap, (sl0, rl0)).start()

        def spread(d):
            spread_columns(
                from_offset(d), log_sum, lc_part, lc_swap, lc_chip, lc_in, (sl0, rl0), (sl1, rl1)
            )

        @pl.when(step == 4)
        def _():
            for d in (0, 1, 7, 2):
                spread(d)

        @pl.when(step > 4)
        def _():
            spread(near_first(step - 1))

    spread_columns(
        from_offset(4), log_sum, lc_part, lc_swap, lc_chip, lc_in, (sl0, rl0), (sl1, rl1)
    )

    for head in range(HEADS):
        peak = rm[head].max(axis=1, keepdims=True)
        rm[head] = jnp.zeros((ROWS, BLOCK), F32)

        @pl.loop(0, TILES)
        def _(tile):
            rm[head] += jnp.exp2(t_scr[tile, head, :, :BLOCK] - peak) + jnp.exp2(t_scr[tile, head, :, BLOCK:] - peak)

        total = rm[head].sum(axis=1, keepdims=True)
        row_term = peak + jnp.log2(total)
        lr[head] = jnp.broadcast_to(row_term, (ROWS, BLOCK))
        extra = query_extra(inter, head, in_three(row_term * (-1.0 / UNIT))).astype(BF16)
        part = qs[head]
        mask = own_lanes(ROWS, head)
        qb_scr[head] = jnp.where(mask, part, extra)
        qf[head] = jnp.where(mask, part + part, extra)

    att[...] = jnp.zeros_like(att)
    wvg[...] = jnp.zeros_like(wvg)

    @pl.loop(0, TILES)
    def _(tile):
        collect_columns(tile, log_sum, lc_chip, lc_in, lc_all, (sl1, rl1))
        rows = src_all[pl.ds(tile * 2, 2)].reshape(TILE, D)

        def make_match(head):
            lc_row = jnp.concatenate([lc_all[tile, kb, head : head + 1, :] for kb in range(2)], axis=1)
            match_scr[head] = jnp.exp2(nt(qf[head], kh[tile, head]) * UNIT - lc_row).astype(BF16)

        def use_match(head):
            match = match_scr[head]
            att[head] += nt(vt_scr[tile, head_lanes(head), :], match)
            gvt = nn(gat_scr[head_lanes(head), :], match)
            gvt_scr[tile, head_lanes(head), :] = gvt.astype(BF16)
            dots = (gvt * vt_scr[tile, head_lanes(head), :].astype(F32)).sum(axis=0, keepdims=True)
            for kb in range(2):
                cd_part[tile, kb, head : head + 1, :] = dots[:, kb * BLOCK : (kb + 1) * BLOCK]

        in_turn(make_match, use_match)
        swap_columns(tile, cd_part, cd_swap, (sc0, rc0)).start()
        wvg[...] += nn(gvt_scr[tile], rows)

        @pl.when(tile > 0)
        def _():
            spread_columns(tile - 1, plain_sum, cd_part, cd_swap, cd_chip, cd_in, (sc0, rc0), (sc1, rc1))

    spread_columns(TILES - 1, plain_sum, cd_part, cd_swap, cd_chip, cd_in, (sc0, rc0), (sc1, rc1))

    att_t = att[...].reshape(D, ROWS)
    att_rows = att_t.T
    for head in range(HEADS):
        rd = (att_rows[:, group_cols(head)] * gam[head].astype(F32)).sum(axis=1, keepdims=True)
        rd_scr[head] = jnp.broadcast_to(rd, (ROWS, BLOCK))
        gam[head] = gam[head] + gam[head]
    out[:ROWS] = (ref[...].astype(F32) + nn(att_rows.astype(BF16), wo[...])).astype(BF16)
    pack_weight(early_bufs[0], 1, nn(att_t.astype(BF16), gout[...]))
    pack_weight(early_bufs[0], 0, wvg[...].T)
    early = all_reduce(early_bufs, early_sems)
    early[0]()
    gq[...] = jnp.zeros_like(gq)
    wkg[...] = jnp.zeros_like(wkg)

    def source_copy(d):
        return send(gs_sum.at[to_offset(d)], gs_in.at[d - 1], (sg1, rg1), d, on_chip(d, core))

    def spread_source(tile):
        send(gs_part.at[tile, core], gs_swap.at[tile], (sg0, rg0), tile, partner).wait_recv()
        gs_sum[tile] = (gs_part[tile, core].astype(F32) + gs_swap[tile].astype(F32)).astype(BF16)
        d = lax.rem(tile + CHIPS - chip, CHIPS)

        @pl.when(d > 0)
        def _():
            source_copy(d).start()

    @pl.loop(0, TILES)
    def _(step):
        tile = by_quarters(step)
        for at, stage in ((1, 1), (5, 2)):

            @pl.when(step == at)
            def _():
                early[stage]()

        collect_columns(tile, plain_sum, cd_chip, cd_in, cd_all, (sc1, rc1))
        rows = src_all[pl.ds(tile * 2, 2)].reshape(TILE, D)
        gk_heads = []

        def make_grad(head):
            cols = group_cols(head)
            for half in range(2):
                rows = slice(half * TILE, (half + 1) * TILE)
                x = nt(qb_scr[head, rows], kh[tile, head])
                gp = nt(gam[head, rows], v_scr[tile, :, cols])
                lines = []
                for kb in range(2):
                    lanes = slice(kb * BLOCK, (kb + 1) * BLOCK)
                    lc_row = lc_all[tile, kb, head : head + 1, :]
                    cd_row = cd_all[tile, kb, head : head + 1, :]
                    u = x[:, lanes] * UNIT
                    r = jnp.exp2(u)
                    c = jnp.exp2(u + lr[head, rows] - lc_row)
                    lines.append((r * (c * gp[:, lanes] - rd_scr[head, rows]) - c * cd_row).astype(BF16))
                match_scr[head, rows] = jnp.concatenate(lines, axis=1)

        def use_grad(head):
            gs = match_scr[head]
            gq[head] += nt(kt_scr[tile, head_lanes(head), :], gs)
            gk_heads.append((nn(qt_all[head_lanes(head), :], gs) * SCALE).astype(BF16))
        in_turn(make_grad, use_grad)
        gkt = jnp.concatenate(gk_heads, axis=0)
        wkg[...] += nn(gkt, rows)
        gst = nn(wk[...], gkt) + nn(wv[...], gvt_scr[tile])
        for kb in range(2):
            gs_part[tile, kb] = gst[:, kb * BLOCK : (kb + 1) * BLOCK].astype(BF16)
        send(gs_part.at[tile, 1 - core], gs_swap.at[tile], (sg0, rg0), tile, partner).start()

        @pl.when(step > 0)
        def _():
            spread_source(by_quarters(step - 1))

    gq_t = (gq[...].reshape(D, ROWS) * SCALE).astype(BF16)
    pack_weight(late_bufs[0], 0, nn(gq_t, ref[...]).T)
    pack_weight(late_bufs[0], 1, wkg[...].T)
    late = all_reduce(late_bufs, late_sems)

    def leave(at, first, count):
        rows = pl.ds(first, count)
        return pltpu.make_async_copy(out.at[rows], out_hbm.at[rows], out_sems.at[at])

    late[0]()
    early[3]()
    gref = (gout[...].astype(F32) + nt(gq_t.T, wq[...])).astype(BF16)
    late[1]()
    out[ROWS : 2 * ROWS] = gref
    spread_source(by_quarters(TILES - 1))
    early[4]()
    late[2]()
    for d in (4, 3, 5, 2, 6, 1, 7):
        source_copy(d).wait_recv()
    gsrc = gs_sum[chip].astype(F32)
    for d in range(CHIPS - 1):
        gsrc = gsrc + gs_in[d].astype(F32)
    out[2 * ROWS : 2 * ROWS + BLOCK] = gsrc.T.astype(BF16)
    leave(0, 0, 2 * ROWS + BLOCK).start()
    early[5]()
    put_weights(out, early_bufs[-1], 1)
    leave(1, OUT_ROWS - 2 * D, 2 * D).start()
    late[3]()

    early[6]()
    for way in range(2):
        for hops in range(1, 5):
            for piece in pieces_of(way, hops):
                ring_copy(blk, way, hops, piece).wait_send()

    @pl.loop(0, TILES)
    def _(tile):
        send(src, src_all.at[blk], (sa1, ra1), tile, partner).wait_send()
        swap_columns(tile, lc_part, lc_swap, (sl0, rl0)).wait_send()
        swap_columns(tile, cd_part, cd_swap, (sc0, rc0)).wait_send()
        send(lc_in.at[tile], lc_in.at[tile], (sl1, rl1), tile, partner).wait_send()
        send(cd_in.at[tile], cd_in.at[tile], (sc1, rc1), tile, partner).wait_send()
        send(gs_part.at[tile, core], gs_swap.at[tile], (sg0, rg0), tile, partner).wait_send()

        @pl.when(tile > 0)
        def _():
            send(gs_sum.at[tile], gs_in.at[0], (sg1, rg1), tile, partner).wait_send()

    late[4]()
    late[5]()
    put_weights(out, late_bufs[-1], 0)
    leave(2, 2 * ROWS + BLOCK, 2 * D).start()
    leave(2, 2 * ROWS + BLOCK, 2 * D).wait()
    leave(1, OUT_ROWS - 2 * D, 2 * D).wait()
    leave(0, 0, 2 * ROWS + BLOCK).wait()

    late[6]()


def shape(dims, dtype):
    return jax.ShapeDtypeStruct(dims, dtype)


def layer(ref, gout, src, wq, wk, wv, wo, inter):
    vm = pltpu.VMEM
    row = (CHUNK, BLOCK)
    reduction = [
        vm((2, PLANE) + row, BF16), vm((PLANE,) + row, BF16), vm((PLANE,) + row, BF16), vm((PLANE - 1,) + row, BF16),
        vm(row, BF16), vm((CHIPS,) + row, BF16), vm(row, BF16), vm((2, PLANE) + row, BF16),
    ]
    heads = (HEADS, ROWS, BLOCK)
    turned = (HEADS, HEAD_DIM, ROWS)
    pair = (TILES, 2, HEADS, BLOCK)
    columns = [vm(pair, F32), vm(pair, F32), vm(pair, F32), vm((TILES, CHIPS - 1, 2, HEADS, BLOCK), F32), vm(pair, F32)]
    scratch = [
        vm((OUT_ROWS, D), BF16),
        vm((2 * CHIPS, BLOCK, D), BF16), vm((TILES, D, TILE), BF16), vm((TILES, HEADS, TILE, BLOCK), BF16),
        vm((TILES, TILE, D), BF16), vm((TILES, D, TILE), BF16), vm(heads, BF16), vm(heads, BF16), vm(heads, BF16),
        vm(heads, BF16), vm((D, ROWS), BF16), vm((D, ROWS), BF16), vm((TILES, HEADS, ROWS, TILE), F32), vm(heads, F32), vm(heads, F32),
        *columns, *columns,
        vm(turned, F32), vm((HEADS, ROWS, TILE), BF16), vm((TILES, D, TILE), BF16), vm(heads, F32), vm((D, D), F32), vm((D, D), F32), vm(turned, F32),
        vm((TILES, 2, D, BLOCK), BF16), vm((TILES, D, BLOCK), BF16), vm((TILES, D, BLOCK), BF16),
        vm((CHIPS - 1, D, BLOCK), BF16),
        *reduction, *reduction,
        DMA, DMA((8 * PIECES,)), DMA((8 * PIECES,)),
    ] + [DMA((n,)) for n in (8,) * 14 + 2 * (2, 2, 15, 15, 7, 7, 15, 15) + (3,)] + [pltpu.SemaphoreType.REGULAR((7,))]
    return pl.pallas_call(
        layer_kernel,
        out_shape=shape((OUT_ROWS, D), BF16),
        in_specs=[VMEM] * 7 + [SMEM],
        out_specs=HBM,
        scratch_shapes=scratch,
        compiler_params=pltpu.CompilerParams(vmem_limit_bytes=60 << 20, collective_id=1, has_side_effects=True),
        name="layer",
    )(ref, gout, src, wq, wk, wv, wo, inter)


def finish_kernel(parts, matched_out, gref_out, gsrc_out, *rest):
    weights, (rows, packed, wide, in_sems, out_sems) = rest[:4], rest[4:]
    first = 2 * ROWS + BLOCK
    load_weights = pltpu.make_async_copy(parts.at[pl.ds(first, 4 * D)], packed, in_sems.at[0])
    load_rows = pltpu.make_async_copy(parts.at[pl.ds(0, first)], rows, in_sems.at[1])
    load_weights.start()
    load_rows.start()
    stores = []
    load_weights.wait()
    for at, out in enumerate(weights):
        wide[at] = packed[at * D : (at + 1) * D].astype(F32)
        stores.append(pltpu.make_async_copy(wide.at[at], out, out_sems.at[at]))
        stores[-1].start()
    load_rows.wait()
    for at, (out, begin, count) in enumerate(
        ((matched_out, 0, ROWS), (gref_out, ROWS, ROWS), (gsrc_out, 2 * ROWS, BLOCK))
    ):
        stores.append(pltpu.make_async_copy(rows.at[pl.ds(begin, count)], out, out_sems.at[4 + at]))
        stores[-1].start()
    for store in stores:
        store.wait()


def finish(parts):
    return pl.pallas_call(
        finish_kernel,
        out_shape=[shape((ROWS, D), BF16)] * 2 + [shape((BLOCK, D), BF16)] + [shape((D, D), F32)] * 4,
        in_specs=[HBM],
        out_specs=[HBM] * 7,
        scratch_shapes=[
            pltpu.VMEM((2 * ROWS + BLOCK, D), BF16), pltpu.VMEM((4 * D, D), BF16), pltpu.VMEM((4, D, D), F32),
            DMA((2,)), DMA((7,)),
        ],
        compiler_params=pltpu.CompilerParams(vmem_limit_bytes=60 << 20),
        name="finish",
    )(parts)


def on_device(ref_feats, src_feats, grad_out, w_query, w_key, w_value, w_out, intersection):
    parts = layer(ref_feats[0], grad_out[0], src_feats[0], w_query, w_key, w_value, w_out, intersection[0])
    matched, gref, gsrc, wqg, wkg, wvg, wog = finish(parts)
    return matched[None], gref[None], gsrc[None], wqg, wkg, wvg, wog


def solution(mesh):
    split = P("scan", "blk", None)
    return jax.shard_map(
        on_device, mesh=mesh,
        in_specs=(split, split, split, P(), P(), P(), P(), split),
        out_specs=(split, split, split, P(), P(), P(), P()),
        check_vma=False,
    )
```

```python
import functools
import math

import jax
import jax.numpy as jnp
from jax import lax
from jax.experimental import pallas as pl
from jax.experimental.pallas import tpu as pltpu
from jax.sharding import PartitionSpec as P

HEADS = 4
HEAD_DIM = 64
BLOCK = 128
D = 256
ROWS = 512
KEYS = 2048
TILE = 256
TILES = KEYS // TILE
QBLOCKS = ROWS // BLOCK
KBLOCKS = KEYS // BLOCK
CHIPS = 8
PLANE = 16
CHUNK = 32
PIECES = 4
OUT_ROWS = 2 * ROWS + BLOCK + 4 * D
NEG = -1.0e30
SCALE = HEAD_DIM**-0.5
UNIT = SCALE * math.log2(math.e)
F32 = jnp.float32
BF16 = jnp.bfloat16
MESH = pl.DeviceIdType.MESH
VMEM = pl.BlockSpec(memory_space=pltpu.VMEM)
HBM = pl.BlockSpec(memory_space=pltpu.HBM)
SMEM = pl.BlockSpec(memory_space=pltpu.SMEM)
DMA = pltpu.SemaphoreType.DMA


def nn(a, b):
    return jnp.dot(a, b, preferred_element_type=F32)


def nt(a, b):
    return lax.dot_general(a, b, (((1,), (1,)), ((), ())), preferred_element_type=F32)


def lanes_of(rows):
    return lax.broadcasted_iota(jnp.int32, (rows, BLOCK), 1)


def own_lanes(rows, head):
    lane = lanes_of(rows)
    return (lane < HEAD_DIM) if head % 2 == 0 else (lane >= HEAD_DIM)


def spare(head):
    return HEAD_DIM if head % 2 == 0 else 0


def group_cols(head):
    return slice((head // 2) * BLOCK, (head // 2 + 1) * BLOCK)


def head_lanes(head):
    return slice(head * HEAD_DIM, (head + 1) * HEAD_DIM)


def query_extra(inter, head, pieces):
    base = spare(head)
    lane = lanes_of(1)
    grid = []
    for qb in range(QBLOCKS):
        row = jnp.zeros((1, BLOCK), F32)
        for kb in range(KBLOCKS):
            bias = jnp.where(inter[qb, kb] == 1, 0.0, NEG).astype(F32)
            row = jnp.where(lane == base + kb, bias, row)
        grid.append(jnp.broadcast_to(row, (BLOCK, BLOCK)))
    extra = jnp.concatenate(grid, axis=0)
    if pieces is not None:
        lane = lanes_of(ROWS)
        for at, piece in enumerate(pieces):
            extra = jnp.where(lane == base + KBLOCKS + at, piece, extra)
    return extra


def key_extra(tile, head):
    base = spare(head)
    lane = lanes_of(TILE)
    row = lax.broadcasted_iota(jnp.int32, (TILE, BLOCK), 0)
    block = tile * 2 + jnp.where(row >= BLOCK, 1, 0)
    hot = (lane - base == block) | ((lane >= base + KBLOCKS) & (lane < base + KBLOCKS + 3))
    return jnp.where(hot, 1.0, 0.0)


def in_three(value):
    first = value.astype(BF16).astype(F32)
    second = (value - first).astype(BF16).astype(F32)
    third = (value - first - second).astype(BF16).astype(F32)
    return first, second, third


def log_sum(parts):
    peak = functools.reduce(jnp.maximum, parts)
    return peak + jnp.log2(sum(jnp.exp2(part - peak) for part in parts))


def plain_sum(parts):
    return sum(parts)


def pack_weight(wg, core, matrix):
    for half in range(2):
        for part in range(8):
            wg[core, 8 * half + part] = matrix[
                CHUNK * part : CHUNK * (part + 1), half * BLOCK : (half + 1) * BLOCK
            ].astype(BF16)


def put_weights(out, packed, pair):
    for core in range(2):
        first = 2 * ROWS + BLOCK + (2 * pair + core) * D
        for half in range(2):
            for part in range(8):
                out[first + CHUNK * part : first + CHUNK * (part + 1), half * BLOCK : (half + 1) * BLOCK] = packed[
                    core, 8 * half + part
                ]


def in_turn(make, use):
    make(0)
    for head in range(HEADS):
        if head + 1 < HEADS:
            make(head + 1)
        use(head)


def send(src, dst, sems, index, target):
    return pltpu.make_async_remote_copy(
        src_ref=src, dst_ref=dst, send_sem=sems[0].at[index], recv_sem=sems[1].at[index],
        device_id=target, device_id_type=MESH,
    )


def layer_kernel(
    ref_hbm, gout_hbm, src, wq_hbm, wk_hbm, wv_hbm, wo_hbm, inter,
    out_hbm,
    ref, gout, wq, wk, wv, wo, out, src_all, kt_scr, kh, v_scr, vt_scr, qs, qf, qb_scr, gam, gat_scr, qt_all, t_scr, rm, lr,
    lc_part, lc_swap, lc_chip, lc_in, lc_all, cd_part, cd_swap, cd_chip, cd_in, cd_all,
    att, match_scr, gvt_scr, rd_scr, wvg, wkg, gq,
    gs_part, gs_swap, gs_sum, gs_in, *rest,
):
    early_bufs, late_bufs, rest = rest[:8], rest[8:16], rest[16:]
    own_sem, sa0, ra0, sa1, ra1, sl0, rl0, sl1, rl1, sc0, rc0, sc1, rc1, sg0, rg0, sg1, rg1 = rest[:17]
    early_sems, late_sems, out_sems, known, load_sems = (
        rest[17:25], rest[25:33], rest[33], rest[34], rest[35]
    )
    blk = lax.axis_index("blk")
    scan = lax.axis_index("scan")
    chip = lax.div(blk, 2)
    core = lax.rem(blk, 2)
    partner = {"blk": chip * 2 + 1 - core}

    def on_chip(offset, core_at):
        return {"blk": lax.rem(chip + offset, CHIPS) * 2 + core_at}

    def from_offset(d):
        return lax.rem(chip + CHIPS - d, CHIPS)

    def to_offset(d):
        return lax.rem(chip + d, CHIPS)

    def ring_copy(block, way, hops, piece, source=None):
        rows = pl.ds(piece * (BLOCK // PIECES), BLOCK // PIECES)
        landing = src_all.at[block, rows]
        return send(
            landing if source is None else source.at[rows], landing, (sa0, ra0),
            (way * 4 + hops - 1) * PIECES + piece, on_chip(1 if way == 0 else CHIPS - 1, core),
        )

    def pieces_of(way, hops):
        return range(PIECES) if hops < 4 else range(way * PIECES // 2, (way + 1) * PIECES // 2)

    def relay(hops):
        for piece in range(PIECES):
            for way in range(2):
                if piece not in pieces_of(way, hops):
                    continue
                origin = from_offset(hops if way == 0 else CHIPS - hops) * 2 + core
                ring_copy(origin, way, hops, piece).wait_recv()
                if hops < 4 and piece in pieces_of(way, hops + 1):
                    ring_copy(origin, way, hops + 1, piece).start()
        for d in (hops, CHIPS - hops) if hops < 4 else (hops,):
            origin = from_offset(d) * 2 + core
            send(src_all.at[origin], src_all.at[origin], (sa1, ra1), d, partner).start()

    plane = [{"scan": lax.rem(scan + d, PLANE)} for d in range(1, PLANE)]
    pairs = ((wq_hbm, wq), (ref_hbm, ref), (wo_hbm, wo), (gout_hbm, gout), (wk_hbm, wk), (wv_hbm, wv))
    loads = [pltpu.make_async_copy(a, b, load_sems.at[at]) for at, (a, b) in enumerate(pairs)]
    own = pltpu.make_async_copy(src, src_all.at[blk], own_sem)
    barrier = pltpu.get_barrier_semaphore()
    row_at, col_at = lax.div(scan, 4), lax.rem(scan, 4)
    beside_z = [on_chip(1, core), on_chip(CHIPS - 1, core)]
    beside_x = [{"scan": row_at * 4 + lax.rem(col_at + d, 4)} for d in (1, 3)]
    beside_y = [{"scan": lax.rem(row_at + d, 4) * 4 + col_at} for d in (1, 3)]
    everyone = [partner] + beside_z + beside_x + beside_y

    def tell(at, targets):
        for target in targets:
            pl.semaphore_signal(known.at[at], inc=1, device_id=target, device_id_type=MESH)

    def hear(at):
        pl.semaphore_wait(known.at[at], 2)

    for target in everyone:
        pl.semaphore_signal(barrier, inc=1, device_id=target, device_id_type=MESH)
    for load in loads:
        load.start()
    own.start()

    def all_reduce(bufs, sems):
        wg, w_swap, w_sum, w_in, w_part, z_all, w_row, w_all = bufs
        swap_sems, in_sems, z_sems, out_sems = [sems[2 * i : 2 * i + 2] for i in range(4)]
        swap = [
            send(wg.at[1 - core], w_swap, swap_sems, 0, partner),
            send(w_all.at[core], w_all.at[core], swap_sems, 1, partner),
        ]

        def in_plane(d):
            return send(w_sum.at[lax.rem(scan + d, PLANE)], w_in.at[d - 1], in_sems, d - 1, plane[d - 1])

        def in_column(d):
            return send(w_part, z_all.at[chip], z_sems, d - 1, on_chip(d, core))

        def back_plane(d):
            return send(w_row, w_all.at[core, scan], out_sems, d - 1, plane[d - 1])

        def stage_1():
            swap[0].wait_recv()
            w_sum[...] = (wg[core].astype(F32) + w_swap[...].astype(F32)).astype(BF16)
            for d in range(1, PLANE):
                in_plane(d).start()

        def stage_2():
            for d in range(1, PLANE):
                in_plane(d).wait_recv()
            total = w_sum[scan].astype(F32)
            for d in range(PLANE - 1):
                total = total + w_in[d].astype(F32)
            part = total.astype(BF16)
            w_part[...] = part
            z_all[chip] = part
            for d in range(1, CHIPS):
                in_column(d).start()

        def stage_3():
            for d in range(1, CHIPS):
                in_column(d).wait_recv()
            total = z_all[0].astype(F32)
            for c in range(1, CHIPS):
                total = total + z_all[c].astype(F32)
            row = total.astype(BF16)
            w_row[...] = row
            w_all[core, scan] = row
            for d in range(1, PLANE):
                back_plane(d).start()

        def stage_4():
            for d in range(1, PLANE):
                back_plane(d).wait_recv()
            swap[1].start()

        def left():
            for copy in swap:
                copy.wait_send()
            for make, count in ((in_plane, PLANE), (in_column, CHIPS), (back_plane, PLANE)):
                for d in range(1, count):
                    make(d).wait_send()

        return swap[0].start, stage_1, stage_2, stage_3, stage_4, swap[1].wait_recv, left

    pl.semaphore_wait(barrier, len(everyone))
    for piece in range(PIECES):
        for way in range(2):
            ring_copy(blk, way, 1, piece, src).start()
    send(src, src_all.at[blk], (sa1, ra1), 0, partner).start()
    tell(0, beside_z)
    tell(4, beside_x)

    for load in loads:
        load.wait()
    q_rows = nn(ref[...], wq[...]).astype(BF16)
    for head in range(HEADS):
        part = q_rows[:, group_cols(head)]
        extra = query_extra(inter, head, None).astype(BF16)
        qs[head] = jnp.where(own_lanes(ROWS, head), part, extra)
    qt_all[...] = q_rows.T
    rm[...] = jnp.full_like(rm, -3.0e38)
    ga_rows = nt(gout[...], wo[...]).astype(BF16)
    gat_scr[...] = nt(wo[...], gout[...]).astype(BF16)
    for head in range(HEADS):
        part = ga_rows[:, group_cols(head)]
        gam[head] = jnp.where(own_lanes(ROWS, head), part, jnp.zeros_like(part))
    wvt = wv[...].T
    wkt = wk[...].T
    own.wait()

    def near_first(step):
        half = lax.div(step + 1, 2)
        return jnp.where(lax.rem(step, 2) == 1, half, lax.rem(CHIPS - half, CHIPS))

    def by_quarters(step):
        return lax.div(step, 4) * 4 + lax.rem(chip + 1 + step, 4)

    def swap_columns(tile, part, swap, sems):
        return send(part.at[tile], swap.at[tile], sems, tile, partner)

    def spread_columns(tile, combine, part, swap, chip_sum, inbox, sems_swap, sems):
        swap_columns(tile, part, swap, sems_swap).wait_recv()
        chip_sum[tile] = combine([part[tile], swap[tile]])
        for d in range(1, CHIPS):
            for c in range(2):
                send(chip_sum.at[tile, core], inbox.at[tile, d - 1, core], sems, tile, on_chip(d, c)).start()

    def collect_columns(tile, combine, chip_sum, inbox, total, sems):
        send(inbox.at[tile], inbox.at[tile], sems, tile, partner).wait_recv()
        total[tile] = combine([chip_sum[tile]] + [inbox[tile, d] for d in range(CHIPS - 1)])

    @pl.loop(0, TILES)
    def _(step):
        d = near_first(step)
        tile = from_offset(d)

        for at, hops in ((1, 1), (2, 2), (4, 3), (6, 4)):

            @pl.when(step == at)
            def _():
                relay(hops)

        for at, rounds in (
            (1, ((0, 1, beside_z),)), (2, ((1, 2, beside_z), (4, 5, beside_y))), (3, ((2, 3, beside_z),)),
            (4, ((3, None, None), (5, 6, beside_y))), (6, ((6, None, None),)),
        ):

            @pl.when(step == at)
            def _():
                for heard, told, targets in rounds:
                    hear(heard)
                    if told is not None:
                        tell(told, targets)

        send(src, src_all.at[tile * 2 + 1 - core], (sa1, ra1), d, partner).wait_recv()
        rows = src_all[pl.ds(tile * 2, 2)].reshape(TILE, D)
        k_tile = nn(rows, wk[...]).astype(BF16)
        kt_scr[tile] = nt(wkt, rows).astype(BF16)
        v_scr[tile] = nn(rows, wv[...]).astype(BF16)
        vt_scr[tile] = nt(wvt, rows).astype(BF16)
        for head in range(HEADS):
            keys = jnp.where(own_lanes(TILE, head), k_tile[:, group_cols(head)], key_extra(tile, head).astype(BF16))
            kh[tile, head] = keys
            t = nt(qs[head], keys) * UNIT
            t_scr[tile, head] = t
            rm[head] = jnp.maximum(rm[head], jnp.maximum(t[:, :BLOCK], t[:, BLOCK:]))
            peak = t.max(axis=0, keepdims=True)
            total = jnp.exp2(t - peak).sum(axis=0, keepdims=True)
            lse = peak + jnp.log2(total)
            for kb in range(2):
                lc_part[tile, kb, head : head + 1, :] = lse[:, kb * BLOCK : (kb + 1) * BLOCK]
        swap_columns(tile, lc_part, lc_swap, (sl0, rl0)).start()

        def spread(d):
            spread_columns(
                from_offset(d), log_sum, lc_part, lc_swap, lc_chip, lc_in, (sl0, rl0), (sl1, rl1)
            )

        @pl.when(step == 4)
        def _():
            for d in (0, 1, 7, 2):
                spread(d)

        @pl.when(step > 4)
        def _():
            spread(near_first(step - 1))

    spread_columns(
        from_offset(4), log_sum, lc_part, lc_swap, lc_chip, lc_in, (sl0, rl0), (sl1, rl1)
    )

    for head in range(HEADS):
        peak = rm[head].max(axis=1, keepdims=True)
        rm[head] = jnp.zeros((ROWS, BLOCK), F32)

        @pl.loop(0, TILES)
        def _(tile):
            rm[head] += jnp.exp2(t_scr[tile, head, :, :BLOCK] - peak) + jnp.exp2(t_scr[tile, head, :, BLOCK:] - peak)

        total = rm[head].sum(axis=1, keepdims=True)
        row_term = peak + jnp.log2(total)
        lr[head] = jnp.broadcast_to(row_term, (ROWS, BLOCK))
        extra = query_extra(inter, head, in_three(row_term * (-1.0 / UNIT))).astype(BF16)
        part = qs[head]
        mask = own_lanes(ROWS, head)
        qb_scr[head] = jnp.where(mask, part, extra)
        qf[head] = jnp.where(mask, part + part, extra)

    att[...] = jnp.zeros_like(att)
    wvg[...] = jnp.zeros_like(wvg)

    @pl.loop(0, TILES)
    def _(tile):
        collect_columns(tile, log_sum, lc_chip, lc_in, lc_all, (sl1, rl1))
        rows = src_all[pl.ds(tile * 2, 2)].reshape(TILE, D)

        def make_match(head):
            lc_row = jnp.concatenate([lc_all[tile, kb, head : head + 1, :] for kb in range(2)], axis=1)
            match_scr[head] = jnp.exp2(nt(qf[head], kh[tile, head]) * UNIT - lc_row).astype(BF16)

        def use_match(head):
            match = match_scr[head]
            att[head] += nt(vt_scr[tile, head_lanes(head), :], match)
            gvt = nn(gat_scr[head_lanes(head), :], match)
            gvt_scr[tile, head_lanes(head), :] = gvt.astype(BF16)
            dots = (gvt * vt_scr[tile, head_lanes(head), :].astype(F32)).sum(axis=0, keepdims=True)
            for kb in range(2):
                cd_part[tile, kb, head : head + 1, :] = dots[:, kb * BLOCK : (kb + 1) * BLOCK]

        in_turn(make_match, use_match)
        swap_columns(tile, cd_part, cd_swap, (sc0, rc0)).start()
        wvg[...] += nn(gvt_scr[tile], rows)

        @pl.when(tile > 0)
        def _():
            spread_columns(tile - 1, plain_sum, cd_part, cd_swap, cd_chip, cd_in, (sc0, rc0), (sc1, rc1))

    spread_columns(TILES - 1, plain_sum, cd_part, cd_swap, cd_chip, cd_in, (sc0, rc0), (sc1, rc1))

    att_t = att[...].reshape(D, ROWS)
    att_rows = att_t.T
    for head in range(HEADS):
        rd = (att_rows[:, group_cols(head)] * gam[head].astype(F32)).sum(axis=1, keepdims=True)
        rd_scr[head] = jnp.broadcast_to(rd, (ROWS, BLOCK))
        gam[head] = gam[head] + gam[head]
    out[:ROWS] = (ref[...].astype(F32) + nn(att_rows.astype(BF16), wo[...])).astype(BF16)
    pack_weight(early_bufs[0], 1, nn(att_t.astype(BF16), gout[...]))
    pack_weight(early_bufs[0], 0, wvg[...].T)
    early = all_reduce(early_bufs, early_sems)
    early[0]()
    gq[...] = jnp.zeros_like(gq)
    wkg[...] = jnp.zeros_like(wkg)

    def source_copy(d):
        return send(gs_sum.at[to_offset(d)], gs_in.at[d - 1], (sg1, rg1), d, on_chip(d, core))

    def spread_source(tile):
        send(gs_part.at[tile, core], gs_swap.at[tile], (sg0, rg0), tile, partner).wait_recv()
        gs_sum[tile] = (gs_part[tile, core].astype(F32) + gs_swap[tile].astype(F32)).astype(BF16)
        d = lax.rem(tile + CHIPS - chip, CHIPS)

        @pl.when(d > 0)
        def _():
            source_copy(d).start()

    @pl.loop(0, TILES)
    def _(step):
        tile = by_quarters(step)
        for at, stage in ((1, 1), (5, 2)):

            @pl.when(step == at)
            def _():
                early[stage]()

        collect_columns(tile, plain_sum, cd_chip, cd_in, cd_all, (sc1, rc1))
        rows = src_all[pl.ds(tile * 2, 2)].reshape(TILE, D)
        gk_heads = []

        def make_grad(head):
            cols = group_cols(head)
            for half in range(2):
                rows = slice(half * TILE, (half + 1) * TILE)
                x = nt(qb_scr[head, rows], kh[tile, head])
                gp = nt(gam[head, rows], v_scr[tile, :, cols])
                lines = []
                for kb in range(2):
                    lanes = slice(kb * BLOCK, (kb + 1) * BLOCK)
                    lc_row = lc_all[tile, kb, head : head + 1, :]
                    cd_row = cd_all[tile, kb, head : head + 1, :]
                    u = x[:, lanes] * UNIT
                    r = jnp.exp2(u)
                    c = jnp.exp2(u + lr[head, rows] - lc_row)
                    lines.append((r * (c * gp[:, lanes] - rd_scr[head, rows]) - c * cd_row).astype(BF16))
                match_scr[head, rows] = jnp.concatenate(lines, axis=1)

        def use_grad(head):
            gs = match_scr[head]
            gq[head] += nt(kt_scr[tile, head_lanes(head), :], gs)
            gk_heads.append((nn(qt_all[head_lanes(head), :], gs) * SCALE).astype(BF16))
        in_turn(make_grad, use_grad)
        gkt = jnp.concatenate(gk_heads, axis=0)
        wkg[...] += nn(gkt, rows)
        gst = nn(wk[...], gkt) + nn(wv[...], gvt_scr[tile])
        for kb in range(2):
            gs_part[tile, kb] = gst[:, kb * BLOCK : (kb + 1) * BLOCK].astype(BF16)
        send(gs_part.at[tile, 1 - core], gs_swap.at[tile], (sg0, rg0), tile, partner).start()

        @pl.when(step > 0)
        def _():
            spread_source(by_quarters(step - 1))

    gq_t = (gq[...].reshape(D, ROWS) * SCALE).astype(BF16)
    pack_weight(late_bufs[0], 0, nn(gq_t, ref[...]).T)
    pack_weight(late_bufs[0], 1, wkg[...].T)
    late = all_reduce(late_bufs, late_sems)

    def leave(at, first, count):
        rows = pl.ds(first, count)
        return pltpu.make_async_copy(out.at[rows], out_hbm.at[rows], out_sems.at[at])

    late[0]()
    early[3]()
    gref = (gout[...].astype(F32) + nt(gq_t.T, wq[...])).astype(BF16)
    late[1]()
    out[ROWS : 2 * ROWS] = gref
    spread_source(by_quarters(TILES - 1))
    early[4]()
    late[2]()
    for d in (4, 3, 5, 2, 6, 1, 7):
        source_copy(d).wait_recv()
    gsrc = gs_sum[chip].astype(F32)
    for d in range(CHIPS - 1):
        gsrc = gsrc + gs_in[d].astype(F32)
    out[2 * ROWS : 2 * ROWS + BLOCK] = gsrc.T.astype(BF16)
    leave(0, 0, 2 * ROWS + BLOCK).start()
    early[5]()
    put_weights(out, early_bufs[-1], 1)
    leave(1, OUT_ROWS - 2 * D, 2 * D).start()
    late[3]()

    early[6]()
    for way in range(2):
        for hops in range(1, 5):
            for piece in pieces_of(way, hops):
                ring_copy(blk, way, hops, piece).wait_send()

    @pl.loop(0, TILES)
    def _(tile):
        send(src, src_all.at[blk], (sa1, ra1), tile, partner).wait_send()
        swap_columns(tile, lc_part, lc_swap, (sl0, rl0)).wait_send()
        swap_columns(tile, cd_part, cd_swap, (sc0, rc0)).wait_send()
        send(lc_in.at[tile], lc_in.at[tile], (sl1, rl1), tile, partner).wait_send()
        send(cd_in.at[tile], cd_in.at[tile], (sc1, rc1), tile, partner).wait_send()
        send(gs_part.at[tile, core], gs_swap.at[tile], (sg0, rg0), tile, partner).wait_send()

        @pl.when(tile > 0)
        def _():
            send(gs_sum.at[tile], gs_in.at[0], (sg1, rg1), tile, partner).wait_send()

    late[4]()
    late[5]()
    put_weights(out, late_bufs[-1], 0)
    leave(2, 2 * ROWS + BLOCK, 2 * D).start()
    leave(2, 2 * ROWS + BLOCK, 2 * D).wait()
    leave(1, OUT_ROWS - 2 * D, 2 * D).wait()
    leave(0, 0, 2 * ROWS + BLOCK).wait()

    late[6]()


def shape(dims, dtype):
    return jax.ShapeDtypeStruct(dims, dtype)


def layer(ref, gout, src, wq, wk, wv, wo, inter):
    vm = pltpu.VMEM
    row = (CHUNK, BLOCK)
    reduction = [
        vm((2, PLANE) + row, BF16), vm((PLANE,) + row, BF16), vm((PLANE,) + row, BF16), vm((PLANE - 1,) + row, BF16),
        vm(row, BF16), vm((CHIPS,) + row, BF16), vm(row, BF16), vm((2, PLANE) + row, BF16),
    ]
    heads = (HEADS, ROWS, BLOCK)
    turned = (HEADS, HEAD_DIM, ROWS)
    pair = (TILES, 2, HEADS, BLOCK)
    columns = [vm(pair, F32), vm(pair, F32), vm(pair, F32), vm((TILES, CHIPS - 1, 2, HEADS, BLOCK), F32), vm(pair, F32)]
    scratch = [
        vm((ROWS, D), BF16), vm((ROWS, D), BF16), *[vm((D, D), BF16)] * 4, vm((OUT_ROWS, D), BF16),
        vm((2 * CHIPS, BLOCK, D), BF16), vm((TILES, D, TILE), BF16), vm((TILES, HEADS, TILE, BLOCK), BF16),
        vm((TILES, TILE, D), BF16), vm((TILES, D, TILE), BF16), vm(heads, BF16), vm(heads, BF16), vm(heads, BF16),
        vm(heads, BF16), vm((D, ROWS), BF16), vm((D, ROWS), BF16), vm((TILES, HEADS, ROWS, TILE), F32), vm(heads, F32), vm(heads, F32),
        *columns, *columns,
        vm(turned, F32), vm((HEADS, ROWS, TILE), BF16), vm((TILES, D, TILE), BF16), vm(heads, F32), vm((D, D), F32), vm((D, D), F32), vm(turned, F32),
        vm((TILES, 2, D, BLOCK), BF16), vm((TILES, D, BLOCK), BF16), vm((TILES, D, BLOCK), BF16),
        vm((CHIPS - 1, D, BLOCK), BF16),
        *reduction, *reduction,
        DMA, DMA((8 * PIECES,)), DMA((8 * PIECES,)),
    ] + [DMA((n,)) for n in (8,) * 14 + 2 * (2, 2, 15, 15, 7, 7, 15, 15) + (3,)] + [pltpu.SemaphoreType.REGULAR((7,)), DMA((6,))]
    return pl.pallas_call(
        layer_kernel,
        out_shape=shape((OUT_ROWS, D), BF16),
        in_specs=[HBM, HBM, VMEM, HBM, HBM, HBM, HBM, SMEM],
        out_specs=HBM,
        scratch_shapes=scratch,
        compiler_params=pltpu.CompilerParams(vmem_limit_bytes=60 << 20, collective_id=1, has_side_effects=True),
        name="layer",
    )(ref, gout, src, wq, wk, wv, wo, inter)


def finish_kernel(parts, matched_out, gref_out, gsrc_out, *rest):
    weights, (rows, packed, wide, in_sems, out_sems) = rest[:4], rest[4:]
    first = 2 * ROWS + BLOCK
    load_weights = pltpu.make_async_copy(parts.at[pl.ds(first, 4 * D)], packed, in_sems.at[0])
    load_rows = pltpu.make_async_copy(parts.at[pl.ds(0, first)], rows, in_sems.at[1])
    load_weights.start()
    load_rows.start()
    stores = []
    load_weights.wait()
    for at, out in enumerate(weights):
        wide[at] = packed[at * D : (at + 1) * D].astype(F32)
        stores.append(pltpu.make_async_copy(wide.at[at], out, out_sems.at[at]))
        stores[-1].start()
    load_rows.wait()
    for at, (out, begin, count) in enumerate(
        ((matched_out, 0, ROWS), (gref_out, ROWS, ROWS), (gsrc_out, 2 * ROWS, BLOCK))
    ):
        stores.append(pltpu.make_async_copy(rows.at[pl.ds(begin, count)], out, out_sems.at[4 + at]))
        stores[-1].start()
    for store in stores:
        store.wait()


def finish(parts):
    return pl.pallas_call(
        finish_kernel,
        out_shape=[shape((ROWS, D), BF16)] * 2 + [shape((BLOCK, D), BF16)] + [shape((D, D), F32)] * 4,
        in_specs=[HBM],
        out_specs=[HBM] * 7,
        scratch_shapes=[
            pltpu.VMEM((2 * ROWS + BLOCK, D), BF16), pltpu.VMEM((4 * D, D), BF16), pltpu.VMEM((4, D, D), F32),
            DMA((2,)), DMA((7,)),
        ],
        compiler_params=pltpu.CompilerParams(vmem_limit_bytes=60 << 20),
        name="finish",
    )(parts)


def on_device(ref_feats, src_feats, grad_out, w_query, w_key, w_value, w_out, intersection):
    parts = layer(ref_feats[0], grad_out[0], src_feats[0], w_query, w_key, w_value, w_out, intersection[0])
    matched, gref, gsrc, wqg, wkg, wvg, wog = finish(parts)
    return matched[None], gref[None], gsrc[None], wqg, wkg, wvg, wog


def solution(mesh):
    split = P("scan", "blk", None)
    return jax.shard_map(
        on_device, mesh=mesh,
        in_specs=(split, split, split, P(), P(), P(), P(), split),
        out_specs=(split, split, split, P(), P(), P(), P()),
        check_vma=False,
    )
```
